256 devices in a mesh: ctx: 32 (over z, x), tp: 8 (over y, core).
Axes of the slice: x: 4, y: 4, z: 8, core: 2. Of those that a mesh axis runs over, the one named last changes fastest.
Arguments:
- projected: bfloat16 [3, 8192, 4096], P(None, 'ctx', 'tp'), may hold values from -6 to 6
- conv_weight: float32 [3, 4, 4096], P(None, None, 'tp'), may hold values from -3 to 3
- log_decay: float32 [32, 8192], P('tp', 'ctx'), may hold values from -2 to 0
- write_rate: float32 [32, 8192], P('tp', 'ctx'), may hold values from 0 to 1
- doc_bounds: int32 [8, 2], replicated, may hold values from 0 to 64, as said below
- out_gate: bfloat16 [8192, 4096], P('ctx', 'tp'), may hold values from -6 to 6
- norm_gain: float32 [128], replicated, may hold values from 0.1 to 1.9
- out_weight: bfloat16 [4096, 4096], P('tp'), may hold values from -0.09375 to 0.09375
Outputs:
- layer_out: bfloat16 [8192, 4096], P(('ctx', 'tp'))
The draws below stay inside these ranges and needn't reach their ends.
Inputs may be any that keep to these rules, and one draw needn't show every extreme that they name: `doc_bounds`: row i holds the first block and one past the last block of document i, in units of 128 tokens; rows are in order, row 0 starts at 0, each row starts where the previous one ends, the last ends at 64, and every document has at least one block.
All inputs are finite; a program needn't handle non-finite values.
Results may differ from the reference program's by a relative error of at most 0.017.
Values may be sent and summed in bfloat16 or wider, within the bound.
A program may use at most 64 MiB of HBM per device.

```python
import jax
import jax.numpy as jnp
from jax import lax

D = 4096
H = 32
DK = 128
SPAN = 128
KERNEL = 4
DOCS = 8
TOK_DEV = 256
SEQUENCE_TOKENS = 8192
NCH = 64
N_TP = 8


def head_kinds(key):
    fast_share = 0.5
    return jax.random.uniform(jax.random.fold_in(key, 11), (H,)) < fast_share


def log_uniform(key, shape, low, high):
    return jnp.exp(jax.random.uniform(key, shape, jnp.float32, jnp.log(low), jnp.log(high)))


def draw_log_decay(key, part):
    fast_heads = head_kinds(key)
    divided_keys = jax.random.split(jax.random.fold_in(key, 21), 6)
    fast_rate = log_uniform(divided_keys[0], (H,), 1.0 / 50, 1.0 / 30)
    slow_rate = log_uniform(divided_keys[1], (H,), 0.05, 0.3) / SEQUENCE_TOKENS
    baseline_rate = jnp.where(fast_heads, fast_rate, slow_rate)
    block_multiplier = jnp.repeat(log_uniform(divided_keys[2], (H, SEQUENCE_TOKENS // TOK_DEV), 0.5, 2.0), TOK_DEV, axis=1)
    token_multiplier = log_uniform(divided_keys[3], (H, SEQUENCE_TOKENS), 0.5, 2.0)
    spike_position = jax.random.randint(divided_keys[4], (3,), 0, SEQUENCE_TOKENS)
    spike_decrease = jax.random.uniform(divided_keys[5], (3,), jnp.float32, 0.22, 0.51)
    token_positions = jnp.arange(SEQUENCE_TOKENS)
    spike_total_sum = jnp.sum(jnp.where(token_positions[None, :] == spike_position[:, None], spike_decrease[:, None], 0.0), axis=0)
    return (-(baseline_rate[:, None] * block_multiplier * token_multiplier) - spike_total_sum[None, :]).astype(jnp.float32)


def draw_write_rate(key, part):
    fast_heads = head_kinds(key)
    divided_keys = jax.random.split(jax.random.fold_in(key, 31), 3)
    fast_base = jax.random.uniform(divided_keys[0], (H,), jnp.float32, 0.3, 0.7)
    slow_base = log_uniform(divided_keys[1], (H,), 0.25, 1.0) * DK / SEQUENCE_TOKENS
    baseline_rate = jnp.where(fast_heads, fast_base, slow_base)
    return (baseline_rate[:, None] * jax.random.uniform(divided_keys[2], (H, SEQUENCE_TOKENS), jnp.float32, 0.6, 1.4)).astype(jnp.float32)


def draw_doc_bounds(key, part):
    shuffled = jax.random.permutation(jax.random.fold_in(key, 41), NCH - 1)
    cut_points = jnp.sort(shuffled[:DOCS - 1] + 1).astype(jnp.int32)
    doc_starts = jnp.concatenate([jnp.zeros((1,), jnp.int32), cut_points])
    doc_ends = jnp.concatenate([cut_points, jnp.full((1,), NCH, jnp.int32)])
    return jnp.stack([doc_starts, doc_ends], axis=1).astype(jnp.int32)


def level_of(rng, extent, pieces, least, high):
    def one(dim, blocks):
        draws = jax.random.uniform(jax.random.fold_in(jax.random.fold_in(rng, 6), dim), (blocks,), jnp.float32, least / len(pieces), high / len(pieces))
        return jnp.repeat(jnp.exp(draws), extent[dim] // blocks).reshape((-1,) + (1,) * (len(extent) - dim - 1))

    level = one(*pieces[0])
    for cut in pieces[1:]:
        level = level * one(*cut)
    return level


def bell_draw(key, dims, spread, most, cuts=(), kind=jnp.bfloat16):
    factor_of = level_of(key, dims, cuts, -0.22, 0.18) if cuts else 1.0
    result = jax.random.normal(key, dims, jnp.float32) * spread * factor_of
    return jnp.minimum(jnp.maximum(result, -most), most).astype(kind)


def setup_inputs(seed: int = 0) -> dict:
    streams_of = jax.random.split(jax.random.key(seed), 9)
    return {
        "projected": bell_draw(streams_of[0], (3, SEQUENCE_TOKENS, H * DK), 1.0, 6.0, ((1, 32), (2, 8))),
        "conv_weight": bell_draw(streams_of[1], (3, KERNEL, H * DK), KERNEL ** -0.5, 3.0, ((2, 8),), jnp.float32),
        "log_decay": draw_log_decay(jax.random.fold_in(streams_of[8], 71), 0),
        "write_rate": draw_write_rate(jax.random.fold_in(streams_of[8], 71), 0),
        "doc_bounds": draw_doc_bounds(jax.random.fold_in(streams_of[8], 71), 0),
        "out_gate": bell_draw(streams_of[5], (SEQUENCE_TOKENS, H * DK), 1.0, 6.0, ((0, 32), (1, 8))),
        "norm_gain": jnp.clip(1.0 + 0.18 * jax.random.normal(streams_of[6], (DK,), jnp.float32), 0.1, 1.9),
        "out_weight": bell_draw(streams_of[7], (H * DK, D), (H * DK) ** -0.5, 0.09375, ((0, 8),)),
    }


def rounded(values):
    return lax.optimization_barrier(values.astype(jnp.bfloat16)).astype(jnp.float32)

def reference(projected, conv_weight, log_decay, write_rate, doc_bounds, out_gate, norm_gain, out_weight):
    highest = lax.Precision.HIGHEST
    token_positions = jnp.arange(SEQUENCE_TOKENS, dtype=jnp.int32)
    starts = (doc_bounds[:, 0] * SPAN).astype(jnp.int32)
    document = (lax.optimization_barrier(jnp.sum((token_positions[:, None] >= starts[None, :]).astype(jnp.int32), axis=1)) - 1).astype(jnp.int32)
    streams = projected.astype(jnp.float32)
    convolved = jnp.zeros(streams.shape, jnp.float32)
    for tap_lag in range(KERNEL):
        shifted = jnp.pad(streams, ((0, 0), (tap_lag, 0), (0, 0)))[:, :SEQUENCE_TOKENS, :]
        earlier_doc = jnp.concatenate([jnp.full((tap_lag,), -1, jnp.int32), document[:SEQUENCE_TOKENS - tap_lag].astype(jnp.int32)])
        allowed = (earlier_doc == document).astype(jnp.float32)
        convolved = convolved + conv_weight[:, tap_lag, None, :] * shifted * allowed[None, :, None]
    activated = jax.nn.silu(convolved).reshape(3, SEQUENCE_TOKENS, H, DK)
    query_key = activated[:2]
    query_key = query_key / jnp.sqrt(lax.optimization_barrier(jnp.sum(query_key * query_key, axis=-1, keepdims=True)) + 1e-06)
    queries = rounded(query_key[0])
    key_vecs = rounded(query_key[1])
    value_vecs = rounded(activated[2])
    resets = jnp.any(token_positions[:, None] == starts[None, :], axis=1)
    keep_flag = 1.0 - resets.astype(jnp.float32)
    decay_rows = jnp.exp(log_decay.T)
    write_rows = write_rate.T

    def advance(carried, step_item):
        keep_now, decay_now, rate_now, query_now, key_now, value_now = step_item
        carried = keep_now * carried
        along_key = jnp.einsum('hvk,hk->hv', carried, key_now, precision=highest)
        carried = decay_now[:, None, None] * (carried - rate_now[:, None, None] * along_key[:, :, None] * key_now[:, None, :]) + rate_now[:, None, None] * value_now[:, :, None] * key_now[:, None, :]
        return (carried, jnp.einsum('hvk,hk->hv', carried, query_now, precision=highest))
    attended = lax.scan(advance, jnp.zeros((H, DK, DK), jnp.float32), (keep_flag, decay_rows, write_rows, queries, key_vecs, value_vecs))[1]
    gated = jax.nn.silu(out_gate.astype(jnp.float32).reshape(SEQUENCE_TOKENS, H, DK))
    normed = attended / jnp.sqrt(lax.optimization_barrier(jnp.mean(attended * attended, axis=-1, keepdims=True)) + 1e-05) * norm_gain * gated
    normed = normed.astype(jnp.bfloat16).reshape(SEQUENCE_TOKENS, H * DK)
    group_width = H // N_TP * DK
    summed = jnp.zeros((SEQUENCE_TOKENS, D), jnp.float32)
    for group_idx in range(N_TP):
        partial_term = jnp.dot(normed[:, group_idx * group_width:(group_idx + 1) * group_width], out_weight[group_idx * group_width:(group_idx + 1) * group_width], preferred_element_type=jnp.float32)
        summed = summed + rounded(partial_term)
    return summed.astype(jnp.bfloat16)
```

```python
import functools

import jax
import jax.numpy as jnp
from jax import lax
from jax.experimental import pallas as pl
from jax.experimental.pallas import tpu as pltpu
from jax.sharding import PartitionSpec as P

MESH = pl.DeviceIdType.MESH
F32 = jnp.float32
BF16 = jnp.bfloat16
SPAN = 128
TAPS = 4
NX = 4
NY = 4
HEADS = 4
NP = 8
BLK = 512
NBLK = 8
RCH = 2


def mm(a, b):
    return lax.dot_general(a, b, (((1,), (0,)), ((), ())), preferred_element_type=F32)


def mmt(a, b):
    return lax.dot_general(a, b, (((1,), (1,)), ((), ())), preferred_element_type=F32)


def silu(u):
    return u / (1.0 + jnp.exp(-u))


def kernel(
    nz, proj_hbm, cw_ref, ld_ref, wr_ref, db_ref, gate_hbm, gain_ref, w_hbm, out_ref,
    proj, halo, ext, gate, w_own, w_par,
    gbuf, cbuf, masks, kq, rt, vtmp, lb, pb_s, xb, yb, wub, wts, t1o1, t2, o2, tos, tin,
    pt, po, rowt, rowo, srx, snd, es, ein, qfin, lfin, sg,
    nb, nrx, acc, pb, rxo, rx1, rx2, cs,
    lsem, hsem, wsem, xs_sem, xr_sem, zs_sem, zr_sem, es_sem, er_sem, ns_sem, nr_sem, rs_sem, rr_sem,
):
    ctx = lax.axis_index("ctx")
    tp = lax.axis_index("tp")
    z, x = lax.div(ctx, NX), lax.rem(ctx, NX)
    y, core = lax.div(tp, 2), lax.rem(tp, 2)
    nctx = nz * NX
    nxt = lax.rem(ctx + 1, nctx)
    prv = lax.rem(ctx + nctx - 1, nctx)
    zup = lax.rem(z + 1, nz)
    zdn = lax.rem(z + nz - 1, nz)
    right = lax.rem(y + 1, NY)
    left = lax.rem(y + NY - 1, NY)
    opp = lax.rem(y + 2, NY)
    other = 1 - core

    def remote(src, dst, ssem, rsem, device):
        return pltpu.make_async_remote_copy(
            src_ref=src, dst_ref=dst, send_sem=ssem, recv_sem=rsem,
            device_id=device, device_id_type=MESH,
        )

    barrier = pltpu.get_barrier_semaphore()
    peers = [(nxt, tp), (prv, tp)]
    peers += [(z * NX + lax.rem(x + r, NX), tp) for r in range(1, NX)]
    peers += [(zup * NX + x, tp), (zdn * NX + x, tp)]
    peers += [(ctx, right * 2 + core), (ctx, left * 2 + core), (ctx, y * 2 + other)]
    for device in peers:
        pl.semaphore_signal(barrier, inc=1, device_id=device, device_id_type=MESH)

    loads = [
        pltpu.make_async_copy(proj_hbm, proj, lsem.at[0]),
        pltpu.make_async_copy(gate_hbm, gate, lsem.at[1]),
        pltpu.make_async_copy(w_hbm, w_own, lsem.at[2]),
    ]
    loads[0].start()

    pl.semaphore_wait(barrier, len(peers))
    rows = proj_hbm.shape[1]
    halo_copy = remote(proj_hbm.at[:, pl.ds(rows - 16, 16), :], halo, hsem.at[0], hsem.at[1], (nxt, tp))
    halo_copy.start()
    loads[1].start()
    loads[2].start()
    w_copy = remote(w_hbm, w_par, wsem.at[0], wsem.at[1], (ctx, y * 2 + other))
    w_copy.start()

    gbuf[...] = jnp.zeros((128, 128), F32)
    gbuf[0:4, :] = ld_ref[:, 0:128]
    gbuf[4:8, :] = ld_ref[:, 128:256]
    gbuf[8:12, :] = wr_ref[:, 0:128]
    gbuf[12:16, :] = wr_ref[:, 128:256]
    run = gbuf[0:8, :]
    lane = lax.broadcasted_iota(jnp.int32, (8, 128), 1)
    for step in (1, 2, 4, 8, 16, 32, 64):
        run = run + jnp.where(lane >= step, pltpu.roll(run, step, 1), 0.0)
    gbuf[0:8, :] = run
    cbuf[...] = gbuf[...].T

    row_i = lax.broadcasted_iota(jnp.int32, (128, 128), 0)
    col_i = lax.broadcasted_iota(jnp.int32, (128, 128), 1)
    eye = row_i == col_i
    eye_f = jnp.where(eye, 1.0, 0.0)
    for level in range(1, 7):
        low = lax.shift_right_logical(row_i, level)
        low_j = lax.shift_right_logical(col_i, level)
        same = lax.shift_right_logical(row_i, level + 1) == lax.shift_right_logical(col_i, level + 1)
        masks[level - 1] = jnp.where(same & (low > low_j), 1.0, 0.0).astype(BF16)

    keeps = []
    for span in range(2):
        hit = jnp.int32(0)
        for d in range(db_ref.shape[0]):
            hit = hit + jnp.where(db_ref[d, 0] == ctx * 2 + span, 1, 0)
        keeps.append(1.0 - jnp.minimum(hit, 1).astype(F32))

    ones = jnp.full((128, 128), 1.0, BF16)

    def conv_span(span):
        base = span * SPAN
        for s in (1, 2, 0):
            if span == 0:
                before = halo[s, 8:16, :].astype(F32)
            else:
                before = proj[s, base - 8 : base, :].astype(F32)
            ext[s, 0:8, :] = before * keeps[span]
            ext[s, 8:136, :] = proj[s, base : base + SPAN, :].astype(F32)
            for h in range(HEADS):
                p = span * HEADS + h
                cols = pl.ds(h * 128, 128)
                u = cw_ref[s, 0:1, cols] * ext[s, 8:136, cols]
                for j in range(1, TAPS):
                    u = u + cw_ref[s, j : j + 1, cols] * ext[s, 8 - j : 136 - j, cols]
                a = silu(u)
                if s == 2:
                    rt[p, 128:256, :] = (a.T * gbuf[8 + p : 9 + p, :]).astype(BF16)
                else:
                    ss = mm((a * a).astype(BF16), ones)
                    n = a * lax.rsqrt(ss + 1e-06)
                    nbf = n.astype(BF16)
                    if s == 1:
                        kq[p, 0:128, :] = nbf
                        scale = gbuf[8 + p : 9 + p, :] * jnp.exp(gbuf[p : p + 1, :])
                        rt[p, 0:128, :] = (nbf.astype(F32).T * scale).astype(BF16)
                    else:
                        kq[p, 128:256, :] = nbf

    def scores(p):
        a = mmt(kq[p], kq[p, 0:128, :])
        gcol = jnp.broadcast_to(cbuf[:, p : p + 1], (128, 128))
        bcol = jnp.broadcast_to(cbuf[:, 8 + p : 9 + p], (128, 128))
        dm = jnp.exp(jnp.minimum(gcol - gbuf[p : p + 1, :], 0.0))
        low = jnp.where(row_i > col_i, bcol * dm * a[0:128], 0.0)
        lb[p] = low.astype(BF16)
        pb_s[p] = jnp.where(row_i >= col_i, dm * a[128:256], 0.0).astype(BF16)
        pair = lax.shift_right_logical(row_i, 1) == lax.shift_right_logical(col_i, 1)
        xb[p] = (eye_f - jnp.where(pair, low, 0.0)).astype(BF16)

    loads[0].wait()
    conv_span(1)
    halo_copy.wait()
    conv_span(0)
    for p in range(NP):
        scores(p)
    for level in range(1, 7):
        for p in range(NP):
            yb[p] = mm(xb[p], lb[p] * masks[level - 1]).astype(BF16)
        for p in range(NP):
            xb[p] = xb[p] - mm(yb[p], xb[p]).astype(BF16)
    for p in range(NP):
        wu = mmt(rt[p], xb[p])
        wub[p] = wu.astype(BF16)
        g = gbuf[p : p + 1, :]
        wts[p] = (wu * jnp.exp(g[:, 127:128] - g)).astype(BF16)
    for h in range(HEADS):
        for span in range(2):
            p = span * HEADS + h
            to = mm(wts[p], kq[p, 0:128, :])
            last = jnp.exp(gbuf[p : p + 1, 127:128])
            t = keeps[span] * (last * eye_f - to[0:128])
            if span == 0:
                t1o1[h, 0:128, :] = t.astype(BF16)
                t1o1[h, 128:256, :] = to[128:256].astype(BF16)
            else:
                t2[h] = t.astype(BF16)
                o2[h] = to[128:256]
    for h in range(HEADS):
        d = mm(t1o1[h], t2[h])
        tos[h, 0:128, :] = d[0:128].astype(BF16)
        tos[h, 128:256, :] = (d[128:256] + o2[h]).astype(BF16)

    x_copies = []
    for r in range(1, NX):
        to_x = lax.rem(x + r, NX)
        copy = remote(tos.at[to_x], tin.at[x], xs_sem.at[r - 1], xr_sem.at[r - 1], (z * NX + to_x, tp))
        copy.start()
        x_copies.append(copy)
    tin[x] = tos[x]

    for h in range(HEADS):
        for span in range(2):
            p = span * HEADS + h
            pw = mmt(pb_s[p], wub[p])
            gcol = jnp.broadcast_to(cbuf[:, p : p + 1], (128, 128))
            q = keeps[span] * (jnp.exp(gcol) * kq[p, 128:256, :].astype(F32) - pw[:, 0:128])
            if span == 0:
                qfin[h, 0:128, :] = q.astype(BF16)
                lfin[h, 0:128, :] = pw[:, 128:256]
            else:
                q2 = mmt(q.astype(BF16), t1o1[h])
                qfin[h, 128:256, :] = q2[:, 0:128].astype(BF16)
                lfin[h, 128:256, :] = pw[:, 128:256] + q2[:, 128:256]
    loads[1].wait()
    for h in range(HEADS):
        cols = pl.ds(h * 128, 128)
        sg[h] = silu(gate[:, cols].astype(F32)) * gain_ref[0:1, :]

    for copy in x_copies:
        copy.wait()

    pt[0] = eye_f.astype(BF16)
    po[0] = jnp.zeros((128, 128), F32)
    pt[1] = tin[0, 0:128, :]
    po[1] = tin[0, 128:256, :].astype(F32)
    cur = tin[0]
    for j in range(1, NX):
        step = mm(cur, tin[j, 0:128, :])
        off = step[128:256] + tin[j, 128:256, :].astype(F32)
        if j < NX - 1:
            pt[j + 1] = step[0:128].astype(BF16)
            po[j + 1] = off
            cur = jnp.concatenate([step[0:128], off], axis=0).astype(BF16)
        else:
            rowt[...] = step[0:128].astype(BF16)
            rowo[...] = off

    crows = 128 // RCH

    def z_copy(i):
        part = pl.ds(i * crows, crows)
        return remote(snd.at[part, :], srx.at[part, :], zs_sem.at[i], zr_sem.at[i], (zup * NX + x, tp))

    @pl.when(z == 0)
    def _():
        srx[...] = jnp.zeros((128, 128), BF16)

    for i in range(RCH):
        @pl.when(z > 0)
        def _():
            z_copy(i).wait_recv()

        part = pl.ds(i * crows, crows)
        snd[part, :] = (mm(srx[part, :], rowt[...]) + rowo[part, :]).astype(BF16)

        @pl.when(z < nz - 1)
        def _():
            z_copy(i).start()

    e_copies = []
    for r in range(1, NX):
        to_x = lax.rem(x + r, NX)
        es[r - 1] = (mm(srx[...], pt[to_x]) + po[to_x]).astype(BF16)
        copy = remote(es.at[r - 1], ein.at[x], es_sem.at[r - 1], er_sem.at[r - 1], (z * NX + to_x, tp))
        copy.start()
        e_copies.append(copy)
    ein[x] = (mm(srx[...], pt[x]) + po[x]).astype(BF16)

    mean_ones = jnp.full((128, 128), 1.0 / 128.0, BF16)
    n_copies = []
    for r in range(NX):
        head = lax.rem(x + NX - r, NX)
        if r > 0:
            e_copies[r - 1].wait_recv()
        att = mmt(qfin[head], ein[head]) + lfin[head]
        ms = mm((att * att).astype(BF16), mean_ones)
        nrm = (att * lax.rsqrt(ms + 1e-05) * sg[head]).astype(BF16)
        cols = pl.ds(pl.multiple_of(head * 128, 128), 128)
        for c in range(2):
            for b in range(NY):
                lo = b * 64 + c * 32
                nb[c, b * 32 : b * 32 + 32, cols] = nrm[lo : lo + 32, :]
        copy = remote(
            nb.at[other, :, cols], nrx.at[:, cols], ns_sem.at[r], nr_sem.at[r], (ctx, y * 2 + other)
        )
        copy.start()
        n_copies.append(copy)

    loads[2].wait()
    for b in range(NBLK):
        cols = pl.ds(b * BLK, BLK)
        acc[:, cols] = mm(nb[core], w_own[:, cols])
    w_copy.wait()
    for copy in n_copies:
        copy.wait()

    order = (0, 4, 1, 5, 2, 6, 3, 7)
    half = NBLK // 2
    o_copies, d_copies, c_copies = {}, {}, {}
    for b in order:
        cols = pl.ds(b * BLK, BLK)
        res = (acc[:, cols] + mm(nrx[...], w_par[:, cols])).astype(BF16)
        for d in range(NY):
            pb[b, d] = res[d * 32 : d * 32 + 32, :]
        first, second = (right, left) if b < half else (left, right)
        o_copies[b] = remote(
            pb.at[b, opp], rxo.at[b], rs_sem.at[0, b], rr_sem.at[0, b], (ctx, first * 2 + core)
        )
        o_copies[b].start()
        d_copies[b] = remote(
            pb.at[b, second], rx1.at[b], rs_sem.at[1, b], rr_sem.at[1, b], (ctx, second * 2 + core)
        )
        d_copies[b].start()
    for b in order:
        first = right if b < half else left
        o_copies[b].wait_recv()
        cs[b] = (pb[b, first].astype(F32) + rxo[b].astype(F32)).astype(BF16)
        c_copies[b] = remote(
            cs.at[b], rx2.at[b], rs_sem.at[2, b], rr_sem.at[2, b], (ctx, first * 2 + core)
        )
        c_copies[b].start()
    for b in order:
        d_copies[b].wait_recv()
        c_copies[b].wait_recv()
        total = pb[b, y].astype(F32) + rx1[b].astype(F32) + rx2[b].astype(F32)
        out_ref[:, pl.ds(b * BLK, BLK)] = total.astype(BF16)

    for i in range(RCH):
        @pl.when(z < nz - 1)
        def _():
            z_copy(i).wait_send()

    for copy in e_copies:
        copy.wait_send()
    for b in order:
        o_copies[b].wait_send()
        d_copies[b].wait_send()
        c_copies[b].wait_send()


def body(nz, projected, conv_weight, log_decay, write_rate, doc_bounds, out_gate, norm_gain, out_weight):
    v = pltpu.VMEM
    dma = pltpu.SemaphoreType.DMA
    vspec = pl.BlockSpec(memory_space=pltpu.VMEM)
    aspec = pl.BlockSpec(memory_space=pl.ANY)
    scratch = [
        v((3, 256, 512), BF16), v((3, 16, 512), BF16), v((3, 136, 512), F32), v((256, 512), BF16),
        v((512, 4096), BF16), v((512, 4096), BF16),
        v((128, 128), F32), v((128, 128), F32), v((6, 128, 128), BF16),
        v((NP, 256, 128), BF16), v((NP, 256, 128), BF16), v((8, 128), F32),
        v((NP, 128, 128), BF16), v((NP, 128, 128), BF16), v((NP, 128, 128), BF16), v((NP, 128, 128), BF16),
        v((NP, 256, 128), BF16), v((NP, 256, 128), BF16),
        v((HEADS, 256, 128), BF16), v((HEADS, 128, 128), BF16), v((HEADS, 128, 128), F32),
        v((HEADS, 256, 128), BF16), v((NX, 256, 128), BF16),
        v((NX, 128, 128), BF16), v((NX, 128, 128), F32), v((128, 128), BF16), v((128, 128), F32),
        v((128, 128), BF16), v((128, 128), BF16), v((NX - 1, 128, 128), BF16), v((NX, 128, 128), BF16),
        v((HEADS, 256, 128), BF16), v((HEADS, 256, 128), F32), v((HEADS, 256, 128), F32),
        v((2, 128, 512), BF16), v((128, 512), BF16), v((128, 4096), F32),
        v((NBLK, NY, 32, BLK), BF16), v((NBLK, 32, BLK), BF16), v((NBLK, 32, BLK), BF16),
        v((NBLK, 32, BLK), BF16), v((NBLK, 32, BLK), BF16),
        dma((3,)), dma((2,)), dma((2,)), dma((3,)), dma((3,)), dma((RCH,)), dma((RCH,)),
        dma((3,)), dma((3,)), dma((4,)), dma((4,)), dma((3, NBLK)), dma((3, NBLK)),
    ]
    return pl.pallas_call(
        functools.partial(kernel, nz),
        out_shape=jax.ShapeDtypeStruct((32, 4096), BF16),
        in_specs=[aspec, vspec, vspec, vspec, pl.BlockSpec(memory_space=pltpu.SMEM), aspec, vspec, aspec],
        out_specs=vspec,
        scratch_shapes=scratch,
        compiler_params=pltpu.CompilerParams(
            collective_id=0, has_side_effects=True, vmem_limit_bytes=56 * 1024 * 1024
        ),
    )(
        projected, conv_weight, log_decay, write_rate, doc_bounds, out_gate,
        norm_gain.reshape(1, -1), out_weight,
    )


def solution(mesh):
    in_specs = (
        P(None, "ctx", "tp"),
        P(None, None, "tp"),
        P("tp", "ctx"),
        P("tp", "ctx"),
        P(),
        P("ctx", "tp"),
        P(),
        P("tp", None),
    )
    out_specs = P(("ctx", "tp"), None)
    nz = mesh.shape["ctx"] // NX
    return jax.shard_map(
        functools.partial(body, nz), mesh=mesh, in_specs=in_specs, out_specs=out_specs, check_vma=False
    )
```

```python
import functools

import jax
import jax.numpy as jnp
from jax import lax
from jax.experimental import pallas as pl
from jax.experimental.pallas import tpu as pltpu
from jax.sharding import PartitionSpec as P

MESH = pl.DeviceIdType.MESH
F32 = jnp.float32
BF16 = jnp.bfloat16
SPAN = 128
TAPS = 4
NX = 4
NY = 4
HEADS = 4
NP = 8
BLK = 512
NBLK = 8
RCH = 4
PCH = 4
LOW = 3


def mm(a, b):
    return lax.dot_general(a, b, (((1,), (0,)), ((), ())), preferred_element_type=F32)


def mmt(a, b):
    return lax.dot_general(a, b, (((1,), (1,)), ((), ())), preferred_element_type=F32)


def silu(u):
    return u / (1.0 + jnp.exp(-u))


def kernel(
    nz, proj_hbm, cw_hbm, ld_hbm, wr_hbm, db_hbm, gate_hbm, gain_hbm, w_hbm, own_out, rx1, rx2,
    cw_ref, ld_ref, wr_ref, db_ref, gain_ref,
    proj, halo, ext, gate, w_own, w_par,
    gbuf, cbuf, masks, kq, rt, vtmp, lb, pb_s, xb, yb, wub, wts, t1o1, t2, o2, tos, tin,
    pt, po, qt, qo, rowt, rowo, prx, psnd, srx, snd, es, ein, qfin, lfin, sg,
    nb, nrx, acc, pb, rxo, cs,
    lsem, hsem, wsem, xs_sem, xr_sem, zs_sem, zr_sem, ps_sem, pr_sem, rdy, fsem, es_sem, er_sem, ns_sem, nr_sem, rs_sem, rr_sem,
):
    ctx = lax.axis_index("ctx")
    tp = lax.axis_index("tp")
    z, x = lax.div(ctx, NX), lax.rem(ctx, NX)
    y, core = lax.div(tp, 2), lax.rem(tp, 2)
    nctx = nz * NX
    nxt = lax.rem(ctx + 1, nctx)
    prv = lax.rem(ctx + nctx - 1, nctx)
    zup = lax.rem(z + 1, nz)
    zdn = lax.rem(z + nz - 1, nz)
    right = lax.rem(y + 1, NY)
    left = lax.rem(y + NY - 1, NY)
    opp = lax.rem(y + 2, NY)
    other = 1 - core

    def remote(src, dst, ssem, rsem, device):
        return pltpu.make_async_remote_copy(
            src_ref=src, dst_ref=dst, send_sem=ssem, recv_sem=rsem,
            device_id=device, device_id_type=MESH,
        )

    barrier = pltpu.get_barrier_semaphore()
    peers = [(nxt, tp), (prv, tp)]
    peers += [(z * NX + lax.rem(x + r, NX), tp) for r in range(1, NX)]
    peers += [(zup * NX + x, tp), (zdn * NX + x, tp)]
    peers += [(ctx, right * 2 + core), (ctx, left * 2 + core), (ctx, y * 2 + other)]
    for device in peers:
        pl.semaphore_signal(barrier, inc=1, device_id=device, device_id_type=MESH)

    loads = [
        pltpu.make_async_copy(proj_hbm, proj, lsem.at[0]),
        pltpu.make_async_copy(gate_hbm, gate, lsem.at[1]),
        pltpu.make_async_copy(w_hbm, w_own, lsem.at[2]),
    ]
    small = [
        pltpu.make_async_copy(ld_hbm, ld_ref, lsem.at[3]),
        pltpu.make_async_copy(wr_hbm, wr_ref, lsem.at[4]),
        pltpu.make_async_copy(db_hbm, db_ref, lsem.at[5]),
        pltpu.make_async_copy(cw_hbm, cw_ref, lsem.at[6]),
        pltpu.make_async_copy(gain_hbm, gain_ref, lsem.at[7]),
    ]
    for copy in small:
        copy.start()
    loads[0].start()

    pl.semaphore_wait(barrier, len(peers))
    rows = proj_hbm.shape[1]
    halo_copy = remote(proj_hbm.at[:, pl.ds(rows - 16, 16), :], halo, hsem.at[0], hsem.at[1], (nxt, tp))
    halo_copy.start()
    loads[1].start()
    loads[2].start()
    w_copy = remote(w_hbm, w_par, wsem.at[0], wsem.at[1], (ctx, y * 2 + other))
    w_copy.start()

    @pl.when(z == LOW + 1)
    def _():
        pl.semaphore_signal(rdy, inc=1, device_id=(zdn * NX + x, tp), device_id_type=MESH)

    @pl.when(z == nz - 1)
    def _():
        pl.semaphore_signal(rdy, inc=1, device_id=(zup * NX + x, tp), device_id_type=MESH)

    for copy in small:
        copy.wait()

    gbuf[...] = jnp.zeros((128, 128), F32)
    gbuf[0:4, :] = ld_ref[:, 0:128]
    gbuf[4:8, :] = ld_ref[:, 128:256]
    gbuf[8:12, :] = wr_ref[:, 0:128]
    gbuf[12:16, :] = wr_ref[:, 128:256]
    run = gbuf[0:8, :]
    lane = lax.broadcasted_iota(jnp.int32, (8, 128), 1)
    for step in (1, 2, 4, 8, 16, 32, 64):
        run = run + jnp.where(lane >= step, pltpu.roll(run, step, 1), 0.0)
    gbuf[0:8, :] = run
    cbuf[...] = gbuf[...].T

    row_i = lax.broadcasted_iota(jnp.int32, (128, 128), 0)
    col_i = lax.broadcasted_iota(jnp.int32, (128, 128), 1)
    eye = row_i == col_i
    eye_f = jnp.where(eye, 1.0, 0.0)
    for level in range(1, 7):
        low = lax.shift_right_logical(row_i, level)
        low_j = lax.shift_right_logical(col_i, level)
        same = lax.shift_right_logical(row_i, level + 1) == lax.shift_right_logical(col_i, level + 1)
        masks[level - 1] = jnp.where(same & (low > low_j), 1.0, 0.0).astype(BF16)

    keeps = []
    for span in range(2):
        hit = jnp.int32(0)
        for d in range(db_ref.shape[1]):
            hit = hit + jnp.where(db_ref[0, d] == ctx * 2 + span, 1, 0)
        keeps.append(1.0 - jnp.minimum(hit, 1).astype(F32))

    ones = jnp.full((128, 128), 1.0, BF16)

    def conv_span(span):
        base = span * SPAN
        for s in (1, 2, 0):
            if span == 0:
                before = halo[s, 8:16, :].astype(F32)
            else:
                before = proj[s, base - 8 : base, :].astype(F32)
            ext[s, 0:8, :] = before * keeps[span]
            ext[s, 8:136, :] = proj[s, base : base + SPAN, :].astype(F32)
            for h in range(HEADS):
                p = span * HEADS + h
                cols = pl.ds(h * 128, 128)
                u = cw_ref[s, 0:1, cols] * ext[s, 8:136, cols]
                for j in range(1, TAPS):
                    u = u + cw_ref[s, j : j + 1, cols] * ext[s, 8 - j : 136 - j, cols]
                a = silu(u)
                if s == 2:
                    rt[p, 128:256, :] = (a.T * gbuf[8 + p : 9 + p, :]).astype(BF16)
                else:
                    ss = mm((a * a).astype(BF16), ones)
                    n = a * lax.rsqrt(ss + 1e-06)
                    nbf = n.astype(BF16)
                    if s == 1:
                        kq[p, 0:128, :] = nbf
                        scale = gbuf[8 + p : 9 + p, :] * jnp.exp(gbuf[p : p + 1, :])
                        rt[p, 0:128, :] = (nbf.astype(F32).T * scale).astype(BF16)
                    else:
                        kq[p, 128:256, :] = nbf

    def scores(p):
        a = mmt(kq[p], kq[p, 0:128, :])
        gcol = jnp.broadcast_to(cbuf[:, p : p + 1], (128, 128))
        bcol = jnp.broadcast_to(cbuf[:, 8 + p : 9 + p], (128, 128))
        dm = jnp.exp(jnp.minimum(gcol - gbuf[p : p + 1, :], 0.0))
        low = jnp.where(row_i > col_i, bcol * dm * a[0:128], 0.0)
        lb[p] = low.astype(BF16)
        pb_s[p] = jnp.where(row_i >= col_i, dm * a[128:256], 0.0).astype(BF16)
        pair = lax.shift_right_logical(row_i, 1) == lax.shift_right_logical(col_i, 1)
        xb[p] = (eye_f - jnp.where(pair, low, 0.0)).astype(BF16)

    loads[0].wait()
    conv_span(1)
    halo_copy.wait()
    conv_span(0)
    for p in range(NP):
        scores(p)
    for level in range(1, 7):
        for p in range(NP):
            yb[p] = mm(xb[p], lb[p] * masks[level - 1]).astype(BF16)
        for p in range(NP):
            xb[p] = xb[p] - mm(yb[p], xb[p]).astype(BF16)
    for p in range(NP):
        wu = mmt(rt[p], xb[p])
        wub[p] = wu.astype(BF16)
        g = gbuf[p : p + 1, :]
        wts[p] = (wu * jnp.exp(g[:, 127:128] - g)).astype(BF16)
    for h in range(HEADS):
        for span in range(2):
            p = span * HEADS + h
            to = mm(wts[p], kq[p, 0:128, :])
            last = jnp.exp(gbuf[p : p + 1, 127:128])
            t = keeps[span] * (last * eye_f - to[0:128])
            if span == 0:
                t1o1[h, 0:128, :] = t.astype(BF16)
                t1o1[h, 128:256, :] = to[128:256].astype(BF16)
            else:
                t2[h] = t.astype(BF16)
                o2[h] = to[128:256]
    for h in range(HEADS):
        d = mm(t1o1[h], t2[h])
        tos[h, 0:128, :] = d[0:128].astype(BF16)
        tos[h, 128:256, :] = (d[128:256] + o2[h]).astype(BF16)

    x_copies = []
    for r in (2, 1, 3):
        to_x = lax.rem(x + r, NX)
        copy = remote(tos.at[to_x], tin.at[x], xs_sem.at[r - 1], xr_sem.at[r - 1], (z * NX + to_x, tp))
        copy.start()
        x_copies.append(copy)
    tin[x] = tos[x]

    @pl.when(z == LOW)
    def _():
        pl.semaphore_wait(rdy, 1)
        pl.semaphore_signal(rdy, inc=1, device_id=(zdn * NX + x, tp), device_id_type=MESH)

    for h in range(HEADS):
        for span in range(2):
            p = span * HEADS + h
            pw = mmt(pb_s[p], wub[p])
            gcol = jnp.broadcast_to(cbuf[:, p : p + 1], (128, 128))
            q = keeps[span] * (jnp.exp(gcol) * kq[p, 128:256, :].astype(F32) - pw[:, 0:128])
            if span == 0:
                qfin[h, 0:128, :] = q.astype(BF16)
                lfin[h, 0:128, :] = pw[:, 128:256]
            else:
                q2 = mmt(q.astype(BF16), t1o1[h])
                qfin[h, 128:256, :] = q2[:, 0:128].astype(BF16)
                lfin[h, 128:256, :] = pw[:, 128:256] + q2[:, 128:256]
    loads[1].wait()
    for h in range(HEADS):
        cols = pl.ds(h * 128, 128)
        sg[h] = silu(gate[:, cols].astype(F32)) * gain_ref[0:1, :]

    for copy in x_copies:
        copy.wait()

    pt[0] = eye_f.astype(BF16)
    po[0] = jnp.zeros((128, 128), F32)
    pt[1] = tin[0, 0:128, :]
    po[1] = tin[0, 128:256, :].astype(F32)
    cur = tin[0]
    for j in range(1, NX):
        step = mm(cur, tin[j, 0:128, :])
        off = step[128:256] + tin[j, 128:256, :].astype(F32)
        if j < NX - 1:
            pt[j + 1] = step[0:128].astype(BF16)
            po[j + 1] = off
            cur = jnp.concatenate([step[0:128], off], axis=0).astype(BF16)
        else:
            rowt[...] = step[0:128].astype(BF16)
            rowo[...] = off

    crows = 128 // RCH
    prows = 256 // PCH

    def s_copy(i, to, k):
        part = pl.ds(i * crows, crows)
        return remote(snd.at[part, :], srx.at[part, :], zs_sem.at[i, k], zr_sem.at[i], (to * NX + x, tp))

    def p_copy(i):
        part = pl.ds(i * prows, prows)
        return remote(psnd.at[part, :], prx.at[part, :], ps_sem.at[i], pr_sem.at[i], (zup * NX + x, tp))

    @pl.when(z == 0)
    def _():
        snd[...] = rowo[...].astype(BF16)
        pl.semaphore_wait(rdy, 1)
        for i in range(RCH):
            s_copy(i, zup, 0).start()
        srx[...] = jnp.zeros((128, 128), BF16)

    @pl.when(z == LOW)
    def _():
        psnd[0:128, :] = rowt[...]
        psnd[128:256, :] = rowo[...].astype(BF16)
        for i in range(PCH):
            p_copy(i).start()

    @pl.when(z <= LOW)
    def _():
        prx[0:128, :] = eye_f.astype(BF16)
        prx[128:256, :] = jnp.zeros((128, 128), BF16)

    @pl.when(z > LOW)
    def _():
        for i in range(PCH):
            part = pl.ds(i * prows, prows)
            p_copy(i).wait_recv()

            @pl.when(z < nz - 1)
            def _():
                new = mm(prx[part, :], rowt[...])
                if i * prows >= 128:
                    new = new + rowo[i * prows - 128 : (i + 1) * prows - 128, :]
                psnd[part, :] = new.astype(BF16)
                p_copy(i).start()

    for j in range(NX):
        new = mm(prx[...], pt[j])
        qt[j] = new[0:128].astype(BF16)
        qo[j] = new[128:256] + po[j]

    @pl.when(z == LOW - 1)
    def _():
        pl.semaphore_wait(rdy, 1)

    for i in range(RCH):
        part = pl.ds(i * crows, crows)

        @pl.when(z > 0)
        def _():
            s_copy(i, zup, 0).wait_recv()

        @pl.when((z > 0) & (z < LOW))
        def _():
            snd[part, :] = (mm(srx[part, :], rowt[...]) + rowo[part, :]).astype(BF16)

        @pl.when((z > 0) & (z < LOW - 1))
        def _():
            s_copy(i, zup, 0).start()

        @pl.when(z == LOW - 1)
        def _():
            for far in range(nz - 1, LOW - 1, -1):
                s_copy(i, far, far - LOW).start()

    e_copies = {}
    for r in (2, 1, 3):
        to_x = lax.rem(x + r, NX)
        es[r - 1] = (mm(srx[...], qt[to_x]) + qo[to_x]).astype(BF16)
        copy = remote(es.at[r - 1], ein.at[x], es_sem.at[r - 1], er_sem.at[r - 1], (z * NX + to_x, tp))
        copy.start()
        e_copies[r] = copy
    ein[x] = (mm(srx[...], qt[x]) + qo[x]).astype(BF16)

    mean_ones = jnp.full((128, 128), 1.0 / 128.0, BF16)
    n_copies = []
    for r in (0, 1, 3, 2):
        head = lax.rem(x + NX - r, NX)
        if r > 0:
            e_copies[r].wait_recv()
        att = mmt(qfin[head], ein[head]) + lfin[head]
        ms = mm((att * att).astype(BF16), mean_ones)
        nrm = (att * lax.rsqrt(ms + 1e-05) * sg[head]).astype(BF16)
        cols = pl.ds(pl.multiple_of(head * 128, 128), 128)
        for c in range(2):
            for b in range(NY):
                lo = b * 64 + c * 32
                nb[c, b * 32 : b * 32 + 32, cols] = nrm[lo : lo + 32, :]
        copy = remote(
            nb.at[other, :, cols], nrx.at[:, cols], ns_sem.at[r], nr_sem.at[r], (ctx, y * 2 + other)
        )
        copy.start()
        n_copies.append(copy)

    loads[2].wait()
    for b in range(NBLK):
        cols = pl.ds(b * BLK, BLK)
        acc[:, cols] = mm(nb[core], w_own[:, cols])
    w_copy.wait()
    for copy in n_copies:
        copy.wait()

    order = (0, 4, 1, 5, 2, 6, 3, 7)
    half = NBLK // 2
    o_copies, d_copies, c_copies, f_copies = {}, {}, {}, []
    for b in order:
        cols = pl.ds(b * BLK, BLK)
        res = (acc[:, cols] + mm(nrx[...], w_par[:, cols])).astype(BF16)
        for d in range(NY):
            pb[b, d] = res[d * 32 : d * 32 + 32, :]
        first, second = (right, left) if b < half else (left, right)
        o_copies[b] = remote(
            pb.at[b, opp], rxo.at[b], rs_sem.at[0, b], rr_sem.at[0, b], (ctx, first * 2 + core)
        )
        o_copies[b].start()
        d_copies[b] = remote(
            pb.at[b, second], rx1.at[:, cols], rs_sem.at[1, b], rr_sem.at[1, b], (ctx, second * 2 + core)
        )
        d_copies[b].start()
        f_copies.append(pltpu.make_async_copy(pb.at[b, y], own_out.at[:, cols], fsem.at[b]))
        f_copies[-1].start()
    for b in order:
        first = right if b < half else left
        cols = pl.ds(b * BLK, BLK)
        o_copies[b].wait_recv()
        cs[b] = (pb[b, first].astype(F32) + rxo[b].astype(F32)).astype(BF16)
        c_copies[b] = remote(
            cs.at[b], rx2.at[:, cols], rs_sem.at[2, b], rr_sem.at[2, b], (ctx, first * 2 + core)
        )
        c_copies[b].start()
    for b in order:
        d_copies[b].wait_recv()
        c_copies[b].wait_recv()

    for copy in f_copies:
        copy.wait()

    @pl.when(z < LOW - 1)
    def _():
        for i in range(RCH):
            s_copy(i, zup, 0).wait_send()

    @pl.when(z == LOW - 1)
    def _():
        for i in range(RCH):
            for far in range(LOW, nz):
                s_copy(i, far, far - LOW).wait_send()

    @pl.when((z >= LOW) & (z < nz - 1))
    def _():
        for i in range(PCH):
            p_copy(i).wait_send()

    for copy in e_copies.values():
        copy.wait_send()
    for b in order:
        o_copies[b].wait_send()
        d_copies[b].wait_send()
        c_copies[b].wait_send()


def body(nz, projected, conv_weight, log_decay, write_rate, doc_bounds, out_gate, norm_gain, out_weight):
    v = pltpu.VMEM
    dma = pltpu.SemaphoreType.DMA
    vspec = pl.BlockSpec(memory_space=pltpu.VMEM)
    aspec = pl.BlockSpec(memory_space=pl.ANY)
    scratch = [
        v((3, TAPS, 512), F32), v((HEADS, 256), F32), v((HEADS, 256), F32),
        pltpu.SMEM((2, 8), jnp.int32), v((1, 128), F32),
        v((3, 256, 512), BF16), v((3, 16, 512), BF16), v((3, 136, 512), F32), v((256, 512), BF16),
        v((512, 4096), BF16), v((512, 4096), BF16),
        v((128, 128), F32), v((128, 128), F32), v((6, 128, 128), BF16),
        v((NP, 256, 128), BF16), v((NP, 256, 128), BF16), v((8, 128), F32),
        v((NP, 128, 128), BF16), v((NP, 128, 128), BF16), v((NP, 128, 128), BF16), v((NP, 128, 128), BF16),
        v((NP, 256, 128), BF16), v((NP, 256, 128), BF16),
        v((HEADS, 256, 128), BF16), v((HEADS, 128, 128), BF16), v((HEADS, 128, 128), F32),
        v((HEADS, 256, 128), BF16), v((NX, 256, 128), BF16),
        v((NX, 128, 128), BF16), v((NX, 128, 128), F32), v((NX, 128, 128), BF16), v((NX, 128, 128), F32),
        v((128, 128), BF16), v((128, 128), F32), v((256, 128), BF16), v((256, 128), BF16),
        v((128, 128), BF16), v((128, 128), BF16), v((NX - 1, 128, 128), BF16), v((NX, 128, 128), BF16),
        v((HEADS, 256, 128), BF16), v((HEADS, 256, 128), F32), v((HEADS, 256, 128), F32),
        v((2, 128, 512), BF16), v((128, 512), BF16), v((128, 4096), F32),
        v((NBLK, NY, 32, BLK), BF16), v((NBLK, 32, BLK), BF16), v((NBLK, 32, BLK), BF16),
        dma((8,)), dma((2,)), dma((2,)), dma((3,)), dma((3,)), dma((RCH, nz - LOW)), dma((RCH,)),
        dma((PCH,)), dma((PCH,)), pltpu.SemaphoreType.REGULAR, dma((NBLK,)),
        dma((3,)), dma((3,)), dma((4,)), dma((4,)), dma((3, NBLK)), dma((3, NBLK)),
    ]
    half = jax.ShapeDtypeStruct((32, 4096), BF16)
    own, one, two = pl.pallas_call(
        functools.partial(kernel, nz),
        out_shape=(half, half, half),
        in_specs=[aspec] * 8,
        out_specs=(aspec, aspec, aspec),
        scratch_shapes=scratch,
        compiler_params=pltpu.CompilerParams(
            collective_id=0, has_side_effects=True, vmem_limit_bytes=56 * 1024 * 1024
        ),
    )(
        projected, conv_weight, log_decay, write_rate, doc_bounds.T, out_gate,
        norm_gain.reshape(1, -1), out_weight,
    )
    return (own.astype(F32) + one.astype(F32) + two.astype(F32)).astype(BF16)


def solution(mesh):
    in_specs = (
        P(None, "ctx", "tp"),
        P(None, None, "tp"),
        P("tp", "ctx"),
        P("tp", "ctx"),
        P(),
        P("ctx", "tp"),
        P(),
        P("tp", None),
    )
    out_specs = P(("ctx", "tp"), None)
    nz = mesh.shape["ctx"] // NX
    return jax.shard_map(
        functools.partial(body, nz), mesh=mesh, in_specs=in_specs, out_specs=out_specs, check_vma=False
    )
```

```python
import functools

import jax
import jax.numpy as jnp
from jax import lax
from jax.experimental import pallas as pl
from jax.experimental.pallas import tpu as pltpu
from jax.sharding import PartitionSpec as P

MESH = pl.DeviceIdType.MESH
F32 = jnp.float32
BF16 = jnp.bfloat16
SPAN = 128
TAPS = 4
NX = 4
NY = 4
HEADS = 4
NP = 8
BLK = 512
NBLK = 8
RCH = 4
PCH = 4
HEAD = 4
LOW = 3


def mm(a, b):
    return lax.dot_general(a, b, (((1,), (0,)), ((), ())), preferred_element_type=F32)


def mmt(a, b):
    return lax.dot_general(a, b, (((1,), (1,)), ((), ())), preferred_element_type=F32)


def silu(u):
    return u / (1.0 + jnp.exp(-u))


def kernel(
    nz, proj_hbm, cw_hbm, ld_hbm, wr_hbm, db_hbm, gate_hbm, gain_hbm, w_hbm, own_out, rx1, rx2,
    cw_ref, ld_ref, wr_ref, db_ref, gain_ref,
    proj, halo, ext, gate, w_own, w_par,
    gbuf, cbuf, masks, kq, rt, vb, lb, pb_s, xb, yb, xc, wub, wts, t1o1, t2, o2, tos, tin,
    pt, po, qt, qo, rowt, rowo, prx, psnd, srx, snd, es, ein, qfin, lfin, sg,
    nb, nrx, acc, pb, rxo, cs,
    lsem, hsem, wsem, xs_sem, xr_sem, zs_sem, zr_sem, ps_sem, pr_sem, rdy, fsem, es_sem, er_sem, ns_sem, nr_sem, rs_sem, rr_sem,
):
    ctx = lax.axis_index("ctx")
    tp = lax.axis_index("tp")
    z, x = lax.div(ctx, NX), lax.rem(ctx, NX)
    y, core = lax.div(tp, 2), lax.rem(tp, 2)
    nctx = nz * NX
    nxt = lax.rem(ctx + 1, nctx)
    prv = lax.rem(ctx + nctx - 1, nctx)
    zup = lax.rem(z + 1, nz)
    zdn = lax.rem(z + nz - 1, nz)
    right = lax.rem(y + 1, NY)
    left = lax.rem(y + NY - 1, NY)
    opp = lax.rem(y + 2, NY)
    other = 1 - core

    def remote(src, dst, ssem, rsem, device):
        return pltpu.make_async_remote_copy(
            src_ref=src, dst_ref=dst, send_sem=ssem, recv_sem=rsem,
            device_id=device, device_id_type=MESH,
        )

    barrier = pltpu.get_barrier_semaphore()
    peers = [(nxt, tp), (prv, tp)]
    peers += [(z * NX + lax.rem(x + r, NX), tp) for r in range(1, NX)]
    peers += [(zup * NX + x, tp), (zdn * NX + x, tp)]
    peers += [(ctx, right * 2 + core), (ctx, left * 2 + core), (ctx, y * 2 + other)]
    for device in peers:
        pl.semaphore_signal(barrier, inc=1, device_id=device, device_id_type=MESH)

    loads = [
        pltpu.make_async_copy(proj_hbm, proj, lsem.at[0]),
        pltpu.make_async_copy(gate_hbm, gate, lsem.at[1]),
        pltpu.make_async_copy(w_hbm, w_own, lsem.at[2]),
    ]
    small = [
        pltpu.make_async_copy(ld_hbm, ld_ref, lsem.at[3]),
        pltpu.make_async_copy(wr_hbm, wr_ref, lsem.at[4]),
        pltpu.make_async_copy(db_hbm, db_ref, lsem.at[5]),
        pltpu.make_async_copy(cw_hbm, cw_ref, lsem.at[6]),
        pltpu.make_async_copy(gain_hbm, gain_ref, lsem.at[7]),
    ]
    for copy in small:
        copy.start()
    loads[0].start()

    row_i = lax.broadcasted_iota(jnp.int32, (128, 128), 0)
    col_i = lax.broadcasted_iota(jnp.int32, (128, 128), 1)
    eye = row_i == col_i
    eye_f = jnp.where(eye, 1.0, 0.0)
    for level in range(1, 7):
        low = lax.shift_right_logical(row_i, level)
        low_j = lax.shift_right_logical(col_i, level)
        same = lax.shift_right_logical(row_i, level + 1) == lax.shift_right_logical(col_i, level + 1)
        masks[level - 1] = jnp.where(same & (low > low_j), 1.0, 0.0).astype(BF16)

    pl.semaphore_wait(barrier, len(peers))
    rows = proj_hbm.shape[1]
    halo_copy = remote(proj_hbm.at[:, pl.ds(rows - 16, 16), :], halo, hsem.at[0], hsem.at[1], (nxt, tp))
    halo_copy.start()
    loads[1].start()
    loads[2].start()
    w_copy = remote(w_hbm, w_par, wsem.at[0], wsem.at[1], (ctx, y * 2 + other))
    w_copy.start()

    @pl.when(z == LOW + 1)
    def _():
        pl.semaphore_signal(rdy, inc=1, device_id=(zdn * NX + x, tp), device_id_type=MESH)

    @pl.when(z == nz - 1)
    def _():
        pl.semaphore_signal(rdy, inc=1, device_id=(zup * NX + x, tp), device_id_type=MESH)

    for copy in small:
        copy.wait()

    gbuf[...] = jnp.zeros((128, 128), F32)
    gbuf[0:4, :] = ld_ref[:, 0:128]
    gbuf[4:8, :] = ld_ref[:, 128:256]
    gbuf[8:12, :] = wr_ref[:, 0:128]
    gbuf[12:16, :] = wr_ref[:, 128:256]
    run = gbuf[0:8, :]
    lane = lax.broadcasted_iota(jnp.int32, (8, 128), 1)
    for step in (1, 2, 4, 8, 16, 32, 64):
        run = run + jnp.where(lane >= step, pltpu.roll(run, step, 1), 0.0)
    gbuf[0:8, :] = run
    cbuf[...] = gbuf[...].T

    keeps = []
    for span in range(2):
        hit = jnp.int32(0)
        for d in range(db_ref.shape[1]):
            hit = hit + jnp.where(db_ref[0, d] == ctx * 2 + span, 1, 0)
        keeps.append(1.0 - jnp.minimum(hit, 1).astype(F32))

    ones = jnp.full((128, 128), 1.0, BF16)

    def activate(s, h, first, count):
        cols = pl.ds(h * 128, 128)
        u = cw_ref[s, 0:1, cols] * ext[s, 8 + first : 8 + first + count, cols]
        for j in range(1, TAPS):
            lo = 8 + first - j
            u = u + cw_ref[s, j : j + 1, cols] * ext[s, lo : lo + count, cols]
        return silu(u)

    def unit(a):
        ss = mm((a * a).astype(BF16), ones)
        return (a * lax.rsqrt(ss + 1e-06)).astype(BF16)

    def fill(streams, span, first, count):
        for s in streams:
            for h in range(HEADS):
                p = span * HEADS + h
                a = activate(s, h, first, count)
                if s == 1:
                    kq[p, first : first + count, :] = unit(a)
                elif s == 0:
                    kq[p, 128 + first : 128 + first + count, :] = unit(a)
                else:
                    vb[p, first : first + count, :] = a.astype(BF16)

    def transposed(p):
        beta = gbuf[8 + p : 9 + p, :]
        scale = beta * jnp.exp(gbuf[p : p + 1, :])
        rt[p, 0:128, :] = (kq[p, 0:128, :].astype(F32).T * scale).astype(BF16)
        rt[p, 128:256, :] = (vb[p].astype(F32).T * beta).astype(BF16)

    def decays(p):
        gcol = jnp.broadcast_to(cbuf[:, p : p + 1], (128, 128))
        bcol = jnp.broadcast_to(cbuf[:, 8 + p : 9 + p], (128, 128))
        dm = jnp.exp(jnp.minimum(gcol - gbuf[p : p + 1, :], 0.0))
        return dm, bcol * dm

    def scores(p):
        a = mmt(kq[p, 0:128, :], kq[p, 0:128, :])
        return jnp.where(row_i > col_i, decays(p)[1] * a, 0.0)

    def pairs(low):
        pair = lax.shift_right_logical(row_i, 1) == lax.shift_right_logical(col_i, 1)
        return (eye_f - jnp.where(pair, low, 0.0)).astype(BF16)

    def updates(p):
        wu = mmt(rt[p], xb[p])
        wub[p] = wu.astype(BF16)
        g = gbuf[p : p + 1, :]
        wts[p] = (wu * jnp.exp(g[:, 127:128] - g)).astype(BF16)

    def maps(p):
        span, h = p // HEADS, p % HEADS
        to = mm(wts[p], kq[p, 0:128, :])
        last = jnp.exp(gbuf[p : p + 1, 127:128])
        t = keeps[span] * (last * eye_f - to[0:128])
        if span == 0:
            t1o1[h, 0:128, :] = t.astype(BF16)
            t1o1[h, 128:256, :] = to[128:256].astype(BF16)
        else:
            t2[h] = t.astype(BF16)
            o2[h] = to[128:256]

    first_span = range(HEADS)
    second_span = range(HEADS, NP)

    loads[0].wait()
    for span in (1, 0):
        for s in (1, 2):
            if span == 0:
                ext[s, 0:8, :] = jnp.zeros((8, 512), F32)
            else:
                ext[s, 0:8, :] = proj[s, SPAN - 8 : SPAN, :].astype(F32) * keeps[1]
            ext[s, 8:136, :] = proj[s, span * SPAN : span * SPAN + SPAN, :].astype(F32)
        fill((1, 2), span, 0, SPAN)
    for p in second_span:
        low = scores(p)
        lb[p] = low.astype(BF16)
        xb[p] = pairs(low)
    for p in first_span:
        low = jnp.where(col_i >= HEAD, scores(p), 0.0)
        lb[p] = low.astype(BF16)
        xb[p] = pairs(low)
    for p in second_span:
        transposed(p)
    for level in range(1, 7):
        for p in range(NP):
            yb[p] = mm(xb[p], lb[p] * masks[level - 1]).astype(BF16)
        for p in range(NP):
            xb[p] = xb[p] - mm(yb[p], xb[p]).astype(BF16)
    for p in second_span:
        updates(p)
    for p in second_span:
        maps(p)

    halo_copy.wait()
    for s in (1, 2):
        ext[s, 0:8, :] = halo[s, 8:16, :].astype(F32) * keeps[0]
    fill((1, 2), 0, 0, 16)
    corner = (row_i < HEAD) & (col_i < HEAD)
    below = (row_i >= HEAD) & (col_i < HEAD)
    for p in first_span:
        low = scores(p)
        lb[p] = jnp.where(below, low, 0.0).astype(BF16)
        low = jnp.where(corner, low, 0.0)
        yb[p] = low.astype(BF16)
        xc[p] = pairs(low)
    for p in first_span:
        transposed(p)
    for p in first_span:
        yb[p] = mm(xc[p], yb[p] * masks[0]).astype(BF16)
    for p in first_span:
        xb[p] = xb[p] + (xc[p] - eye_f.astype(BF16) - mm(yb[p], xc[p]).astype(BF16))
    for p in first_span:
        yb[p] = mm(xb[p], lb[p]).astype(BF16)
    for p in first_span:
        xb[p] = xb[p] - mm(yb[p], xb[p]).astype(BF16)
    for p in first_span:
        updates(p)
    for p in first_span:
        maps(p)
    for h in range(HEADS):
        d = mm(t1o1[h], t2[h])
        tos[h, 0:128, :] = d[0:128].astype(BF16)
        tos[h, 128:256, :] = (d[128:256] + o2[h]).astype(BF16)

    x_copies = []
    for r in (2, 1, 3):
        to_x = lax.rem(x + r, NX)
        copy = remote(tos.at[to_x], tin.at[x], xs_sem.at[r - 1], xr_sem.at[r - 1], (z * NX + to_x, tp))
        copy.start()
        x_copies.append(copy)
    tin[x] = tos[x]

    @pl.when(z == LOW)
    def _():
        pl.semaphore_wait(rdy, 1)
        pl.semaphore_signal(rdy, inc=1, device_id=(zdn * NX + x, tp), device_id_type=MESH)

    for span in range(2):
        before = halo[0, 8:16, :] if span == 0 else proj[0, SPAN - 8 : SPAN, :]
        ext[0, 0:8, :] = before.astype(F32) * keeps[span]
        ext[0, 8:136, :] = proj[0, span * SPAN : span * SPAN + SPAN, :].astype(F32)
        fill((0,), span, 0, SPAN)
    for p in range(NP):
        a = mmt(kq[p, 128:256, :], kq[p, 0:128, :])
        pb_s[p] = jnp.where(row_i >= col_i, decays(p)[0] * a, 0.0).astype(BF16)
    for h in range(HEADS):
        for span in range(2):
            p = span * HEADS + h
            pw = mmt(pb_s[p], wub[p])
            gcol = jnp.broadcast_to(cbuf[:, p : p + 1], (128, 128))
            q = keeps[span] * (jnp.exp(gcol) * kq[p, 128:256, :].astype(F32) - pw[:, 0:128])
            if span == 0:
                qfin[h, 0:128, :] = q.astype(BF16)
                lfin[h, 0:128, :] = pw[:, 128:256]
            else:
                q2 = mmt(q.astype(BF16), t1o1[h])
                qfin[h, 128:256, :] = q2[:, 0:128].astype(BF16)
                lfin[h, 128:256, :] = pw[:, 128:256] + q2[:, 128:256]
    loads[1].wait()
    for h in range(HEADS):
        cols = pl.ds(h * 128, 128)
        sg[h] = silu(gate[:, cols].astype(F32)) * gain_ref[0:1, :]

    for copy in x_copies:
        copy.wait()

    pt[0] = eye_f.astype(BF16)
    po[0] = jnp.zeros((128, 128), F32)
    pt[1] = tin[0, 0:128, :]
    po[1] = tin[0, 128:256, :].astype(F32)
    cur = tin[0]
    for j in range(1, NX):
        step = mm(cur, tin[j, 0:128, :])
        off = step[128:256] + tin[j, 128:256, :].astype(F32)
        if j < NX - 1:
            pt[j + 1] = step[0:128].astype(BF16)
            po[j + 1] = off
            cur = jnp.concatenate([step[0:128], off], axis=0).astype(BF16)
        else:
            rowt[...] = step[0:128].astype(BF16)
            rowo[...] = off

    crows = 128 // RCH
    prows = 256 // PCH

    def s_copy(i, to, k):
        part = pl.ds(i * crows, crows)
        return remote(snd.at[part, :], srx.at[part, :], zs_sem.at[i, k], zr_sem.at[i], (to * NX + x, tp))

    def p_copy(i):
        part = pl.ds(i * prows, prows)
        return remote(psnd.at[part, :], prx.at[part, :], ps_sem.at[i], pr_sem.at[i], (zup * NX + x, tp))

    @pl.when(z == 0)
    def _():
        snd[...] = rowo[...].astype(BF16)
        pl.semaphore_wait(rdy, 1)
        for i in range(RCH):
            s_copy(i, zup, 0).start()
        srx[...] = jnp.zeros((128, 128), BF16)

    @pl.when(z == LOW)
    def _():
        psnd[0:128, :] = rowt[...]
        psnd[128:256, :] = rowo[...].astype(BF16)
        for i in range(PCH):
            p_copy(i).start()

    @pl.when(z <= LOW)
    def _():
        prx[0:128, :] = eye_f.astype(BF16)
        prx[128:256, :] = jnp.zeros((128, 128), BF16)

    @pl.when(z > LOW)
    def _():
        for i in range(PCH):
            part = pl.ds(i * prows, prows)
            p_copy(i).wait_recv()

            @pl.when(z < nz - 1)
            def _():
                new = mm(prx[part, :], rowt[...])
                if i * prows >= 128:
                    new = new + rowo[i * prows - 128 : (i + 1) * prows - 128, :]
                psnd[part, :] = new.astype(BF16)
                p_copy(i).start()

    for j in range(NX):
        new = mm(prx[...], pt[j])
        qt[j] = new[0:128].astype(BF16)
        qo[j] = new[128:256] + po[j]

    @pl.when(z == LOW - 1)
    def _():
        pl.semaphore_wait(rdy, 1)

    for i in range(RCH):
        part = pl.ds(i * crows, crows)

        @pl.when(z > 0)
        def _():
            s_copy(i, zup, 0).wait_recv()

        @pl.when((z > 0) & (z < LOW))
        def _():
            snd[part, :] = (mm(srx[part, :], rowt[...]) + rowo[part, :]).astype(BF16)

        @pl.when((z > 0) & (z < LOW - 1))
        def _():
            s_copy(i, zup, 0).start()

        @pl.when(z == LOW - 1)
        def _():
            for far in range(nz - 1, LOW - 1, -1):
                s_copy(i, far, far - LOW).start()

    e_copies = {}
    for r in (2, 1, 3):
        to_x = lax.rem(x + r, NX)
        es[r - 1] = (mm(srx[...], qt[to_x]) + qo[to_x]).astype(BF16)
        copy = remote(es.at[r - 1], ein.at[x], es_sem.at[r - 1], er_sem.at[r - 1], (z * NX + to_x, tp))
        copy.start()
        e_copies[r] = copy
    ein[x] = (mm(srx[...], qt[x]) + qo[x]).astype(BF16)

    mean_ones = jnp.full((128, 128), 1.0 / 128.0, BF16)
    n_copies = []
    for r in (0, 1, 3, 2):
        head = lax.rem(x + NX - r, NX)
        if r > 0:
            e_copies[r].wait_recv()
        att = mmt(qfin[head], ein[head]) + lfin[head]
        ms = mm((att * att).astype(BF16), mean_ones)
        nrm = (att * lax.rsqrt(ms + 1e-05) * sg[head]).astype(BF16)
        cols = pl.ds(pl.multiple_of(head * 128, 128), 128)
        for c in range(2):
            for b in range(NY):
                lo = b * 64 + c * 32
                nb[c, b * 32 : b * 32 + 32, cols] = nrm[lo : lo + 32, :]
        copy = remote(
            nb.at[other, :, cols], nrx.at[:, cols], ns_sem.at[r], nr_sem.at[r], (ctx, y * 2 + other)
        )
        copy.start()
        n_copies.append(copy)

    loads[2].wait()
    for b in range(NBLK):
        cols = pl.ds(b * BLK, BLK)
        acc[:, cols] = mm(nb[core], w_own[:, cols])
    w_copy.wait()
    for copy in n_copies:
        copy.wait()

    order = (0, 4, 1, 5, 2, 6, 3, 7)
    half = NBLK // 2
    o_copies, d_copies, c_copies, f_copies = {}, {}, {}, []
    for b in order:
        cols = pl.ds(b * BLK, BLK)
        res = (acc[:, cols] + mm(nrx[...], w_par[:, cols])).astype(BF16)
        for d in range(NY):
            pb[b, d] = res[d * 32 : d * 32 + 32, :]
        first, second = (right, left) if b < half else (left, right)
        o_copies[b] = remote(
            pb.at[b, opp], rxo.at[b], rs_sem.at[0, b], rr_sem.at[0, b], (ctx, first * 2 + core)
        )
        o_copies[b].start()
        d_copies[b] = remote(
            pb.at[b, second], rx1.at[:, cols], rs_sem.at[1, b], rr_sem.at[1, b], (ctx, second * 2 + core)
        )
        d_copies[b].start()
        f_copies.append(pltpu.make_async_copy(pb.at[b, y], own_out.at[:, cols], fsem.at[b]))
        f_copies[-1].start()
    for b in order:
        first = right if b < half else left
        cols = pl.ds(b * BLK, BLK)
        o_copies[b].wait_recv()
        cs[b] = (pb[b, first].astype(F32) + rxo[b].astype(F32)).astype(BF16)
        c_copies[b] = remote(
            cs.at[b], rx2.at[:, cols], rs_sem.at[2, b], rr_sem.at[2, b], (ctx, first * 2 + core)
        )
        c_copies[b].start()
    for b in order:
        d_copies[b].wait_recv()
        c_copies[b].wait_recv()

    for copy in f_copies:
        copy.wait()

    @pl.when(z < LOW - 1)
    def _():
        for i in range(RCH):
            s_copy(i, zup, 0).wait_send()

    @pl.when(z == LOW - 1)
    def _():
        for i in range(RCH):
            for far in range(LOW, nz):
                s_copy(i, far, far - LOW).wait_send()

    @pl.when((z >= LOW) & (z < nz - 1))
    def _():
        for i in range(PCH):
            p_copy(i).wait_send()

    for copy in e_copies.values():
        copy.wait_send()
    for b in order:
        o_copies[b].wait_send()
        d_copies[b].wait_send()
        c_copies[b].wait_send()


def body(nz, projected, conv_weight, log_decay, write_rate, doc_bounds, out_gate, norm_gain, out_weight):
    v = pltpu.VMEM
    dma = pltpu.SemaphoreType.DMA
    vspec = pl.BlockSpec(memory_space=pltpu.VMEM)
    aspec = pl.BlockSpec(memory_space=pl.ANY)
    scratch = [
        v((3, TAPS, 512), F32), v((HEADS, 256), F32), v((HEADS, 256), F32),
        pltpu.SMEM((2, 8), jnp.int32), v((1, 128), F32),
        v((3, 256, 512), BF16), v((3, 16, 512), BF16), v((3, 136, 512), F32), v((256, 512), BF16),
        v((512, 4096), BF16), v((512, 4096), BF16),
        v((128, 128), F32), v((128, 128), F32), v((6, 128, 128), BF16),
        v((NP, 256, 128), BF16), v((NP, 256, 128), BF16), v((NP, 128, 128), BF16),
        v((NP, 128, 128), BF16), v((NP, 128, 128), BF16), v((NP, 128, 128), BF16), v((NP, 128, 128), BF16),
        v((HEADS, 128, 128), BF16),
        v((NP, 256, 128), BF16), v((NP, 256, 128), BF16),
        v((HEADS, 256, 128), BF16), v((HEADS, 128, 128), BF16), v((HEADS, 128, 128), F32),
        v((HEADS, 256, 128), BF16), v((NX, 256, 128), BF16),
        v((NX, 128, 128), BF16), v((NX, 128, 128), F32), v((NX, 128, 128), BF16), v((NX, 128, 128), F32),
        v((128, 128), BF16), v((128, 128), F32), v((256, 128), BF16), v((256, 128), BF16),
        v((128, 128), BF16), v((128, 128), BF16), v((NX - 1, 128, 128), BF16), v((NX, 128, 128), BF16),
        v((HEADS, 256, 128), BF16), v((HEADS, 256, 128), F32), v((HEADS, 256, 128), F32),
        v((2, 128, 512), BF16), v((128, 512), BF16), v((128, 4096), F32),
        v((NBLK, NY, 32, BLK), BF16), v((NBLK, 32, BLK), BF16), v((NBLK, 32, BLK), BF16),
        dma((8,)), dma((2,)), dma((2,)), dma((3,)), dma((3,)), dma((RCH, nz - LOW)), dma((RCH,)),
        dma((PCH,)), dma((PCH,)), pltpu.SemaphoreType.REGULAR, dma((NBLK,)),
        dma((3,)), dma((3,)), dma((4,)), dma((4,)), dma((3, NBLK)), dma((3, NBLK)),
    ]
    half = jax.ShapeDtypeStruct((32, 4096), BF16)
    own, one, two = pl.pallas_call(
        functools.partial(kernel, nz),
        out_shape=(half, half, half),
        in_specs=[aspec] * 8,
        out_specs=(aspec, aspec, aspec),
        scratch_shapes=scratch,
        compiler_params=pltpu.CompilerParams(
            collective_id=0, has_side_effects=True, vmem_limit_bytes=56 * 1024 * 1024
        ),
    )(
        projected, conv_weight, log_decay, write_rate, doc_bounds.T, out_gate,
        norm_gain.reshape(1, -1), out_weight,
    )
    return (own.astype(F32) + one.astype(F32) + two.astype(F32)).astype(BF16)


def solution(mesh):
    in_specs = (
        P(None, "ctx", "tp"),
        P(None, None, "tp"),
        P("tp", "ctx"),
        P("tp", "ctx"),
        P(),
        P("ctx", "tp"),
        P(),
        P("tp", None),
    )
    out_specs = P(("ctx", "tp"), None)
    nz = mesh.shape["ctx"] // NX
    return jax.shard_map(
        functools.partial(body, nz), mesh=mesh, in_specs=in_specs, out_specs=out_specs, check_vma=False
    )
```

```python
import functools

import jax
import jax.numpy as jnp
from jax import lax
from jax.experimental import pallas as pl
from jax.experimental.pallas import tpu as pltpu
from jax.sharding import PartitionSpec as P

MESH = pl.DeviceIdType.MESH
F32 = jnp.float32
BF16 = jnp.bfloat16
SPAN = 128
TAPS = 4
NX = 4
NY = 4
HEADS = 4
NP = 8
BLK = 512
NBLK = 8
RCH = 4
PCH = 4
HEAD = 4
LOW = 3


def mm(a, b):
    return lax.dot_general(a, b, (((1,), (0,)), ((), ())), preferred_element_type=F32)


def mmt(a, b):
    return lax.dot_general(a, b, (((1,), (1,)), ((), ())), preferred_element_type=F32)


def silu(u):
    return u / (1.0 + jnp.exp(-u))


def kernel(
    nz, proj_hbm, cw_hbm, ld_hbm, wr_hbm, db_hbm, gate_hbm, gain_hbm, w_hbm, own_out, rx1, rx2,
    cw_ref, ld_ref, wr_ref, db_ref, gain_ref,
    proj, halo, ext, gate, w_own, w_par,
    gbuf, cbuf, masks, kq, rt, vb, lb, pb_s, xb, yb, xc, wub, wts, t1o1, t2, o2, tos, tin, am, ain, ab, mb,
    pt, po, qt, qo, rowt, rowo, prx, psnd, srx, snd, es, ein, qfin, lfin, sg,
    nb, nrx, acc, pb, rxo, cs,
    lsem, hsem, wsem, xs_sem, xr_sem, as_sem, ar_sem, zs_sem, zr_sem, ps_sem, pr_sem, rdy, fsem, es_sem, er_sem, ns_sem, nr_sem, rs_sem, rr_sem,
):
    ctx = lax.axis_index("ctx")
    tp = lax.axis_index("tp")
    z, x = lax.div(ctx, NX), lax.rem(ctx, NX)
    y, core = lax.div(tp, 2), lax.rem(tp, 2)
    nctx = nz * NX
    nxt = lax.rem(ctx + 1, nctx)
    prv = lax.rem(ctx + nctx - 1, nctx)
    zup = lax.rem(z + 1, nz)
    zdn = lax.rem(z + nz - 1, nz)
    right = lax.rem(y + 1, NY)
    left = lax.rem(y + NY - 1, NY)
    opp = lax.rem(y + 2, NY)
    other = 1 - core

    def remote(src, dst, ssem, rsem, device):
        return pltpu.make_async_remote_copy(
            src_ref=src, dst_ref=dst, send_sem=ssem, recv_sem=rsem,
            device_id=device, device_id_type=MESH,
        )

    barrier = pltpu.get_barrier_semaphore()
    peers = [(nxt, tp), (prv, tp)]
    peers += [(z * NX + lax.rem(x + r, NX), tp) for r in range(1, NX)]
    peers += [(zup * NX + x, tp), (zdn * NX + x, tp)]
    peers += [(ctx, right * 2 + core), (ctx, left * 2 + core), (ctx, y * 2 + other)]
    for device in peers:
        pl.semaphore_signal(barrier, inc=1, device_id=device, device_id_type=MESH)

    loads = [
        pltpu.make_async_copy(proj_hbm, proj, lsem.at[0]),
        pltpu.make_async_copy(gate_hbm, gate, lsem.at[1]),
        pltpu.make_async_copy(w_hbm, w_own, lsem.at[2]),
    ]
    small = [
        pltpu.make_async_copy(ld_hbm, ld_ref, lsem.at[3]),
        pltpu.make_async_copy(wr_hbm, wr_ref, lsem.at[4]),
        pltpu.make_async_copy(db_hbm, db_ref, lsem.at[5]),
        pltpu.make_async_copy(cw_hbm, cw_ref, lsem.at[6]),
        pltpu.make_async_copy(gain_hbm, gain_ref, lsem.at[7]),
    ]
    for copy in small:
        copy.start()
    loads[0].start()

    row_i = lax.broadcasted_iota(jnp.int32, (128, 128), 0)
    col_i = lax.broadcasted_iota(jnp.int32, (128, 128), 1)
    eye = row_i == col_i
    eye_f = jnp.where(eye, 1.0, 0.0)
    for level in range(1, 7):
        low = lax.shift_right_logical(row_i, level)
        low_j = lax.shift_right_logical(col_i, level)
        same = lax.shift_right_logical(row_i, level + 1) == lax.shift_right_logical(col_i, level + 1)
        masks[level - 1] = jnp.where(same & (low > low_j), 1.0, 0.0).astype(BF16)

    for copy in small:
        copy.wait()

    gbuf[...] = jnp.zeros((128, 128), F32)
    gbuf[0:4, :] = ld_ref[:, 0:128]
    gbuf[4:8, :] = ld_ref[:, 128:256]
    gbuf[8:12, :] = wr_ref[:, 0:128]
    gbuf[12:16, :] = wr_ref[:, 128:256]
    run = gbuf[0:8, :]
    lane = lax.broadcasted_iota(jnp.int32, (8, 128), 1)
    for step in (1, 2, 4, 8, 16, 32, 64):
        run = run + jnp.where(lane >= step, pltpu.roll(run, step, 1), 0.0)
    gbuf[0:8, :] = run
    cbuf[...] = gbuf[...].T

    keeps = []
    for span in range(2):
        hit = jnp.int32(0)
        for d in range(db_ref.shape[1]):
            hit = hit + jnp.where(db_ref[0, d] == ctx * 2 + span, 1, 0)
        keeps.append(1.0 - jnp.minimum(hit, 1).astype(F32))

    ones = jnp.full((128, 128), 1.0, BF16)

    def activate(s, h, first, count):
        cols = pl.ds(h * 128, 128)
        u = cw_ref[s, 0:1, cols] * ext[s, 8 + first : 8 + first + count, cols]
        for j in range(1, TAPS):
            lo = 8 + first - j
            u = u + cw_ref[s, j : j + 1, cols] * ext[s, lo : lo + count, cols]
        return silu(u)

    def unit(a):
        ss = mm((a * a).astype(BF16), ones)
        return (a * lax.rsqrt(ss + 1e-06)).astype(BF16)

    def fill(streams, span, first, count):
        for s in streams:
            for h in range(HEADS):
                p = span * HEADS + h
                a = activate(s, h, first, count)
                if s == 1:
                    kq[p, first : first + count, :] = unit(a)
                elif s == 0:
                    kq[p, 128 + first : 128 + first + count, :] = unit(a)
                else:
                    vb[p, first : first + count, :] = a.astype(BF16)

    def transposed(p, skip=0):
        beta = gbuf[8 + p : 9 + p, :]
        g = gbuf[p : p + 1, :]
        if skip:
            g = g - g[:, skip - 1 : skip]
            beta = jnp.where(col_i[0:1, :] >= skip, beta, 0.0)
        scale = beta * jnp.exp(g)
        rt[p, 0:128, :] = (kq[p, 0:128, :].astype(F32).T * scale).astype(BF16)
        rt[p, 128:256, :] = (vb[p].astype(F32).T * beta).astype(BF16)

    def decays(p):
        gcol = jnp.broadcast_to(cbuf[:, p : p + 1], (128, 128))
        bcol = jnp.broadcast_to(cbuf[:, 8 + p : 9 + p], (128, 128))
        dm = jnp.exp(jnp.minimum(gcol - gbuf[p : p + 1, :], 0.0))
        return dm, bcol * dm

    def scores(p):
        a = mmt(kq[p, 0:128, :], kq[p, 0:128, :])
        return jnp.where(row_i > col_i, decays(p)[1] * a, 0.0)

    def pairs(low):
        pair = lax.shift_right_logical(row_i, 1) == lax.shift_right_logical(col_i, 1)
        return (eye_f - jnp.where(pair, low, 0.0)).astype(BF16)

    def updates(p):
        wu = mmt(rt[p], xb[p])
        wub[p] = wu.astype(BF16)
        g = gbuf[p : p + 1, :]
        wts[p] = (wu * jnp.exp(g[:, 127:128] - g)).astype(BF16)

    def maps(p):
        span, h = p // HEADS, p % HEADS
        to = mm(wts[p], kq[p, 0:128, :])
        last = jnp.exp(gbuf[p : p + 1, 127:128])
        t = keeps[span] * (last * eye_f - to[0:128])
        if span == 0:
            t1o1[h, 0:128, :] = t.astype(BF16)
            t1o1[h, 128:256, :] = to[128:256].astype(BF16)
        else:
            t2[h] = t.astype(BF16)
            o2[h] = to[128:256]

    first_span = range(HEADS)
    second_span = range(HEADS, NP)

    rows = proj_hbm.shape[1]
    halo_copy = remote(proj_hbm.at[:, pl.ds(rows - 16, 16), :], halo, hsem.at[0], hsem.at[1], (nxt, tp))
    w_copy = remote(w_hbm, w_par, wsem.at[0], wsem.at[1], (ctx, y * 2 + other))

    def enter():
        pl.semaphore_wait(barrier, len(peers))
        halo_copy.start()
        loads[1].start()
        loads[2].start()
        w_copy.start()

        @pl.when(z == LOW + 1)
        def _():
            pl.semaphore_signal(rdy, inc=1, device_id=(zdn * NX + x, tp), device_id_type=MESH)

        @pl.when(z == nz - 1)
        def _():
            pl.semaphore_signal(rdy, inc=1, device_id=(zup * NX + x, tp), device_id_type=MESH)

    loads[0].wait()
    for span in (1, 0):
        for s in (1, 2):
            if span == 0:
                ext[s, 0:8, :] = jnp.zeros((8, 512), F32)
            else:
                ext[s, 0:8, :] = proj[s, SPAN - 8 : SPAN, :].astype(F32) * keeps[1]
            ext[s, 8:136, :] = proj[s, span * SPAN : span * SPAN + SPAN, :].astype(F32)
        fill((1, 2), span, 0, SPAN)
        if span == 1:
            enter()
    for p in range(NP):
        low = scores(p)
        if p < HEADS:
            low = jnp.where(col_i >= HEAD, low, 0.0)
        lb[p] = low.astype(BF16)
        xb[p] = pairs(low)
    for p in second_span:
        transposed(p)
    for p in first_span:
        transposed(p, HEAD)
    for level in range(1, 7):
        for p in range(NP):
            yb[p] = mm(xb[p], lb[p] * masks[level - 1]).astype(BF16)
        for p in range(NP):
            xb[p] = xb[p] - mm(yb[p], xb[p]).astype(BF16)
    for p in range(NP):
        updates(p)
    for p in second_span:
        maps(p)
    for p in first_span:
        to = mm(wts[p], kq[p, 0:128, :])
        last = jnp.exp(gbuf[p : p + 1, 127:128] - gbuf[p : p + 1, HEAD - 1 : HEAD])
        t1o1[p, 0:128, :] = (last * eye_f - to[0:128]).astype(BF16)
        t1o1[p, 128:256, :] = to[128:256].astype(BF16)
    for h in range(HEADS):
        d = mm(t1o1[h], t2[h])
        tos[h, 0:128, :] = d[0:128].astype(BF16)
        tos[h, 128:256, :] = (d[128:256] + o2[h]).astype(BF16)

    x_copies = []
    for r in (2, 1, 3):
        to_x = lax.rem(x + r, NX)
        copy = remote(tos.at[to_x], tin.at[x], xs_sem.at[r - 1], xr_sem.at[r - 1], (z * NX + to_x, tp))
        copy.start()
        x_copies.append(copy)
    tin[x] = tos[x]

    @pl.when(z == LOW)
    def _():
        pl.semaphore_wait(rdy, 1)
        pl.semaphore_signal(rdy, inc=1, device_id=(zdn * NX + x, tp), device_id_type=MESH)

    halo_copy.wait()
    for s in (1, 2):
        ext[s, 0:8, :] = halo[s, 8:16, :].astype(F32) * keeps[0]
    fill((1, 2), 0, 0, 16)
    for h in range(HEADS):
        keys = kq[h, 0:16, :].astype(F32)
        gcol = jnp.broadcast_to(cbuf[0:16, h : h + 1], (16, 128))
        bcol = jnp.broadcast_to(cbuf[0:16, 8 + h : 9 + h], (16, 128))
        low = bcol * jnp.exp(jnp.minimum(gcol - gbuf[h : h + 1, :], 0.0))
        low = low * mmt(kq[h, 0:16, :], kq[h, 0:128, :])
        rk = keys * bcol * jnp.exp(gcol)
        rv = vb[h, 0:16, :].astype(F32) * bcol
        ws, us = [], []
        for i in range(HEAD):
            w_row, u_row = rk[i : i + 1, :], rv[i : i + 1, :]
            for j in range(i):
                c = jnp.broadcast_to(low[i : i + 1, j : j + 1], (1, 128))
                w_row = w_row - c * ws[j]
                u_row = u_row - c * us[j]
            ws.append(w_row)
            us.append(u_row)
        end = jnp.broadcast_to(cbuf[HEAD - 1 : HEAD, h : h + 1], (8, 128))
        am[h] = jnp.zeros((32, 128), F32)
        for i in range(HEAD):
            am[h, i : i + 1, :] = -keeps[0] * ws[i]
            am[h, 8 + i : 9 + i, :] = us[i]
        tail = jnp.exp(end - gcol[0:8]) * keys[0:8]
        am[h, 16:24, :] = jnp.where(row_i[0:8] < HEAD, tail, 0.0)
        am[h, 24:32, :] = keeps[0] * jnp.exp(end)
    a_copies = []
    for r in (2, 1, 3):
        to_x = lax.rem(x + r, NX)
        copy = remote(am.at[to_x], ain.at[x], as_sem.at[r - 1], ar_sem.at[r - 1], (z * NX + to_x, tp))
        copy.start()
        a_copies.append(copy)
    ain[x] = am[x]

    corner = (row_i < HEAD) & (col_i < HEAD)
    below = (row_i >= HEAD) & (col_i < HEAD)
    for p in first_span:
        low = scores(p)
        lb[p] = jnp.where(below, low, 0.0).astype(BF16)
        low = jnp.where(corner, low, 0.0)
        yb[p] = low.astype(BF16)
        xc[p] = pairs(low)
    for p in first_span:
        transposed(p)
    for p in first_span:
        yb[p] = mm(xc[p], yb[p] * masks[0]).astype(BF16)
    for p in first_span:
        xb[p] = xb[p] + (xc[p] - eye_f.astype(BF16) - mm(yb[p], xc[p]).astype(BF16))
    for p in first_span:
        yb[p] = mm(xb[p], lb[p]).astype(BF16)
    for p in first_span:
        xb[p] = xb[p] - mm(yb[p], xb[p]).astype(BF16)
    for p in first_span:
        updates(p)
    for p in first_span:
        maps(p)

    for span in range(2):
        before = halo[0, 8:16, :] if span == 0 else proj[0, SPAN - 8 : SPAN, :]
        ext[0, 0:8, :] = before.astype(F32) * keeps[span]
        ext[0, 8:136, :] = proj[0, span * SPAN : span * SPAN + SPAN, :].astype(F32)
        fill((0,), span, 0, SPAN)
    for p in range(NP):
        a = mmt(kq[p, 128:256, :], kq[p, 0:128, :])
        pb_s[p] = jnp.where(row_i >= col_i, decays(p)[0] * a, 0.0).astype(BF16)
    for h in range(HEADS):
        for span in range(2):
            p = span * HEADS + h
            pw = mmt(pb_s[p], wub[p])
            gcol = jnp.broadcast_to(cbuf[:, p : p + 1], (128, 128))
            q = keeps[span] * (jnp.exp(gcol) * kq[p, 128:256, :].astype(F32) - pw[:, 0:128])
            if span == 0:
                qfin[h, 0:128, :] = q.astype(BF16)
                lfin[h, 0:128, :] = pw[:, 128:256]
            else:
                q2 = mmt(q.astype(BF16), t1o1[h])
                qfin[h, 128:256, :] = q2[:, 0:128].astype(BF16)
                lfin[h, 128:256, :] = pw[:, 128:256] + q2[:, 128:256]
    loads[1].wait()
    for h in range(HEADS):
        cols = pl.ds(h * 128, 128)
        sg[h] = silu(gate[:, cols].astype(F32)) * gain_ref[0:1, :]

    for copy in x_copies:
        copy.wait()
    for copy in a_copies:
        copy.wait()

    for j in range(NX):
        ab[j] = mm(ain[j, 16:24, :].astype(BF16), tin[j, 0:128, :])
    for j in range(NX):
        wu = jnp.concatenate([ain[j, 0:8, :], ain[j, 8:16, :]], axis=1).astype(BF16)
        low = lax.dot_general(wu, ab[j].astype(BF16), (((0,), (0,)), ((), ())), preferred_element_type=F32)
        mb[j, 0:128, :] = (tin[j, 0:128, :].astype(F32) * ain[j, 24:25, :] + low[0:128]).astype(BF16)
        mb[j, 128:256, :] = (tin[j, 128:256, :].astype(F32) + low[128:256]).astype(BF16)
    pt[0] = eye_f.astype(BF16)
    po[0] = jnp.zeros((128, 128), F32)
    pt[1] = mb[0, 0:128, :]
    po[1] = mb[0, 128:256, :].astype(F32)
    cur = mb[0]
    for j in range(1, NX):
        step = mm(cur, mb[j, 0:128, :])
        off = step[128:256] + mb[j, 128:256, :].astype(F32)
        if j < NX - 1:
            pt[j + 1] = step[0:128].astype(BF16)
            po[j + 1] = off
            cur = jnp.concatenate([step[0:128], off], axis=0).astype(BF16)
        else:
            rowt[...] = step[0:128].astype(BF16)
            rowo[...] = off

    crows = 128 // RCH
    prows = 256 // PCH

    def s_copy(i, to, k):
        part = pl.ds(i * crows, crows)
        return remote(snd.at[part, :], srx.at[part, :], zs_sem.at[i, k], zr_sem.at[i], (to * NX + x, tp))

    def p_copy(i):
        part = pl.ds(i * prows, prows)
        return remote(psnd.at[part, :], prx.at[part, :], ps_sem.at[i], pr_sem.at[i], (zup * NX + x, tp))

    @pl.when(z == 0)
    def _():
        snd[...] = rowo[...].astype(BF16)
        pl.semaphore_wait(rdy, 1)
        for i in range(RCH):
            s_copy(i, zup, 0).start()
        srx[...] = jnp.zeros((128, 128), BF16)

    @pl.when(z == LOW)
    def _():
        psnd[0:128, :] = rowt[...]
        psnd[128:256, :] = rowo[...].astype(BF16)
        for i in range(PCH):
            p_copy(i).start()

    @pl.when(z <= LOW)
    def _():
        prx[0:128, :] = eye_f.astype(BF16)
        prx[128:256, :] = jnp.zeros((128, 128), BF16)

    @pl.when(z > LOW)
    def _():
        for i in range(PCH):
            part = pl.ds(i * prows, prows)
            p_copy(i).wait_recv()

            @pl.when(z < nz - 1)
            def _():
                new = mm(prx[part, :], rowt[...])
                if i * prows >= 128:
                    new = new + rowo[i * prows - 128 : (i + 1) * prows - 128, :]
                psnd[part, :] = new.astype(BF16)
                p_copy(i).start()

    for j in range(NX):
        new = mm(prx[...], pt[j])
        qt[j] = new[0:128].astype(BF16)
        qo[j] = new[128:256] + po[j]

    @pl.when(z == LOW - 1)
    def _():
        pl.semaphore_wait(rdy, 1)

    def e_copy(r, i, to_x):
        part = pl.ds(i * crows, crows)
        return remote(
            es.at[r - 1, part, :], ein.at[x, part, :], es_sem.at[r - 1, i], er_sem.at[r - 1, i], (z * NX + to_x, tp)
        )

    e_copies = {}
    for i in range(RCH):
        part = pl.ds(i * crows, crows)

        @pl.when(z > 0)
        def _():
            s_copy(i, zup, 0).wait_recv()

        @pl.when((z > 0) & (z < LOW))
        def _():
            snd[part, :] = (mm(srx[part, :], rowt[...]) + rowo[part, :]).astype(BF16)

        @pl.when((z > 0) & (z < LOW - 1))
        def _():
            s_copy(i, zup, 0).start()

        @pl.when(z == LOW - 1)
        def _():
            for far in range(nz - 1, LOW - 1, -1):
                s_copy(i, far, far - LOW).start()

        for r in (2, 1, 3):
            to_x = lax.rem(x + r, NX)
            es[r - 1, part, :] = (mm(srx[part, :], qt[to_x]) + qo[to_x, part, :]).astype(BF16)
            e_copies[r, i] = e_copy(r, i, to_x)
            e_copies[r, i].start()
        ein[x, part, :] = (mm(srx[part, :], qt[x]) + qo[x, part, :]).astype(BF16)

    mean_ones = jnp.full((128, 128), 1.0 / 128.0, BF16)
    n_copies = []
    for r in (0, 1, 3, 2):
        head = lax.rem(x + NX - r, NX)
        if r > 0:
            for i in range(RCH):
                e_copies[r, i].wait_recv()
        att = mmt(qfin[head], ein[head]) + lfin[head]
        ms = mm((att * att).astype(BF16), mean_ones)
        nrm = (att * lax.rsqrt(ms + 1e-05) * sg[head]).astype(BF16)
        cols = pl.ds(pl.multiple_of(head * 128, 128), 128)
        for c in range(2):
            for b in range(NY):
                lo = b * 64 + c * 32
                nb[c, b * 32 : b * 32 + 32, cols] = nrm[lo : lo + 32, :]
        copy = remote(
            nb.at[other, :, cols], nrx.at[:, cols], ns_sem.at[r], nr_sem.at[r], (ctx, y * 2 + other)
        )
        copy.start()
        n_copies.append(copy)

    loads[2].wait()
    for b in range(NBLK):
        cols = pl.ds(b * BLK, BLK)
        acc[:, cols] = mm(nb[core], w_own[:, cols])
    w_copy.wait()
    for copy in n_copies:
        copy.wait()

    order = (0, 4, 1, 5, 2, 6, 3, 7)
    half = NBLK // 2
    o_copies, d_copies, c_copies, f_copies = {}, {}, {}, []
    for b in order:
        cols = pl.ds(b * BLK, BLK)
        res = (acc[:, cols] + mm(nrx[...], w_par[:, cols])).astype(BF16)
        for d in range(NY):
            pb[b, d] = res[d * 32 : d * 32 + 32, :]
        first, second = (right, left) if b < half else (left, right)
        o_copies[b] = remote(
            pb.at[b, opp], rxo.at[b], rs_sem.at[0, b], rr_sem.at[0, b], (ctx, first * 2 + core)
        )
        o_copies[b].start()
        d_copies[b] = remote(
            pb.at[b, second], rx1.at[:, cols], rs_sem.at[1, b], rr_sem.at[1, b], (ctx, second * 2 + core)
        )
        d_copies[b].start()
        f_copies.append(pltpu.make_async_copy(pb.at[b, y], own_out.at[:, cols], fsem.at[b]))
        f_copies[-1].start()
    for b in order:
        first = right if b < half else left
        cols = pl.ds(b * BLK, BLK)
        o_copies[b].wait_recv()
        cs[b] = (pb[b, first].astype(F32) + rxo[b].astype(F32)).astype(BF16)
        c_copies[b] = remote(
            cs.at[b], rx2.at[:, cols], rs_sem.at[2, b], rr_sem.at[2, b], (ctx, first * 2 + core)
        )
        c_copies[b].start()
    for b in order:
        d_copies[b].wait_recv()
        c_copies[b].wait_recv()

    for copy in f_copies:
        copy.wait()

    @pl.when(z < LOW - 1)
    def _():
        for i in range(RCH):
            s_copy(i, zup, 0).wait_send()

    @pl.when(z == LOW - 1)
    def _():
        for i in range(RCH):
            for far in range(LOW, nz):
                s_copy(i, far, far - LOW).wait_send()

    @pl.when((z >= LOW) & (z < nz - 1))
    def _():
        for i in range(PCH):
            p_copy(i).wait_send()

    for copy in e_copies.values():
        copy.wait_send()
    for b in order:
        o_copies[b].wait_send()
        d_copies[b].wait_send()
        c_copies[b].wait_send()


def body(nz, projected, conv_weight, log_decay, write_rate, doc_bounds, out_gate, norm_gain, out_weight):
    v = pltpu.VMEM
    dma = pltpu.SemaphoreType.DMA
    vspec = pl.BlockSpec(memory_space=pltpu.VMEM)
    aspec = pl.BlockSpec(memory_space=pl.ANY)
    scratch = [
        v((3, TAPS, 512), F32), v((HEADS, 256), F32), v((HEADS, 256), F32),
        pltpu.SMEM((2, 8), jnp.int32), v((1, 128), F32),
        v((3, 256, 512), BF16), v((3, 16, 512), BF16), v((3, 136, 512), F32), v((256, 512), BF16),
        v((512, 4096), BF16), v((512, 4096), BF16),
        v((128, 128), F32), v((128, 128), F32), v((6, 128, 128), BF16),
        v((NP, 256, 128), BF16), v((NP, 256, 128), BF16), v((NP, 128, 128), BF16),
        v((NP, 128, 128), BF16), v((NP, 128, 128), BF16), v((NP, 128, 128), BF16), v((NP, 128, 128), BF16),
        v((HEADS, 128, 128), BF16),
        v((NP, 256, 128), BF16), v((NP, 256, 128), BF16),
        v((HEADS, 256, 128), BF16), v((HEADS, 128, 128), BF16), v((HEADS, 128, 128), F32),
        v((HEADS, 256, 128), BF16), v((NX, 256, 128), BF16),
        v((HEADS, 32, 128), F32), v((NX, 32, 128), F32), v((NX, 8, 128), F32), v((NX, 256, 128), BF16),
        v((NX, 128, 128), BF16), v((NX, 128, 128), F32), v((NX, 128, 128), BF16), v((NX, 128, 128), F32),
        v((128, 128), BF16), v((128, 128), F32), v((256, 128), BF16), v((256, 128), BF16),
        v((128, 128), BF16), v((128, 128), BF16), v((NX - 1, 128, 128), BF16), v((NX, 128, 128), BF16),
        v((HEADS, 256, 128), BF16), v((HEADS, 256, 128), F32), v((HEADS, 256, 128), F32),
        v((2, 128, 512), BF16), v((128, 512), BF16), v((128, 4096), F32),
        v((NBLK, NY, 32, BLK), BF16), v((NBLK, 32, BLK), BF16), v((NBLK, 32, BLK), BF16),
        dma((8,)), dma((2,)), dma((2,)), dma((3,)), dma((3,)), dma((3,)), dma((3,)), dma((RCH, nz - LOW)), dma((RCH,)),
        dma((PCH,)), dma((PCH,)), pltpu.SemaphoreType.REGULAR, dma((NBLK,)),
        dma((3, RCH)), dma((3, RCH)), dma((4,)), dma((4,)), dma((3, NBLK)), dma((3, NBLK)),
    ]
    half = jax.ShapeDtypeStruct((32, 4096), BF16)
    own, one, two = pl.pallas_call(
        functools.partial(kernel, nz),
        out_shape=(half, half, half),
        in_specs=[aspec] * 8,
        out_specs=(aspec, aspec, aspec),
        scratch_shapes=scratch,
        compiler_params=pltpu.CompilerParams(
            collective_id=0, has_side_effects=True, vmem_limit_bytes=56 * 1024 * 1024
        ),
    )(
        projected, conv_weight, log_decay, write_rate, doc_bounds.T, out_gate,
        norm_gain.reshape(1, -1), out_weight,
    )
    return (own.astype(F32) + one.astype(F32) + two.astype(F32)).astype(BF16)


def solution(mesh):
    in_specs = (
        P(None, "ctx", "tp"),
        P(None, None, "tp"),
        P("tp", "ctx"),
        P("tp", "ctx"),
        P(),
        P("ctx", "tp"),
        P(),
        P("tp", None),
    )
    out_specs = P(("ctx", "tp"), None)
    nz = mesh.shape["ctx"] // NX
    return jax.shard_map(
        functools.partial(body, nz), mesh=mesh, in_specs=in_specs, out_specs=out_specs, check_vma=False
    )
```

```python
import functools

import jax
import jax.numpy as jnp
from jax import lax
from jax.experimental import pallas as pl
from jax.experimental.pallas import tpu as pltpu
from jax.sharding import PartitionSpec as P

MESH = pl.DeviceIdType.MESH
F32 = jnp.float32
BF16 = jnp.bfloat16
SPAN = 128
TAPS = 4
NX = 4
NY = 4
HEADS = 4
NP = 8
BLK = 1024
NBLK = 4
RCH = 1
HEAD = 4


def mm(a, b):
    return lax.dot_general(a, b, (((1,), (0,)), ((), ())), preferred_element_type=F32)


def mmt(a, b):
    return lax.dot_general(a, b, (((1,), (1,)), ((), ())), preferred_element_type=F32)


def silu(u):
    return u / (1.0 + jnp.exp(-u))


def kernel(
    nz, proj_hbm, cw_hbm, ld_hbm, wr_hbm, db_hbm, gate_hbm, gain_hbm, w_hbm, own_out, rx1, rx2,
    cw_ref, ld_ref, wr_ref, db_ref, gain_ref,
    proj, halo, ext, gate, w_own, w_par,
    gbuf, cbuf, masks, kq, rt, vb, lb, pb_s, xb, yb, xc, wub, wts, t1o1, t2, o2, tos, tin, am, ain, ab, mb,
    pt, po, qt, qo, rowm, abuf, bbuf, mid, prx, srx, snd, es, ein, qfin, lfin, sg,
    nb, nrx, acc, pb, rxo, cs,
    lsem, hsem, wsem, xs_sem, xr_sem, as_sem, ar_sem, zs_sem, zr_sem, ps_sem, pr_sem, rdy, fsem, es_sem, er_sem, ns_sem, nr_sem, rs_sem, rr_sem,
):
    ctx = lax.axis_index("ctx")
    tp = lax.axis_index("tp")
    z, x = lax.div(ctx, NX), lax.rem(ctx, NX)
    y, core = lax.div(tp, 2), lax.rem(tp, 2)
    nctx = nz * NX
    nxt = lax.rem(ctx + 1, nctx)
    prv = lax.rem(ctx + nctx - 1, nctx)
    zup = lax.rem(z + 1, nz)
    zdn = lax.rem(z + nz - 1, nz)
    right = lax.rem(y + 1, NY)
    left = lax.rem(y + NY - 1, NY)
    opp = lax.rem(y + 2, NY)
    other = 1 - core

    def remote(src, dst, ssem, rsem, device):
        return pltpu.make_async_remote_copy(
            src_ref=src, dst_ref=dst, send_sem=ssem, recv_sem=rsem,
            device_id=device, device_id_type=MESH,
        )

    barrier = pltpu.get_barrier_semaphore()
    peers = [(nxt, tp), (prv, tp)]
    peers += [(z * NX + lax.rem(x + r, NX), tp) for r in range(1, NX)]
    peers += [(zup * NX + x, tp), (zdn * NX + x, tp)]
    peers += [(ctx, right * 2 + core), (ctx, left * 2 + core), (ctx, y * 2 + other)]
    for device in peers:
        pl.semaphore_signal(barrier, inc=1, device_id=device, device_id_type=MESH)

    loads = [
        pltpu.make_async_copy(proj_hbm, proj, lsem.at[0]),
        pltpu.make_async_copy(gate_hbm, gate, lsem.at[1]),
        pltpu.make_async_copy(w_hbm, w_own, lsem.at[2]),
    ]
    small = [
        pltpu.make_async_copy(ld_hbm, ld_ref, lsem.at[3]),
        pltpu.make_async_copy(wr_hbm, wr_ref, lsem.at[4]),
        pltpu.make_async_copy(db_hbm, db_ref, lsem.at[5]),
        pltpu.make_async_copy(cw_hbm, cw_ref, lsem.at[6]),
        pltpu.make_async_copy(gain_hbm, gain_ref, lsem.at[7]),
    ]
    for copy in small:
        copy.start()
    loads[0].start()

    row_i = lax.broadcasted_iota(jnp.int32, (128, 128), 0)
    col_i = lax.broadcasted_iota(jnp.int32, (128, 128), 1)
    eye = row_i == col_i
    eye_f = jnp.where(eye, 1.0, 0.0)
    for level in range(1, 7):
        low = lax.shift_right_logical(row_i, level)
        low_j = lax.shift_right_logical(col_i, level)
        same = lax.shift_right_logical(row_i, level + 1) == lax.shift_right_logical(col_i, level + 1)
        masks[level - 1] = jnp.where(same & (low > low_j), 1.0, 0.0).astype(BF16)

    for copy in small:
        copy.wait()

    gbuf[...] = jnp.zeros((128, 128), F32)
    gbuf[0:4, :] = ld_ref[:, 0:128]
    gbuf[4:8, :] = ld_ref[:, 128:256]
    gbuf[8:12, :] = wr_ref[:, 0:128]
    gbuf[12:16, :] = wr_ref[:, 128:256]
    run = gbuf[0:8, :]
    lane = lax.broadcasted_iota(jnp.int32, (8, 128), 1)
    for step in (1, 2, 4, 8, 16, 32, 64):
        run = run + jnp.where(lane >= step, pltpu.roll(run, step, 1), 0.0)
    gbuf[0:8, :] = run
    cbuf[...] = gbuf[...].T

    keeps = []
    for span in range(2):
        hit = jnp.int32(0)
        for d in range(db_ref.shape[1]):
            hit = hit + jnp.where(db_ref[0, d] == ctx * 2 + span, 1, 0)
        keeps.append(1.0 - jnp.minimum(hit, 1).astype(F32))

    ones = jnp.full((128, 128), 1.0, BF16)

    def activate(s, h, first, count):
        cols = pl.ds(h * 128, 128)
        u = cw_ref[s, 0:1, cols] * ext[s, 8 + first : 8 + first + count, cols]
        for j in range(1, TAPS):
            lo = 8 + first - j
            u = u + cw_ref[s, j : j + 1, cols] * ext[s, lo : lo + count, cols]
        return silu(u)

    def unit(a):
        ss = mm((a * a).astype(BF16), ones)
        return (a * lax.rsqrt(ss + 1e-06)).astype(BF16)

    def fill(streams, span, first, count):
        for s in streams:
            for h in range(HEADS):
                p = span * HEADS + h
                a = activate(s, h, first, count)
                if s == 1:
                    kq[p, first : first + count, :] = unit(a)
                elif s == 0:
                    kq[p, 128 + first : 128 + first + count, :] = unit(a)
                else:
                    vb[p, first : first + count, :] = a.astype(BF16)

    def transposed(p, skip=0):
        beta = gbuf[8 + p : 9 + p, :]
        g = gbuf[p : p + 1, :]
        if skip:
            g = g - g[:, skip - 1 : skip]
            beta = jnp.where(col_i[0:1, :] >= skip, beta, 0.0)
        scale = beta * jnp.exp(g)
        rt[p, 0:128, :] = (kq[p, 0:128, :].astype(F32).T * scale).astype(BF16)
        rt[p, 128:256, :] = (vb[p].astype(F32).T * beta).astype(BF16)

    def decays(p):
        gcol = jnp.broadcast_to(cbuf[:, p : p + 1], (128, 128))
        bcol = jnp.broadcast_to(cbuf[:, 8 + p : 9 + p], (128, 128))
        dm = jnp.exp(jnp.minimum(gcol - gbuf[p : p + 1, :], 0.0))
        return dm, bcol * dm

    def scores(p):
        a = mmt(kq[p, 0:128, :], kq[p, 0:128, :])
        return jnp.where(row_i > col_i, decays(p)[1] * a, 0.0)

    def pairs(low):
        pair = lax.shift_right_logical(row_i, 1) == lax.shift_right_logical(col_i, 1)
        return (eye_f - jnp.where(pair, low, 0.0)).astype(BF16)

    def updates(p):
        wu = mmt(rt[p], xb[p])
        wub[p] = wu.astype(BF16)
        g = gbuf[p : p + 1, :]
        wts[p] = (wu * jnp.exp(g[:, 127:128] - g)).astype(BF16)

    def maps(p):
        span, h = p // HEADS, p % HEADS
        to = mm(wts[p], kq[p, 0:128, :])
        last = jnp.exp(gbuf[p : p + 1, 127:128])
        t = keeps[span] * (last * eye_f - to[0:128])
        if span == 0:
            t1o1[h, 0:128, :] = t.astype(BF16)
            t1o1[h, 128:256, :] = to[128:256].astype(BF16)
        else:
            t2[h] = t.astype(BF16)
            o2[h] = to[128:256]

    first_span = range(HEADS)
    second_span = range(HEADS, NP)

    rows = proj_hbm.shape[1]
    halo_copy = remote(proj_hbm.at[:, pl.ds(rows - 16, 16), :], halo, hsem.at[0], hsem.at[1], (nxt, tp))
    w_copy = remote(w_hbm, w_par, wsem.at[0], wsem.at[1], (ctx, y * 2 + other))

    def enter():
        pl.semaphore_wait(barrier, len(peers))
        halo_copy.start()
        loads[1].start()
        loads[2].start()
        w_copy.start()

        @pl.when((z == 1) | (z == 6))
        def _():
            pl.semaphore_signal(rdy, inc=1, device_id=(zdn * NX + x, tp), device_id_type=MESH)

    def word_from_above(row):
        @pl.when(z == row)
        def _():
            pl.semaphore_wait(rdy, 1)
            if row > 2:
                pl.semaphore_signal(rdy, inc=1, device_id=(zdn * NX + x, tp), device_id_type=MESH)

    loads[0].wait()
    for span in (1, 0):
        for s in (1, 2):
            if span == 0:
                ext[s, 0:8, :] = jnp.zeros((8, 512), F32)
            else:
                ext[s, 0:8, :] = proj[s, SPAN - 8 : SPAN, :].astype(F32) * keeps[1]
            ext[s, 8:136, :] = proj[s, span * SPAN : span * SPAN + SPAN, :].astype(F32)
        fill((1, 2), span, 0, SPAN)
        if span == 1:
            enter()
    for p in range(NP):
        low = scores(p)
        if p < HEADS:
            low = jnp.where(col_i >= HEAD, low, 0.0)
        lb[p] = low.astype(BF16)
        xb[p] = pairs(low)
    for p in second_span:
        transposed(p)
    for p in first_span:
        transposed(p, HEAD)
    for level in range(1, 7):
        for p in range(NP):
            yb[p] = mm(xb[p], lb[p] * masks[level - 1]).astype(BF16)
        for p in range(NP):
            xb[p] = xb[p] - mm(yb[p], xb[p]).astype(BF16)
    for p in range(NP):
        updates(p)
    for p in second_span:
        maps(p)
    for p in first_span:
        to = mm(wts[p], kq[p, 0:128, :])
        last = jnp.exp(gbuf[p : p + 1, 127:128] - gbuf[p : p + 1, HEAD - 1 : HEAD])
        t1o1[p, 0:128, :] = (last * eye_f - to[0:128]).astype(BF16)
        t1o1[p, 128:256, :] = to[128:256].astype(BF16)
    for h in range(HEADS):
        d = mm(t1o1[h], t2[h])
        tos[h, 0:128, :] = d[0:128].astype(BF16)
        tos[h, 128:256, :] = (d[128:256] + o2[h]).astype(BF16)

    x_copies = []
    for r in (2, 1, 3):
        to_x = lax.rem(x + r, NX)
        copy = remote(tos.at[to_x], tin.at[x], xs_sem.at[r - 1], xr_sem.at[r - 1], (z * NX + to_x, tp))
        copy.start()
        x_copies.append(copy)
    tin[x] = tos[x]

    word_from_above(5)

    halo_copy.wait()
    for s in (1, 2):
        ext[s, 0:8, :] = halo[s, 8:16, :].astype(F32) * keeps[0]
    fill((1, 2), 0, 0, 16)
    for h in range(HEADS):
        keys = kq[h, 0:16, :].astype(F32)
        gcol = jnp.broadcast_to(cbuf[0:16, h : h + 1], (16, 128))
        bcol = jnp.broadcast_to(cbuf[0:16, 8 + h : 9 + h], (16, 128))
        low = bcol * jnp.exp(jnp.minimum(gcol - gbuf[h : h + 1, :], 0.0))
        low = low * mmt(kq[h, 0:16, :], kq[h, 0:128, :])
        rk = keys * bcol * jnp.exp(gcol)
        rv = vb[h, 0:16, :].astype(F32) * bcol
        ws, us = [], []
        for i in range(HEAD):
            w_row, u_row = rk[i : i + 1, :], rv[i : i + 1, :]
            for j in range(i):
                c = jnp.broadcast_to(low[i : i + 1, j : j + 1], (1, 128))
                w_row = w_row - c * ws[j]
                u_row = u_row - c * us[j]
            ws.append(w_row)
            us.append(u_row)
        end = jnp.broadcast_to(cbuf[HEAD - 1 : HEAD, h : h + 1], (8, 128))
        am[h] = jnp.zeros((32, 128), F32)
        for i in range(HEAD):
            am[h, i : i + 1, :] = -keeps[0] * ws[i]
            am[h, 8 + i : 9 + i, :] = us[i]
        tail = jnp.exp(end - gcol[0:8]) * keys[0:8]
        am[h, 16:24, :] = jnp.where(row_i[0:8] < HEAD, tail, 0.0)
        am[h, 24:32, :] = keeps[0] * jnp.exp(end)
    a_copies = []
    for r in (2, 1, 3):
        to_x = lax.rem(x + r, NX)
        copy = remote(am.at[to_x], ain.at[x], as_sem.at[r - 1], ar_sem.at[r - 1], (z * NX + to_x, tp))
        copy.start()
        a_copies.append(copy)
    ain[x] = am[x]
    word_from_above(4)

    corner = (row_i < HEAD) & (col_i < HEAD)
    below = (row_i >= HEAD) & (col_i < HEAD)
    for p in first_span:
        low = scores(p)
        lb[p] = jnp.where(below, low, 0.0).astype(BF16)
        low = jnp.where(corner, low, 0.0)
        yb[p] = low.astype(BF16)
        xc[p] = pairs(low)
    for p in first_span:
        transposed(p)
    for p in first_span:
        yb[p] = mm(xc[p], yb[p] * masks[0]).astype(BF16)
    for p in first_span:
        xb[p] = xb[p] + (xc[p] - eye_f.astype(BF16) - mm(yb[p], xc[p]).astype(BF16))
    for p in first_span:
        yb[p] = mm(xb[p], lb[p]).astype(BF16)
    for p in first_span:
        xb[p] = xb[p] - mm(yb[p], xb[p]).astype(BF16)
    for p in first_span:
        updates(p)
    for p in first_span:
        maps(p)

    word_from_above(3)

    for span in range(2):
        before = halo[0, 8:16, :] if span == 0 else proj[0, SPAN - 8 : SPAN, :]
        ext[0, 0:8, :] = before.astype(F32) * keeps[span]
        ext[0, 8:136, :] = proj[0, span * SPAN : span * SPAN + SPAN, :].astype(F32)
        fill((0,), span, 0, SPAN)
    for p in range(NP):
        a = mmt(kq[p, 128:256, :], kq[p, 0:128, :])
        pb_s[p] = jnp.where(row_i >= col_i, decays(p)[0] * a, 0.0).astype(BF16)
    for h in range(HEADS):
        for span in range(2):
            p = span * HEADS + h
            pw = mmt(pb_s[p], wub[p])
            gcol = jnp.broadcast_to(cbuf[:, p : p + 1], (128, 128))
            q = keeps[span] * (jnp.exp(gcol) * kq[p, 128:256, :].astype(F32) - pw[:, 0:128])
            if span == 0:
                qfin[h, 0:128, :] = q.astype(BF16)
                lfin[h, 0:128, :] = pw[:, 128:256]
            else:
                q2 = mmt(q.astype(BF16), t1o1[h])
                qfin[h, 128:256, :] = q2[:, 0:128].astype(BF16)
                lfin[h, 128:256, :] = pw[:, 128:256] + q2[:, 128:256]
    word_from_above(2)
    word_from_above(0)
    loads[1].wait()
    for h in range(HEADS):
        cols = pl.ds(h * 128, 128)
        sg[h] = silu(gate[:, cols].astype(F32)) * gain_ref[0:1, :]

    for copy in x_copies:
        copy.wait()
    for copy in a_copies:
        copy.wait()

    for j in range(NX):
        ab[j] = mm(ain[j, 16:24, :].astype(BF16), tin[j, 0:128, :])
    for j in range(NX):
        wu = jnp.concatenate([ain[j, 0:8, :], ain[j, 8:16, :]], axis=1).astype(BF16)
        low = lax.dot_general(wu, ab[j].astype(BF16), (((0,), (0,)), ((), ())), preferred_element_type=F32)
        mb[j, 0:128, :] = (tin[j, 0:128, :].astype(F32) * ain[j, 24:25, :] + low[0:128]).astype(BF16)
        mb[j, 128:256, :] = (tin[j, 128:256, :].astype(F32) + low[128:256]).astype(BF16)
    pt[0] = eye_f.astype(BF16)
    po[0] = jnp.zeros((128, 128), F32)
    pt[1] = mb[0, 0:128, :]
    po[1] = mb[0, 128:256, :].astype(F32)
    cur = mb[0]
    for j in range(1, NX):
        step = mm(cur, mb[j, 0:128, :])
        off = step[128:256] + mb[j, 128:256, :].astype(F32)
        pt[j + 1] = step[0:128].astype(BF16)
        po[j + 1] = off
        cur = jnp.concatenate([step[0:128], off], axis=0).astype(BF16)
    rowm[...] = cur

    crows = 128 // RCH

    def s_copy(i, to, k):
        part = pl.ds(i * crows, crows)
        return remote(snd.at[part, :], srx.at[part, :], zs_sem.at[i, k], zr_sem.at[i], (to * NX + x, tp))

    def m_copy(src, dst, k, slot, to):
        return remote(src, dst, ps_sem.at[k], pr_sem.at[slot], (to * NX + x, tp))

    def chain(first, second):
        new = mm(first[...], second[0:128, :])
        return new[0:128], new[128:256] + second[128:256, :].astype(F32)

    @pl.when(z == 0)
    def _():
        snd[...] = po[NX].astype(BF16)
        for i in range(RCH):
            s_copy(i, 2, 1).start()
            s_copy(i, 1, 0).start()
        srx[...] = jnp.zeros((128, 128), BF16)

    @pl.when(z == 1)
    def _():
        m_copy(rowm, abuf, 0, 0, 2).start()

    @pl.when(z == 3)
    def _():
        m_copy(rowm, abuf, 0, 0, 4).start()
        m_copy(rowm, abuf, 1, 0, 5).start()

    @pl.when(z == 4)
    def _():
        m_copy(rowm, bbuf, 0, 1, 5).start()

    @pl.when(z == 5)
    def _():
        m_copy(rowm, bbuf, 0, 1, 6).start()

    @pl.when((z == 0) | (z == 1) | (z == 3))
    def _():
        abuf[0:128, :] = eye_f.astype(BF16)
        abuf[128:256, :] = jnp.zeros((128, 128), BF16)

    @pl.when(z < 5)
    def _():
        bbuf[0:128, :] = eye_f.astype(BF16)
        bbuf[128:256, :] = jnp.zeros((128, 128), BF16)

    @pl.when(z == 4)
    def _():
        m_copy(rowm, abuf, 0, 0, 4).wait_recv()
        t, o = chain(abuf, rowm)
        mid[0:128, :] = t.astype(BF16)
        mid[128:256, :] = o.astype(BF16)
        m_copy(mid, abuf, 1, 0, 7).start()
        m_copy(mid, abuf, 2, 0, 6).start()

    @pl.when(z == 6)
    def _():
        m_copy(rowm, bbuf, 0, 1, 6).wait_recv()
        t, o = chain(bbuf, rowm)
        mid[0:128, :] = t.astype(BF16)
        mid[128:256, :] = o.astype(BF16)
        m_copy(mid, bbuf, 0, 1, 7).start()

    @pl.when((z == 2) | (z > 4))
    def _():
        m_copy(rowm, abuf, 0, 0, 2).wait_recv()

    @pl.when((z == 5) | (z == 7))
    def _():
        m_copy(rowm, bbuf, 0, 1, 5).wait_recv()

    t, o = chain(abuf, bbuf)
    prx[0:128, :] = t.astype(BF16)
    prx[128:256, :] = o.astype(BF16)
    for j in range(NX + 1):
        new = mm(prx[...], pt[j])
        qt[j] = new[0:128].astype(BF16)
        qo[j] = new[128:256] + po[j]

    for i in range(RCH):
        part = pl.ds(i * crows, crows)

        @pl.when(z > 0)
        def _():
            s_copy(i, 1, 0).wait_recv()

        @pl.when(z == 2)
        def _():
            snd[part, :] = (mm(srx[part, :], qt[NX]) + qo[NX, part, :]).astype(BF16)
            for far in range(7, 2, -1):
                s_copy(i, far, far - 3).start()

    def e_copy(r, i, to_x):
        return remote(es.at[r - 1], ein.at[x], es_sem.at[r - 1, i], er_sem.at[r - 1, i], (z * NX + to_x, tp))

    e_copies = {}
    for r in (2, 1, 3):
        to_x = lax.rem(x + r, NX)
        es[r - 1] = (mm(srx[...], qt[to_x]) + qo[to_x]).astype(BF16)
        e_copies[r, 0] = e_copy(r, 0, to_x)
        e_copies[r, 0].start()
    ein[x] = (mm(srx[...], qt[x]) + qo[x]).astype(BF16)

    mean_ones = jnp.full((128, 128), 1.0 / 128.0, BF16)
    n_copies = []
    for r in (0, 1, 3, 2):
        head = lax.rem(x + NX - r, NX)
        if r > 0:
            e_copies[r, 0].wait_recv()
        att = mmt(qfin[head], ein[head]) + lfin[head]
        ms = mm((att * att).astype(BF16), mean_ones)
        nrm = (att * lax.rsqrt(ms + 1e-05) * sg[head]).astype(BF16)
        cols = pl.ds(pl.multiple_of(head * 128, 128), 128)
        for c in range(2):
            for b in range(NY):
                lo = b * 64 + c * 32
                nb[c, b * 32 : b * 32 + 32, cols] = nrm[lo : lo + 32, :]
        copy = remote(
            nb.at[other, :, cols], nrx.at[:, cols], ns_sem.at[r], nr_sem.at[r], (ctx, y * 2 + other)
        )
        copy.start()
        n_copies.append(copy)

    loads[2].wait()
    for b in range(NBLK):
        cols = pl.ds(b * BLK, BLK)
        acc[:, cols] = mm(nb[core], w_own[:, cols])
    w_copy.wait()
    for copy in n_copies:
        copy.wait()

    order = (0, 2, 1, 3)
    half = NBLK // 2
    o_copies, d_copies, c_copies, f_copies = {}, {}, {}, []
    for b in order:
        cols = pl.ds(b * BLK, BLK)
        res = (acc[:, cols] + mm(nrx[...], w_par[:, cols])).astype(BF16)
        for d in range(NY):
            pb[b, d] = res[d * 32 : d * 32 + 32, :]
        first, second = (right, left) if b < half else (left, right)
        o_copies[b] = remote(
            pb.at[b, opp], rxo.at[b], rs_sem.at[0, b], rr_sem.at[0, b], (ctx, first * 2 + core)
        )
        o_copies[b].start()
        d_copies[b] = remote(
            pb.at[b, second], rx1.at[:, cols], rs_sem.at[1, b], rr_sem.at[1, b], (ctx, second * 2 + core)
        )
        d_copies[b].start()
        f_copies.append(pltpu.make_async_copy(pb.at[b, y], own_out.at[:, cols], fsem.at[b]))
        f_copies[-1].start()
    for b in order:
        first = right if b < half else left
        cols = pl.ds(b * BLK, BLK)
        o_copies[b].wait_recv()
        cs[b] = (pb[b, first].astype(F32) + rxo[b].astype(F32)).astype(BF16)
        c_copies[b] = remote(
            cs.at[b], rx2.at[:, cols], rs_sem.at[2, b], rr_sem.at[2, b], (ctx, first * 2 + core)
        )
        c_copies[b].start()
    for b in order:
        d_copies[b].wait_recv()
        c_copies[b].wait_recv()

    for copy in f_copies:
        copy.wait()

    for row, count in ((0, 2), (2, 5)):
        @pl.when(z == row)
        def _():
            for i in range(RCH):
                for k in range(count):
                    s_copy(i, 1, k).wait_send()

    for row, count in ((1, 1), (3, 2), (4, 3), (5, 1), (6, 1)):
        @pl.when(z == row)
        def _():
            for k in range(count):
                m_copy(rowm, abuf, k, 0, 2).wait_send()

    for copy in e_copies.values():
        copy.wait_send()
    for b in order:
        o_copies[b].wait_send()
        d_copies[b].wait_send()
        c_copies[b].wait_send()


def body(nz, projected, conv_weight, log_decay, write_rate, doc_bounds, out_gate, norm_gain, out_weight):
    v = pltpu.VMEM
    dma = pltpu.SemaphoreType.DMA
    vspec = pl.BlockSpec(memory_space=pltpu.VMEM)
    aspec = pl.BlockSpec(memory_space=pl.ANY)
    scratch = [
        v((3, TAPS, 512), F32), v((HEADS, 256), F32), v((HEADS, 256), F32),
        pltpu.SMEM((2, 8), jnp.int32), v((1, 128), F32),
        v((3, 256, 512), BF16), v((3, 16, 512), BF16), v((3, 136, 512), F32), v((256, 512), BF16),
        v((512, 4096), BF16), v((512, 4096), BF16),
        v((128, 128), F32), v((128, 128), F32), v((6, 128, 128), BF16),
        v((NP, 256, 128), BF16), v((NP, 256, 128), BF16), v((NP, 128, 128), BF16),
        v((NP, 128, 128), BF16), v((NP, 128, 128), BF16), v((NP, 128, 128), BF16), v((NP, 128, 128), BF16),
        v((HEADS, 128, 128), BF16),
        v((NP, 256, 128), BF16), v((NP, 256, 128), BF16),
        v((HEADS, 256, 128), BF16), v((HEADS, 128, 128), BF16), v((HEADS, 128, 128), F32),
        v((HEADS, 256, 128), BF16), v((NX, 256, 128), BF16),
        v((HEADS, 32, 128), F32), v((NX, 32, 128), F32), v((NX, 8, 128), F32), v((NX, 256, 128), BF16),
        v((NX + 1, 128, 128), BF16), v((NX + 1, 128, 128), F32), v((NX + 1, 128, 128), BF16),
        v((NX + 1, 128, 128), F32), v((256, 128), BF16), v((256, 128), BF16), v((256, 128), BF16),
        v((256, 128), BF16), v((256, 128), BF16),
        v((128, 128), BF16), v((128, 128), BF16), v((NX - 1, 128, 128), BF16), v((NX, 128, 128), BF16),
        v((HEADS, 256, 128), BF16), v((HEADS, 256, 128), F32), v((HEADS, 256, 128), F32),
        v((2, 128, 512), BF16), v((128, 512), BF16), v((128, 4096), F32),
        v((NBLK, NY, 32, BLK), BF16), v((NBLK, 32, BLK), BF16), v((NBLK, 32, BLK), BF16),
        dma((8,)), dma((2,)), dma((2,)), dma((3,)), dma((3,)), dma((3,)), dma((3,)), dma((RCH, 5)), dma((RCH,)),
        dma((3,)), dma((2,)), pltpu.SemaphoreType.REGULAR, dma((NBLK,)),
        dma((3, 1)), dma((3, 1)), dma((4,)), dma((4,)), dma((3, NBLK)), dma((3, NBLK)),
    ]
    half = jax.ShapeDtypeStruct((32, 4096), BF16)
    own, one, two = pl.pallas_call(
        functools.partial(kernel, nz),
        out_shape=(half, half, half),
        in_specs=[aspec] * 8,
        out_specs=(aspec, aspec, aspec),
        scratch_shapes=scratch,
        compiler_params=pltpu.CompilerParams(
            collective_id=0, has_side_effects=True, vmem_limit_bytes=56 * 1024 * 1024
        ),
    )(
        projected, conv_weight, log_decay, write_rate, doc_bounds.T, out_gate,
        norm_gain.reshape(1, -1), out_weight,
    )
    return (own.astype(F32) + one.astype(F32) + two.astype(F32)).astype(BF16)


def solution(mesh):
    in_specs = (
        P(None, "ctx", "tp"),
        P(None, None, "tp"),
        P("tp", "ctx"),
        P("tp", "ctx"),
        P(),
        P("ctx", "tp"),
        P(),
        P("tp", None),
    )
    out_specs = P(("ctx", "tp"), None)
    nz = mesh.shape["ctx"] // NX
    assert nz == 8
    return jax.shard_map(
        functools.partial(body, nz), mesh=mesh, in_specs=in_specs, out_specs=out_specs, check_vma=False
    )
```

```python
import functools

import jax
import jax.numpy as jnp
from jax import lax
from jax.experimental import pallas as pl
from jax.experimental.pallas import tpu as pltpu
from jax.sharding import PartitionSpec as P

MESH = pl.DeviceIdType.MESH
F32 = jnp.float32
BF16 = jnp.bfloat16
SPAN = 128
TAPS = 4
NX = 4
NY = 4
HEADS = 4
NP = 8
BLK = 1024
NBLK = 4
RCH = 1
HEAD = 4


def mm(a, b):
    return lax.dot_general(a, b, (((1,), (0,)), ((), ())), preferred_element_type=F32)


def mmt(a, b):
    return lax.dot_general(a, b, (((1,), (1,)), ((), ())), preferred_element_type=F32)


def silu(u):
    return u / (1.0 + jnp.exp(-u))


def kernel(
    nz, proj_hbm, cw_hbm, ld_hbm, wr_hbm, db_hbm, gate_hbm, gain_hbm, w_hbm, out_ref,
    cw_ref, ld_ref, wr_ref, db_ref, gain_ref,
    proj, halo, ext, gate, w_own, w_par,
    gbuf, cbuf, masks, kq, rt, vb, lb, pb_s, xb, yb, xc, wub, wts, t1o1, t2, o2, tos, tin, am, ain, ab, mb,
    pt, po, qt, qo, rowm, abuf, bbuf, mid, prx, srx, snd, es, ein, qfin, lfin, sg,
    nb, nrx, acc, pb, rxo, rx1, rx2, cs,
    lsem, hsem, wsem, xs_sem, xr_sem, as_sem, ar_sem, zs_sem, zr_sem, ps_sem, pr_sem, rdy, es_sem, er_sem, ns_sem, nr_sem, rs_sem, rr_sem,
):
    ctx = lax.axis_index("ctx")
    tp = lax.axis_index("tp")
    z, x = lax.div(ctx, NX), lax.rem(ctx, NX)
    y, core = lax.div(tp, 2), lax.rem(tp, 2)
    nctx = nz * NX
    nxt = lax.rem(ctx + 1, nctx)
    prv = lax.rem(ctx + nctx - 1, nctx)
    zup = lax.rem(z + 1, nz)
    zdn = lax.rem(z + nz - 1, nz)
    right = lax.rem(y + 1, NY)
    left = lax.rem(y + NY - 1, NY)
    opp = lax.rem(y + 2, NY)
    other = 1 - core

    def remote(src, dst, ssem, rsem, device):
        return pltpu.make_async_remote_copy(
            src_ref=src, dst_ref=dst, send_sem=ssem, recv_sem=rsem,
            device_id=device, device_id_type=MESH,
        )

    barrier = pltpu.get_barrier_semaphore()
    peers = [(nxt, tp), (prv, tp)]
    peers += [(z * NX + lax.rem(x + r, NX), tp) for r in range(1, NX)]
    peers += [(zup * NX + x, tp), (zdn * NX + x, tp)]
    peers += [(ctx, right * 2 + core), (ctx, left * 2 + core), (ctx, y * 2 + other)]
    for device in peers:
        pl.semaphore_signal(barrier, inc=1, device_id=device, device_id_type=MESH)

    loads = [
        pltpu.make_async_copy(proj_hbm, proj, lsem.at[0]),
        pltpu.make_async_copy(gate_hbm, gate, lsem.at[1]),
        pltpu.make_async_copy(w_hbm, w_own, lsem.at[2]),
    ]
    small = [
        pltpu.make_async_copy(ld_hbm, ld_ref, lsem.at[3]),
        pltpu.make_async_copy(wr_hbm, wr_ref, lsem.at[4]),
        pltpu.make_async_copy(db_hbm, db_ref, lsem.at[5]),
        pltpu.make_async_copy(cw_hbm, cw_ref, lsem.at[6]),
        pltpu.make_async_copy(gain_hbm, gain_ref, lsem.at[7]),
    ]
    for copy in small:
        copy.start()
    loads[0].start()

    row_i = lax.broadcasted_iota(jnp.int32, (128, 128), 0)
    col_i = lax.broadcasted_iota(jnp.int32, (128, 128), 1)
    eye = row_i == col_i
    eye_f = jnp.where(eye, 1.0, 0.0)
    for level in range(1, 7):
        low = lax.shift_right_logical(row_i, level)
        low_j = lax.shift_right_logical(col_i, level)
        same = lax.shift_right_logical(row_i, level + 1) == lax.shift_right_logical(col_i, level + 1)
        masks[level - 1] = jnp.where(same & (low > low_j), 1.0, 0.0).astype(BF16)

    for copy in small:
        copy.wait()

    gbuf[...] = jnp.zeros((128, 128), F32)
    gbuf[0:4, :] = ld_ref[:, 0:128]
    gbuf[4:8, :] = ld_ref[:, 128:256]
    gbuf[8:12, :] = wr_ref[:, 0:128]
    gbuf[12:16, :] = wr_ref[:, 128:256]
    run = gbuf[0:8, :]
    lane = lax.broadcasted_iota(jnp.int32, (8, 128), 1)
    for step in (1, 2, 4, 8, 16, 32, 64):
        run = run + jnp.where(lane >= step, pltpu.roll(run, step, 1), 0.0)
    gbuf[0:8, :] = run
    cbuf[...] = gbuf[...].T

    keeps = []
    for span in range(2):
        hit = jnp.int32(0)
        for d in range(db_ref.shape[1]):
            hit = hit + jnp.where(db_ref[0, d] == ctx * 2 + span, 1, 0)
        keeps.append(1.0 - jnp.minimum(hit, 1).astype(F32))

    ones = jnp.full((128, 128), 1.0, BF16)

    def activate(s, h, first, count):
        cols = pl.ds(h * 128, 128)
        u = cw_ref[s, 0:1, cols] * ext[s, 8 + first : 8 + first + count, cols]
        for j in range(1, TAPS):
            lo = 8 + first - j
            u = u + cw_ref[s, j : j + 1, cols] * ext[s, lo : lo + count, cols]
        return silu(u)

    def unit(a):
        ss = mm((a * a).astype(BF16), ones)
        return (a * lax.rsqrt(ss + 1e-06)).astype(BF16)

    def fill(streams, span, first, count):
        for s in streams:
            for h in range(HEADS):
                p = span * HEADS + h
                a = activate(s, h, first, count)
                if s == 1:
                    kq[p, first : first + count, :] = unit(a)
                elif s == 0:
                    kq[p, 128 + first : 128 + first + count, :] = unit(a)
                else:
                    vb[p, first : first + count, :] = a.astype(BF16)

    def transposed(p, skip=0):
        beta = gbuf[8 + p : 9 + p, :]
        g = gbuf[p : p + 1, :]
        if skip:
            g = g - g[:, skip - 1 : skip]
            beta = jnp.where(col_i[0:1, :] >= skip, beta, 0.0)
        scale = beta * jnp.exp(g)
        rt[p, 0:128, :] = (kq[p, 0:128, :].astype(F32).T * scale).astype(BF16)
        rt[p, 128:256, :] = (vb[p].astype(F32).T * beta).astype(BF16)

    def decays(p):
        gcol = jnp.broadcast_to(cbuf[:, p : p + 1], (128, 128))
        bcol = jnp.broadcast_to(cbuf[:, 8 + p : 9 + p], (128, 128))
        dm = jnp.exp(jnp.minimum(gcol - gbuf[p : p + 1, :], 0.0))
        return dm, bcol * dm

    def scores(p):
        a = mmt(kq[p, 0:128, :], kq[p, 0:128, :])
        return jnp.where(row_i > col_i, decays(p)[1] * a, 0.0)

    def pairs(low):
        pair = lax.shift_right_logical(row_i, 1) == lax.shift_right_logical(col_i, 1)
        return (eye_f - jnp.where(pair, low, 0.0)).astype(BF16)

    def updates(p):
        wu = mmt(rt[p], xb[p])
        wub[p] = wu.astype(BF16)
        g = gbuf[p : p + 1, :]
        wts[p] = (wu * jnp.exp(g[:, 127:128] - g)).astype(BF16)

    def maps(p):
        span, h = p // HEADS, p % HEADS
        to = mm(wts[p], kq[p, 0:128, :])
        last = jnp.exp(gbuf[p : p + 1, 127:128])
        t = keeps[span] * (last * eye_f - to[0:128])
        if span == 0:
            t1o1[h, 0:128, :] = t.astype(BF16)
            t1o1[h, 128:256, :] = to[128:256].astype(BF16)
        else:
            t2[h] = t.astype(BF16)
            o2[h] = to[128:256]

    first_span = range(HEADS)
    second_span = range(HEADS, NP)

    rows = proj_hbm.shape[1]
    halo_copy = remote(proj_hbm.at[:, pl.ds(rows - 16, 16), :], halo, hsem.at[0], hsem.at[1], (nxt, tp))
    w_copy = remote(w_hbm, w_par, wsem.at[0], wsem.at[1], (ctx, y * 2 + other))

    def enter():
        pl.semaphore_wait(barrier, len(peers))
        halo_copy.start()
        loads[1].start()
        loads[2].start()
        w_copy.start()

        @pl.when((z == 1) | (z == 6))
        def _():
            pl.semaphore_signal(rdy, inc=1, device_id=(zdn * NX + x, tp), device_id_type=MESH)

    def word_from_above(row):
        @pl.when(z == row)
        def _():
            pl.semaphore_wait(rdy, 1)
            if row > 2:
                pl.semaphore_signal(rdy, inc=1, device_id=(zdn * NX + x, tp), device_id_type=MESH)

    loads[0].wait()
    for span in (1, 0):
        for s in (1, 2):
            if span == 0:
                ext[s, 0:8, :] = jnp.zeros((8, 512), F32)
            else:
                ext[s, 0:8, :] = proj[s, SPAN - 8 : SPAN, :].astype(F32) * keeps[1]
            ext[s, 8:136, :] = proj[s, span * SPAN : span * SPAN + SPAN, :].astype(F32)
        fill((1, 2), span, 0, SPAN)
        if span == 1:
            enter()
    for p in range(NP):
        low = scores(p)
        if p < HEADS:
            low = jnp.where(col_i >= HEAD, low, 0.0)
        lb[p] = low.astype(BF16)
        xb[p] = pairs(low)
    for p in second_span:
        transposed(p)
    for p in first_span:
        transposed(p, HEAD)
    for level in range(1, 7):
        for p in range(NP):
            yb[p] = mm(xb[p], lb[p] * masks[level - 1]).astype(BF16)
        for p in range(NP):
            xb[p] = xb[p] - mm(yb[p], xb[p]).astype(BF16)
    for p in range(NP):
        updates(p)
    for p in second_span:
        maps(p)
    for p in first_span:
        to = mm(wts[p], kq[p, 0:128, :])
        last = jnp.exp(gbuf[p : p + 1, 127:128] - gbuf[p : p + 1, HEAD - 1 : HEAD])
        t1o1[p, 0:128, :] = (last * eye_f - to[0:128]).astype(BF16)
        t1o1[p, 128:256, :] = to[128:256].astype(BF16)
    for h in range(HEADS):
        d = mm(t1o1[h], t2[h])
        tos[h, 0:128, :] = d[0:128].astype(BF16)
        tos[h, 128:256, :] = (d[128:256] + o2[h]).astype(BF16)

    x_copies = []
    for r in (2, 1, 3):
        to_x = lax.rem(x + r, NX)
        copy = remote(tos.at[to_x], tin.at[x], xs_sem.at[r - 1], xr_sem.at[r - 1], (z * NX + to_x, tp))
        copy.start()
        x_copies.append(copy)
    tin[x] = tos[x]

    word_from_above(5)

    halo_copy.wait()
    for s in (1, 2):
        ext[s, 0:8, :] = halo[s, 8:16, :].astype(F32) * keeps[0]
    fill((1, 2), 0, 0, 16)
    for h in range(HEADS):
        keys = kq[h, 0:16, :].astype(F32)
        gcol = jnp.broadcast_to(cbuf[0:16, h : h + 1], (16, 128))
        bcol = jnp.broadcast_to(cbuf[0:16, 8 + h : 9 + h], (16, 128))
        low = bcol * jnp.exp(jnp.minimum(gcol - gbuf[h : h + 1, :], 0.0))
        low = low * mmt(kq[h, 0:16, :], kq[h, 0:128, :])
        rk = keys * bcol * jnp.exp(gcol)
        rv = vb[h, 0:16, :].astype(F32) * bcol
        ws, us = [], []
        for i in range(HEAD):
            w_row, u_row = rk[i : i + 1, :], rv[i : i + 1, :]
            for j in range(i):
                c = jnp.broadcast_to(low[i : i + 1, j : j + 1], (1, 128))
                w_row = w_row - c * ws[j]
                u_row = u_row - c * us[j]
            ws.append(w_row)
            us.append(u_row)
        end = jnp.broadcast_to(cbuf[HEAD - 1 : HEAD, h : h + 1], (8, 128))
        am[h] = jnp.zeros((32, 128), F32)
        for i in range(HEAD):
            am[h, i : i + 1, :] = -keeps[0] * ws[i]
            am[h, 8 + i : 9 + i, :] = us[i]
        tail = jnp.exp(end - gcol[0:8]) * keys[0:8]
        am[h, 16:24, :] = jnp.where(row_i[0:8] < HEAD, tail, 0.0)
        am[h, 24:32, :] = keeps[0] * jnp.exp(end)
    a_copies = []
    for r in (2, 1, 3):
        to_x = lax.rem(x + r, NX)
        copy = remote(am.at[to_x], ain.at[x], as_sem.at[r - 1], ar_sem.at[r - 1], (z * NX + to_x, tp))
        copy.start()
        a_copies.append(copy)
    ain[x] = am[x]
    word_from_above(4)

    corner = (row_i < HEAD) & (col_i < HEAD)
    below = (row_i >= HEAD) & (col_i < HEAD)
    for p in first_span:
        low = scores(p)
        lb[p] = jnp.where(below, low, 0.0).astype(BF16)
        low = jnp.where(corner, low, 0.0)
        yb[p] = low.astype(BF16)
        xc[p] = pairs(low)
    for p in first_span:
        transposed(p)
    for p in first_span:
        yb[p] = mm(xc[p], yb[p] * masks[0]).astype(BF16)
    for p in first_span:
        xb[p] = xb[p] + (xc[p] - eye_f.astype(BF16) - mm(yb[p], xc[p]).astype(BF16))
    for p in first_span:
        yb[p] = mm(xb[p], lb[p]).astype(BF16)
    for p in first_span:
        xb[p] = xb[p] - mm(yb[p], xb[p]).astype(BF16)
    for p in first_span:
        updates(p)
    for p in first_span:
        maps(p)

    word_from_above(3)

    for span in range(2):
        before = halo[0, 8:16, :] if span == 0 else proj[0, SPAN - 8 : SPAN, :]
        ext[0, 0:8, :] = before.astype(F32) * keeps[span]
        ext[0, 8:136, :] = proj[0, span * SPAN : span * SPAN + SPAN, :].astype(F32)
        fill((0,), span, 0, SPAN)
    for p in range(NP):
        a = mmt(kq[p, 128:256, :], kq[p, 0:128, :])
        pb_s[p] = jnp.where(row_i >= col_i, decays(p)[0] * a, 0.0).astype(BF16)
    for h in range(HEADS):
        for span in range(2):
            p = span * HEADS + h
            pw = mmt(pb_s[p], wub[p])
            gcol = jnp.broadcast_to(cbuf[:, p : p + 1], (128, 128))
            q = keeps[span] * (jnp.exp(gcol) * kq[p, 128:256, :].astype(F32) - pw[:, 0:128])
            if span == 0:
                qfin[h, 0:128, :] = q.astype(BF16)
                lfin[h, 0:128, :] = pw[:, 128:256]
            else:
                q2 = mmt(q.astype(BF16), t1o1[h])
                qfin[h, 128:256, :] = q2[:, 0:128].astype(BF16)
                lfin[h, 128:256, :] = pw[:, 128:256] + q2[:, 128:256]
    word_from_above(2)
    word_from_above(0)
    loads[1].wait()
    for h in range(HEADS):
        cols = pl.ds(h * 128, 128)
        sg[h] = silu(gate[:, cols].astype(F32)) * gain_ref[0:1, :]

    for copy in x_copies:
        copy.wait()
    for copy in a_copies:
        copy.wait()

    for j in range(NX):
        ab[j] = mm(ain[j, 16:24, :].astype(BF16), tin[j, 0:128, :])
    for j in range(NX):
        wu = jnp.concatenate([ain[j, 0:8, :], ain[j, 8:16, :]], axis=1).astype(BF16)
        low = lax.dot_general(wu, ab[j].astype(BF16), (((0,), (0,)), ((), ())), preferred_element_type=F32)
        mb[j, 0:128, :] = (tin[j, 0:128, :].astype(F32) * ain[j, 24:25, :] + low[0:128]).astype(BF16)
        mb[j, 128:256, :] = (tin[j, 128:256, :].astype(F32) + low[128:256]).astype(BF16)
    pt[0] = eye_f.astype(BF16)
    po[0] = jnp.zeros((128, 128), F32)
    pt[1] = mb[0, 0:128, :]
    po[1] = mb[0, 128:256, :].astype(F32)
    cur = mb[0]
    for j in range(1, NX):
        step = mm(cur, mb[j, 0:128, :])
        off = step[128:256] + mb[j, 128:256, :].astype(F32)
        pt[j + 1] = step[0:128].astype(BF16)
        po[j + 1] = off
        cur = jnp.concatenate([step[0:128], off], axis=0).astype(BF16)
    rowm[...] = cur

    crows = 128 // RCH

    def s_copy(i, to, k):
        part = pl.ds(i * crows, crows)
        return remote(snd.at[part, :], srx.at[part, :], zs_sem.at[i, k], zr_sem.at[i], (to * NX + x, tp))

    def m_copy(src, dst, k, slot, to):
        return remote(src, dst, ps_sem.at[k], pr_sem.at[slot], (to * NX + x, tp))

    def chain(first, second):
        new = mm(first[...], second[0:128, :])
        return new[0:128], new[128:256] + second[128:256, :].astype(F32)

    @pl.when(z == 0)
    def _():
        snd[...] = po[NX].astype(BF16)
        for i in range(RCH):
            s_copy(i, 2, 1).start()
            s_copy(i, 1, 0).start()
        srx[...] = jnp.zeros((128, 128), BF16)

    @pl.when(z == 1)
    def _():
        m_copy(rowm, abuf, 0, 0, 2).start()

    @pl.when(z == 3)
    def _():
        m_copy(rowm, abuf, 0, 0, 4).start()
        m_copy(rowm, abuf, 1, 0, 5).start()

    @pl.when(z == 4)
    def _():
        m_copy(rowm, bbuf, 0, 1, 5).start()

    @pl.when(z == 5)
    def _():
        m_copy(rowm, bbuf, 0, 1, 6).start()

    @pl.when((z == 0) | (z == 1) | (z == 3))
    def _():
        abuf[0:128, :] = eye_f.astype(BF16)
        abuf[128:256, :] = jnp.zeros((128, 128), BF16)

    @pl.when(z < 5)
    def _():
        bbuf[0:128, :] = eye_f.astype(BF16)
        bbuf[128:256, :] = jnp.zeros((128, 128), BF16)

    @pl.when(z == 4)
    def _():
        m_copy(rowm, abuf, 0, 0, 4).wait_recv()
        t, o = chain(abuf, rowm)
        mid[0:128, :] = t.astype(BF16)
        mid[128:256, :] = o.astype(BF16)
        m_copy(mid, abuf, 1, 0, 7).start()
        m_copy(mid, abuf, 2, 0, 6).start()

    @pl.when(z == 6)
    def _():
        m_copy(rowm, bbuf, 0, 1, 6).wait_recv()
        t, o = chain(bbuf, rowm)
        mid[0:128, :] = t.astype(BF16)
        mid[128:256, :] = o.astype(BF16)
        m_copy(mid, bbuf, 0, 1, 7).start()

    @pl.when((z == 2) | (z > 4))
    def _():
        m_copy(rowm, abuf, 0, 0, 2).wait_recv()

    @pl.when((z == 5) | (z == 7))
    def _():
        m_copy(rowm, bbuf, 0, 1, 5).wait_recv()

    t, o = chain(abuf, bbuf)
    prx[0:128, :] = t.astype(BF16)
    prx[128:256, :] = o.astype(BF16)
    for j in range(NX + 1):
        new = mm(prx[...], pt[j])
        qt[j] = new[0:128].astype(BF16)
        qo[j] = new[128:256] + po[j]

    for i in range(RCH):
        part = pl.ds(i * crows, crows)

        @pl.when(z > 0)
        def _():
            s_copy(i, 1, 0).wait_recv()

        @pl.when(z == 2)
        def _():
            snd[part, :] = (mm(srx[part, :], qt[NX]) + qo[NX, part, :]).astype(BF16)
            for far in range(7, 2, -1):
                s_copy(i, far, far - 3).start()

    def e_copy(r, i, to_x):
        return remote(es.at[r - 1], ein.at[x], es_sem.at[r - 1, i], er_sem.at[r - 1, i], (z * NX + to_x, tp))

    e_copies = {}
    for r in (2, 1, 3):
        to_x = lax.rem(x + r, NX)
        es[r - 1] = (mm(srx[...], qt[to_x]) + qo[to_x]).astype(BF16)
        e_copies[r, 0] = e_copy(r, 0, to_x)
        e_copies[r, 0].start()
    ein[x] = (mm(srx[...], qt[x]) + qo[x]).astype(BF16)

    mean_ones = jnp.full((128, 128), 1.0 / 128.0, BF16)
    n_copies = []
    for r in (0, 1, 3, 2):
        head = lax.rem(x + NX - r, NX)
        if r > 0:
            e_copies[r, 0].wait_recv()
        att = mmt(qfin[head], ein[head]) + lfin[head]
        ms = mm((att * att).astype(BF16), mean_ones)
        nrm = (att * lax.rsqrt(ms + 1e-05) * sg[head]).astype(BF16)
        cols = pl.ds(pl.multiple_of(head * 128, 128), 128)
        for c in range(2):
            for b in range(NY):
                lo = b * 64 + c * 32
                nb[c, b * 32 : b * 32 + 32, cols] = nrm[lo : lo + 32, :]
        copy = remote(
            nb.at[other, :, cols], nrx.at[:, cols], ns_sem.at[r], nr_sem.at[r], (ctx, y * 2 + other)
        )
        copy.start()
        n_copies.append(copy)

    loads[2].wait()
    for b in range(NBLK):
        cols = pl.ds(b * BLK, BLK)
        acc[:, cols] = mm(nb[core], w_own[:, cols])
    w_copy.wait()
    for copy in n_copies:
        copy.wait()

    order = (0, 2, 1, 3)
    half = NBLK // 2
    o_copies, d_copies, c_copies = {}, {}, {}
    for b in order:
        cols = pl.ds(b * BLK, BLK)
        res = (acc[:, cols] + mm(nrx[...], w_par[:, cols])).astype(BF16)
        for d in range(NY):
            pb[b, d] = res[d * 32 : d * 32 + 32, :]
        first, second = (right, left) if b < half else (left, right)
        o_copies[b] = remote(
            pb.at[b, opp], rxo.at[b], rs_sem.at[0, b], rr_sem.at[0, b], (ctx, first * 2 + core)
        )
        o_copies[b].start()
        d_copies[b] = remote(
            pb.at[b, second], rx1.at[:, cols], rs_sem.at[1, b], rr_sem.at[1, b], (ctx, second * 2 + core)
        )
        d_copies[b].start()
    for b in order:
        first = right if b < half else left
        cols = pl.ds(b * BLK, BLK)
        o_copies[b].wait_recv()
        cs[b] = (pb[b, first].astype(F32) + rxo[b].astype(F32)).astype(BF16)
        c_copies[b] = remote(
            cs.at[b], rx2.at[:, cols], rs_sem.at[2, b], rr_sem.at[2, b], (ctx, first * 2 + core)
        )
        c_copies[b].start()
    for b in order:
        d_copies[b].wait_recv()
        c_copies[b].wait_recv()
        cols = pl.ds(b * BLK, BLK)
        total = pb[b, y].astype(F32) + rx1[:, cols].astype(F32) + rx2[:, cols].astype(F32)
        out_ref[:, cols] = total.astype(BF16)

    for row, count in ((0, 2), (2, 5)):
        @pl.when(z == row)
        def _():
            for i in range(RCH):
                for k in range(count):
                    s_copy(i, 1, k).wait_send()

    for row, count in ((1, 1), (3, 2), (4, 3), (5, 1), (6, 1)):
        @pl.when(z == row)
        def _():
            for k in range(count):
                m_copy(rowm, abuf, k, 0, 2).wait_send()

    for copy in e_copies.values():
        copy.wait_send()
    for b in order:
        o_copies[b].wait_send()
        d_copies[b].wait_send()
        c_copies[b].wait_send()


def body(nz, projected, conv_weight, log_decay, write_rate, doc_bounds, out_gate, norm_gain, out_weight):
    v = pltpu.VMEM
    dma = pltpu.SemaphoreType.DMA
    vspec = pl.BlockSpec(memory_space=pltpu.VMEM)
    aspec = pl.BlockSpec(memory_space=pl.ANY)
    scratch = [
        v((3, TAPS, 512), F32), v((HEADS, 256), F32), v((HEADS, 256), F32),
        pltpu.SMEM((2, 8), jnp.int32), v((1, 128), F32),
        v((3, 256, 512), BF16), v((3, 16, 512), BF16), v((3, 136, 512), F32), v((256, 512), BF16),
        v((512, 4096), BF16), v((512, 4096), BF16),
        v((128, 128), F32), v((128, 128), F32), v((6, 128, 128), BF16),
        v((NP, 256, 128), BF16), v((NP, 256, 128), BF16), v((NP, 128, 128), BF16),
        v((NP, 128, 128), BF16), v((NP, 128, 128), BF16), v((NP, 128, 128), BF16), v((NP, 128, 128), BF16),
        v((HEADS, 128, 128), BF16),
        v((NP, 256, 128), BF16), v((NP, 256, 128), BF16),
        v((HEADS, 256, 128), BF16), v((HEADS, 128, 128), BF16), v((HEADS, 128, 128), F32),
        v((HEADS, 256, 128), BF16), v((NX, 256, 128), BF16),
        v((HEADS, 32, 128), F32), v((NX, 32, 128), F32), v((NX, 8, 128), F32), v((NX, 256, 128), BF16),
        v((NX + 1, 128, 128), BF16), v((NX + 1, 128, 128), F32), v((NX + 1, 128, 128), BF16),
        v((NX + 1, 128, 128), F32), v((256, 128), BF16), v((256, 128), BF16), v((256, 128), BF16),
        v((256, 128), BF16), v((256, 128), BF16),
        v((128, 128), BF16), v((128, 128), BF16), v((NX - 1, 128, 128), BF16), v((NX, 128, 128), BF16),
        v((HEADS, 256, 128), BF16), v((HEADS, 256, 128), F32), v((HEADS, 256, 128), F32),
        v((2, 128, 512), BF16), v((128, 512), BF16), v((128, 4096), F32),
        v((NBLK, NY, 32, BLK), BF16), v((NBLK, 32, BLK), BF16), v((32, 4096), BF16), v((32, 4096), BF16),
        v((NBLK, 32, BLK), BF16),
        dma((8,)), dma((2,)), dma((2,)), dma((3,)), dma((3,)), dma((3,)), dma((3,)), dma((RCH, 5)), dma((RCH,)),
        dma((3,)), dma((2,)), pltpu.SemaphoreType.REGULAR,
        dma((3, 1)), dma((3, 1)), dma((4,)), dma((4,)), dma((3, NBLK)), dma((3, NBLK)),
    ]
    return pl.pallas_call(
        functools.partial(kernel, nz),
        out_shape=pltpu.VMEM((32, 4096), BF16),
        in_specs=[aspec] * 8,
        out_specs=vspec,
        scratch_shapes=scratch,
        compiler_params=pltpu.CompilerParams(
            collective_id=0, has_side_effects=True, vmem_limit_bytes=56 * 1024 * 1024
        ),
    )(
        projected, conv_weight, log_decay, write_rate, doc_bounds.T, out_gate,
        norm_gain.reshape(1, -1), out_weight,
    )


def solution(mesh):
    in_specs = (
        P(None, "ctx", "tp"),
        P(None, None, "tp"),
        P("tp", "ctx"),
        P("tp", "ctx"),
        P(),
        P("ctx", "tp"),
        P(),
        P("tp", None),
    )
    out_specs = P(("ctx", "tp"), None)
    nz = mesh.shape["ctx"] // NX
    assert nz == 8
    return jax.shard_map(
        functools.partial(body, nz), mesh=mesh, in_specs=in_specs, out_specs=out_specs, check_vma=False
    )
```

```python
import functools

import jax
import jax.numpy as jnp
from jax import lax
from jax.experimental import pallas as pl
from jax.experimental.pallas import tpu as pltpu
from jax.sharding import PartitionSpec as P

MESH = pl.DeviceIdType.MESH
F32 = jnp.float32
BF16 = jnp.bfloat16
SPAN = 128
TAPS = 4
NX = 4
NY = 4
HEADS = 4
NP = 8
BLK = 1024
NBLK = 4
RCH = 1
HEAD = 4


def mm(a, b):
    return lax.dot_general(a, b, (((1,), (0,)), ((), ())), preferred_element_type=F32)


def mmt(a, b):
    return lax.dot_general(a, b, (((1,), (1,)), ((), ())), preferred_element_type=F32)


def silu(u):
    return u / (1.0 + jnp.exp(-u))


def kernel(
    nz, proj_hbm, cw_hbm, ld_hbm, wr_hbm, db_hbm, gate_hbm, gain_hbm, w_hbm, out_ref,
    cw_ref, ld_ref, wr_ref, db_ref, gain_ref,
    proj, halo, ext, gate, w_own, w_par,
    gbuf, cbuf, masks, kq, rt, vb, lb, pb_s, xb, yb, xc, wub, wts, t1o1, t2, o2, tos, tin, am, amb, ain, ab, mb,
    pt, po, qt, qo, rowm, abuf, bbuf, mid, prx, srx, snd, es, ein, qfin, lfin, sg,
    nb, nrx, acc, pb, rxo, rx1, rx2, cs,
    lsem, hsem, wsem, xs_sem, xr_sem, as_sem, ar_sem, zs_sem, zr_sem, ps_sem, pr_sem, rdy, es_sem, er_sem, ns_sem, nr_sem, rs_sem, rr_sem,
):
    ctx = lax.axis_index("ctx")
    tp = lax.axis_index("tp")
    z, x = lax.div(ctx, NX), lax.rem(ctx, NX)
    y, core = lax.div(tp, 2), lax.rem(tp, 2)
    nctx = nz * NX
    nxt = lax.rem(ctx + 1, nctx)
    prv = lax.rem(ctx + nctx - 1, nctx)
    zup = lax.rem(z + 1, nz)
    zdn = lax.rem(z + nz - 1, nz)
    right = lax.rem(y + 1, NY)
    left = lax.rem(y + NY - 1, NY)
    opp = lax.rem(y + 2, NY)
    other = 1 - core

    def remote(src, dst, ssem, rsem, device):
        return pltpu.make_async_remote_copy(
            src_ref=src, dst_ref=dst, send_sem=ssem, recv_sem=rsem,
            device_id=device, device_id_type=MESH,
        )

    barrier = pltpu.get_barrier_semaphore()
    peers = [(nxt, tp), (prv, tp)]
    peers += [(z * NX + lax.rem(x + r, NX), tp) for r in range(1, NX)]
    peers += [(zup * NX + x, tp), (zdn * NX + x, tp)]
    peers += [(ctx, right * 2 + core), (ctx, left * 2 + core), (ctx, y * 2 + other)]
    for device in peers:
        pl.semaphore_signal(barrier, inc=1, device_id=device, device_id_type=MESH)

    loads = [
        pltpu.make_async_copy(proj_hbm, proj, lsem.at[0]),
        pltpu.make_async_copy(gate_hbm, gate, lsem.at[1]),
        pltpu.make_async_copy(w_hbm, w_own, lsem.at[2]),
    ]
    small = [
        pltpu.make_async_copy(ld_hbm, ld_ref, lsem.at[3]),
        pltpu.make_async_copy(wr_hbm, wr_ref, lsem.at[4]),
        pltpu.make_async_copy(db_hbm, db_ref, lsem.at[5]),
        pltpu.make_async_copy(cw_hbm, cw_ref, lsem.at[6]),
        pltpu.make_async_copy(gain_hbm, gain_ref, lsem.at[7]),
    ]
    for copy in small:
        copy.start()
    loads[0].start()

    row_i = lax.broadcasted_iota(jnp.int32, (128, 128), 0)
    col_i = lax.broadcasted_iota(jnp.int32, (128, 128), 1)
    eye = row_i == col_i
    eye_f = jnp.where(eye, 1.0, 0.0)
    for level in range(1, 7):
        low = lax.shift_right_logical(row_i, level)
        low_j = lax.shift_right_logical(col_i, level)
        same = lax.shift_right_logical(row_i, level + 1) == lax.shift_right_logical(col_i, level + 1)
        masks[level - 1] = jnp.where(same & (low > low_j), 1.0, 0.0).astype(BF16)

    for copy in small:
        copy.wait()

    gbuf[...] = jnp.zeros((128, 128), F32)
    gbuf[0:4, :] = ld_ref[:, 0:128]
    gbuf[4:8, :] = ld_ref[:, 128:256]
    gbuf[8:12, :] = wr_ref[:, 0:128]
    gbuf[12:16, :] = wr_ref[:, 128:256]
    run = gbuf[0:8, :]
    lane = lax.broadcasted_iota(jnp.int32, (8, 128), 1)
    for step in (1, 2, 4, 8, 16, 32, 64):
        run = run + jnp.where(lane >= step, pltpu.roll(run, step, 1), 0.0)
    gbuf[0:8, :] = run
    cbuf[...] = gbuf[...].T

    keeps = []
    for span in range(2):
        hit = jnp.int32(0)
        for d in range(db_ref.shape[1]):
            hit = hit + jnp.where(db_ref[0, d] == ctx * 2 + span, 1, 0)
        keeps.append(1.0 - jnp.minimum(hit, 1).astype(F32))

    ones = jnp.full((128, 128), 1.0, BF16)

    def activate(s, h, first, count):
        cols = pl.ds(h * 128, 128)
        u = cw_ref[s, 0:1, cols] * ext[s, 8 + first : 8 + first + count, cols]
        for j in range(1, TAPS):
            lo = 8 + first - j
            u = u + cw_ref[s, j : j + 1, cols] * ext[s, lo : lo + count, cols]
        return silu(u)

    def unit(a):
        ss = mm((a * a).astype(BF16), ones)
        return (a * lax.rsqrt(ss + 1e-06)).astype(BF16)

    def fill(streams, span, first, count):
        for s in streams:
            for h in range(HEADS):
                p = span * HEADS + h
                a = activate(s, h, first, count)
                if s == 1:
                    kq[p, first : first + count, :] = unit(a)
                elif s == 0:
                    kq[p, 128 + first : 128 + first + count, :] = unit(a)
                else:
                    vb[p, first : first + count, :] = a.astype(BF16)

    def transposed(p, skip=0):
        beta = gbuf[8 + p : 9 + p, :]
        g = gbuf[p : p + 1, :]
        if skip:
            g = g - g[:, skip - 1 : skip]
            beta = jnp.where(col_i[0:1, :] >= skip, beta, 0.0)
        scale = beta * jnp.exp(g)
        rt[p, 0:128, :] = (kq[p, 0:128, :].astype(F32).T * scale).astype(BF16)
        rt[p, 128:256, :] = (vb[p].astype(F32).T * beta).astype(BF16)

    def decays(p):
        gcol = jnp.broadcast_to(cbuf[:, p : p + 1], (128, 128))
        bcol = jnp.broadcast_to(cbuf[:, 8 + p : 9 + p], (128, 128))
        dm = jnp.exp(jnp.minimum(gcol - gbuf[p : p + 1, :], 0.0))
        return dm, bcol * dm

    def scores(p):
        a = mmt(kq[p, 0:128, :], kq[p, 0:128, :])
        return jnp.where(row_i > col_i, decays(p)[1] * a, 0.0)

    def pairs(low):
        pair = lax.shift_right_logical(row_i, 1) == lax.shift_right_logical(col_i, 1)
        return (eye_f - jnp.where(pair, low, 0.0)).astype(BF16)

    def updates(p):
        wu = mmt(rt[p], xb[p])
        wub[p] = wu.astype(BF16)
        g = gbuf[p : p + 1, :]
        wts[p] = (wu * jnp.exp(g[:, 127:128] - g)).astype(BF16)

    def maps(p):
        span, h = p // HEADS, p % HEADS
        to = mm(wts[p], kq[p, 0:128, :])
        last = jnp.exp(gbuf[p : p + 1, 127:128])
        t = keeps[span] * (last * eye_f - to[0:128])
        if span == 0:
            t1o1[h, 0:128, :] = t.astype(BF16)
            t1o1[h, 128:256, :] = to[128:256].astype(BF16)
        else:
            t2[h] = t.astype(BF16)
            o2[h] = to[128:256]

    first_span = range(HEADS)
    second_span = range(HEADS, NP)

    rows = proj_hbm.shape[1]
    last_rows = pl.ds(rows - 8, 8)
    halo_copy = remote(
        proj_hbm.at[pl.ds(1, 2), last_rows, :], halo.at[pl.ds(1, 2)], hsem.at[0], hsem.at[1], (nxt, tp)
    )
    halo_query = remote(
        proj_hbm.at[pl.ds(0, 1), last_rows, :], halo.at[pl.ds(0, 1)], hsem.at[2], hsem.at[3], (nxt, tp)
    )
    w_copy = remote(w_hbm, w_par, wsem.at[0], wsem.at[1], (ctx, y * 2 + other))

    def enter():
        pl.semaphore_wait(barrier, len(peers))
        halo_copy.start()
        halo_query.start()
        loads[1].start()
        loads[2].start()
        w_copy.start()

        @pl.when((z == 1) | (z == 6))
        def _():
            pl.semaphore_signal(rdy, inc=1, device_id=(zdn * NX + x, tp), device_id_type=MESH)

    def word_from_above(row):
        @pl.when(z == row)
        def _():
            pl.semaphore_wait(rdy, 1)
            if row > 2:
                pl.semaphore_signal(rdy, inc=1, device_id=(zdn * NX + x, tp), device_id_type=MESH)

    loads[0].wait()
    for span in (1, 0):
        for s in (1, 2):
            if span == 0:
                ext[s, 0:8, :] = jnp.zeros((8, 512), F32)
            else:
                ext[s, 0:8, :] = proj[s, SPAN - 8 : SPAN, :].astype(F32) * keeps[1]
            ext[s, 8:136, :] = proj[s, span * SPAN : span * SPAN + SPAN, :].astype(F32)
        fill((1, 2), span, 0, SPAN)
        if span == 1:
            enter()
    for p in range(NP):
        low = scores(p)
        if p < HEADS:
            low = jnp.where(col_i >= HEAD, low, 0.0)
        lb[p] = low.astype(BF16)
        xb[p] = pairs(low)
    for p in second_span:
        transposed(p)
    for p in first_span:
        transposed(p, HEAD)
    for level in range(1, 7):
        for p in range(NP):
            yb[p] = mm(xb[p], lb[p] * masks[level - 1]).astype(BF16)
        for p in range(NP):
            xb[p] = xb[p] - mm(yb[p], xb[p]).astype(BF16)
    for p in range(NP):
        updates(p)
    for p in second_span:
        maps(p)
    for p in first_span:
        to = mm(wts[p], kq[p, 0:128, :])
        last = jnp.exp(gbuf[p : p + 1, 127:128] - gbuf[p : p + 1, HEAD - 1 : HEAD])
        t1o1[p, 0:128, :] = (last * eye_f - to[0:128]).astype(BF16)
        t1o1[p, 128:256, :] = to[128:256].astype(BF16)
    for h in range(HEADS):
        d = mm(t1o1[h], t2[h])
        tos[h, 0:128, :] = d[0:128].astype(BF16)
        tos[h, 128:256, :] = (d[128:256] + o2[h]).astype(BF16)

    x_copies = []
    for r in (2, 1, 3):
        to_x = lax.rem(x + r, NX)
        copy = remote(tos.at[to_x], tin.at[x], xs_sem.at[r - 1], xr_sem.at[r - 1], (z * NX + to_x, tp))
        copy.start()
        x_copies.append(copy)
    tin[x] = tos[x]

    word_from_above(5)

    halo_copy.wait()
    for s in (1, 2):
        ext[s, 0:8, :] = halo[s].astype(F32) * keeps[0]
    fill((1, 2), 0, 0, 16)
    for h in range(HEADS):
        keys = kq[h, 0:16, :].astype(F32)
        gcol = jnp.broadcast_to(cbuf[0:16, h : h + 1], (16, 128))
        bcol = jnp.broadcast_to(cbuf[0:16, 8 + h : 9 + h], (16, 128))
        low = bcol * jnp.exp(jnp.minimum(gcol - gbuf[h : h + 1, :], 0.0))
        low = low * mmt(kq[h, 0:16, :], kq[h, 0:128, :])
        rk = keys * bcol * jnp.exp(gcol)
        rv = vb[h, 0:16, :].astype(F32) * bcol
        ws, us = [], []
        for i in range(HEAD):
            w_row, u_row = rk[i : i + 1, :], rv[i : i + 1, :]
            for j in range(i):
                c = jnp.broadcast_to(low[i : i + 1, j : j + 1], (1, 128))
                w_row = w_row - c * ws[j]
                u_row = u_row - c * us[j]
            ws.append(w_row)
            us.append(u_row)
        end = jnp.broadcast_to(cbuf[HEAD - 1 : HEAD, h : h + 1], (8, 128))
        am[h] = jnp.zeros((32, 128), F32)
        for i in range(HEAD):
            am[h, i : i + 1, :] = -keeps[0] * ws[i]
            am[h, 8 + i : 9 + i, :] = us[i]
        tail = jnp.exp(end - gcol[0:8]) * keys[0:8]
        am[h, 16:24, :] = jnp.where(row_i[0:8] < HEAD, tail, 0.0)
        decay = keeps[0] * jnp.exp(end)
        high = decay.astype(BF16).astype(F32)
        am[h, 24:32, :] = jnp.where(row_i[0:8] < 4, high, decay - high)
        amb[h] = am[h].astype(BF16)
    a_copies = []
    for r in (2, 1, 3):
        to_x = lax.rem(x + r, NX)
        copy = remote(amb.at[to_x], ain.at[x], as_sem.at[r - 1], ar_sem.at[r - 1], (z * NX + to_x, tp))
        copy.start()
        a_copies.append(copy)
    ain[x] = amb[x]
    word_from_above(4)

    corner = (row_i < HEAD) & (col_i < HEAD)
    below = (row_i >= HEAD) & (col_i < HEAD)
    for p in first_span:
        low = scores(p)
        lb[p] = jnp.where(below, low, 0.0).astype(BF16)
        low = jnp.where(corner, low, 0.0)
        yb[p] = low.astype(BF16)
        xc[p] = pairs(low)
    for p in first_span:
        transposed(p)
    for p in first_span:
        yb[p] = mm(xc[p], yb[p] * masks[0]).astype(BF16)
    for p in first_span:
        xb[p] = xb[p] + (xc[p] - eye_f.astype(BF16) - mm(yb[p], xc[p]).astype(BF16))
    for p in first_span:
        yb[p] = mm(xb[p], lb[p]).astype(BF16)
    for p in first_span:
        xb[p] = xb[p] - mm(yb[p], xb[p]).astype(BF16)
    for p in first_span:
        updates(p)
    for p in first_span:
        maps(p)

    word_from_above(3)

    halo_query.wait()
    for span in range(2):
        before = halo[0] if span == 0 else proj[0, SPAN - 8 : SPAN, :]
        ext[0, 0:8, :] = before.astype(F32) * keeps[span]
        ext[0, 8:136, :] = proj[0, span * SPAN : span * SPAN + SPAN, :].astype(F32)
        fill((0,), span, 0, SPAN)
    for p in range(NP):
        a = mmt(kq[p, 128:256, :], kq[p, 0:128, :])
        pb_s[p] = jnp.where(row_i >= col_i, decays(p)[0] * a, 0.0).astype(BF16)
    for h in range(HEADS):
        for span in range(2):
            p = span * HEADS + h
            pw = mmt(pb_s[p], wub[p])
            gcol = jnp.broadcast_to(cbuf[:, p : p + 1], (128, 128))
            q = keeps[span] * (jnp.exp(gcol) * kq[p, 128:256, :].astype(F32) - pw[:, 0:128])
            if span == 0:
                qfin[h, 0:128, :] = q.astype(BF16)
                lfin[h, 0:128, :] = pw[:, 128:256]
            else:
                q2 = mmt(q.astype(BF16), t1o1[h])
                qfin[h, 128:256, :] = q2[:, 0:128].astype(BF16)
                lfin[h, 128:256, :] = pw[:, 128:256] + q2[:, 128:256]
    word_from_above(2)
    word_from_above(0)
    loads[1].wait()
    for h in range(HEADS):
        cols = pl.ds(h * 128, 128)
        sg[h] = silu(gate[:, cols].astype(F32)) * gain_ref[0:1, :]

    for copy in x_copies:
        copy.wait()
    for copy in a_copies:
        copy.wait()

    parts = [ain[j].astype(F32) for j in range(NX)]
    for j in range(NX):
        ab[j] = mm(parts[j][16:24].astype(BF16), tin[j, 0:128, :])
    for j in range(NX):
        wu = jnp.concatenate([parts[j][0:8], parts[j][8:16]], axis=1).astype(BF16)
        low = lax.dot_general(wu, ab[j].astype(BF16), (((0,), (0,)), ((), ())), preferred_element_type=F32)
        decay = parts[j][24:25] + parts[j][28:29]
        mb[j, 0:128, :] = (tin[j, 0:128, :].astype(F32) * decay + low[0:128]).astype(BF16)
        mb[j, 128:256, :] = (tin[j, 128:256, :].astype(F32) + low[128:256]).astype(BF16)
    pt[0] = eye_f.astype(BF16)
    po[0] = jnp.zeros((128, 128), F32)
    pt[1] = mb[0, 0:128, :]
    po[1] = mb[0, 128:256, :].astype(F32)
    cur = mb[0]
    for j in range(1, NX):
        step = mm(cur, mb[j, 0:128, :])
        off = step[128:256] + mb[j, 128:256, :].astype(F32)
        pt[j + 1] = step[0:128].astype(BF16)
        po[j + 1] = off
        cur = jnp.concatenate([step[0:128], off], axis=0).astype(BF16)
    rowm[...] = cur

    crows = 128 // RCH

    def s_copy(i, to, k):
        part = pl.ds(i * crows, crows)
        return remote(snd.at[part, :], srx.at[part, :], zs_sem.at[i, k], zr_sem.at[i], (to * NX + x, tp))

    def m_copy(src, dst, k, slot, to):
        return remote(src, dst, ps_sem.at[k], pr_sem.at[slot], (to * NX + x, tp))

    def chain(first, second):
        new = mm(first[...], second[0:128, :])
        return new[0:128], new[128:256] + second[128:256, :].astype(F32)

    @pl.when(z == 0)
    def _():
        snd[...] = po[NX].astype(BF16)
        for i in range(RCH):
            s_copy(i, 2, 1).start()
            s_copy(i, 1, 0).start()
        srx[...] = jnp.zeros((128, 128), BF16)

    @pl.when(z == 1)
    def _():
        m_copy(rowm, abuf, 0, 0, 2).start()

    @pl.when(z == 3)
    def _():
        m_copy(rowm, abuf, 0, 0, 4).start()
        m_copy(rowm, abuf, 1, 0, 5).start()

    @pl.when(z == 4)
    def _():
        m_copy(rowm, bbuf, 0, 1, 5).start()

    @pl.when(z == 5)
    def _():
        m_copy(rowm, bbuf, 0, 1, 6).start()

    @pl.when((z == 0) | (z == 1) | (z == 3))
    def _():
        abuf[0:128, :] = eye_f.astype(BF16)
        abuf[128:256, :] = jnp.zeros((128, 128), BF16)

    @pl.when(z < 5)
    def _():
        bbuf[0:128, :] = eye_f.astype(BF16)
        bbuf[128:256, :] = jnp.zeros((128, 128), BF16)

    @pl.when(z == 4)
    def _():
        m_copy(rowm, abuf, 0, 0, 4).wait_recv()
        t, o = chain(abuf, rowm)
        mid[0:128, :] = t.astype(BF16)
        mid[128:256, :] = o.astype(BF16)
        m_copy(mid, abuf, 1, 0, 7).start()
        m_copy(mid, abuf, 2, 0, 6).start()

    @pl.when(z == 6)
    def _():
        m_copy(rowm, bbuf, 0, 1, 6).wait_recv()
        t, o = chain(bbuf, rowm)
        mid[0:128, :] = t.astype(BF16)
        mid[128:256, :] = o.astype(BF16)
        m_copy(mid, bbuf, 0, 1, 7).start()

    @pl.when((z == 2) | (z > 4))
    def _():
        m_copy(rowm, abuf, 0, 0, 2).wait_recv()

    @pl.when((z == 5) | (z == 7))
    def _():
        m_copy(rowm, bbuf, 0, 1, 5).wait_recv()

    t, o = chain(abuf, bbuf)
    prx[0:128, :] = t.astype(BF16)
    prx[128:256, :] = o.astype(BF16)
    for j in range(NX + 1):
        new = mm(prx[...], pt[j])
        qt[j] = new[0:128].astype(BF16)
        qo[j] = new[128:256] + po[j]

    for i in range(RCH):
        part = pl.ds(i * crows, crows)

        @pl.when(z > 0)
        def _():
            s_copy(i, 1, 0).wait_recv()

        @pl.when(z == 2)
        def _():
            snd[part, :] = (mm(srx[part, :], qt[NX]) + qo[NX, part, :]).astype(BF16)
            for far in range(7, 2, -1):
                s_copy(i, far, far - 3).start()

    def e_copy(r, i, to_x):
        return remote(es.at[r - 1], ein.at[x], es_sem.at[r - 1, i], er_sem.at[r - 1, i], (z * NX + to_x, tp))

    e_copies = {}
    for r in (2, 1, 3):
        to_x = lax.rem(x + r, NX)
        es[r - 1] = (mm(srx[...], qt[to_x]) + qo[to_x]).astype(BF16)
        e_copies[r, 0] = e_copy(r, 0, to_x)
        e_copies[r, 0].start()
    ein[x] = (mm(srx[...], qt[x]) + qo[x]).astype(BF16)

    mean_ones = jnp.full((128, 128), 1.0 / 128.0, BF16)
    n_copies = []
    for r in (0, 1, 3, 2):
        head = lax.rem(x + NX - r, NX)
        if r > 0:
            e_copies[r, 0].wait_recv()
        att = mmt(qfin[head], ein[head]) + lfin[head]
        ms = mm((att * att).astype(BF16), mean_ones)
        nrm = (att * lax.rsqrt(ms + 1e-05) * sg[head]).astype(BF16)
        cols = pl.ds(pl.multiple_of(head * 128, 128), 128)
        for c in range(2):
            for b in range(NY):
                lo = b * 64 + c * 32
                nb[c, b * 32 : b * 32 + 32, cols] = nrm[lo : lo + 32, :]
        copy = remote(
            nb.at[other, :, cols], nrx.at[:, cols], ns_sem.at[r], nr_sem.at[r], (ctx, y * 2 + other)
        )
        copy.start()
        n_copies.append(copy)

    loads[2].wait()
    for b in range(NBLK):
        cols = pl.ds(b * BLK, BLK)
        acc[:, cols] = mm(nb[core], w_own[:, cols])
    w_copy.wait()
    for copy in n_copies:
        copy.wait()

    order = (0, 2, 1, 3)
    half = NBLK // 2
    o_copies, d_copies, c_copies = {}, {}, {}
    for b in order:
        cols = pl.ds(b * BLK, BLK)
        res = (acc[:, cols] + mm(nrx[...], w_par[:, cols])).astype(BF16)
        for d in range(NY):
            pb[b, d] = res[d * 32 : d * 32 + 32, :]
        first, second = (right, left) if b < half else (left, right)
        o_copies[b] = remote(
            pb.at[b, opp], rxo.at[b], rs_sem.at[0, b], rr_sem.at[0, b], (ctx, first * 2 + core)
        )
        o_copies[b].start()
        d_copies[b] = remote(
            pb.at[b, second], rx1.at[:, cols], rs_sem.at[1, b], rr_sem.at[1, b], (ctx, second * 2 + core)
        )
        d_copies[b].start()
    for b in order:
        first = right if b < half else left
        cols = pl.ds(b * BLK, BLK)
        o_copies[b].wait_recv()
        cs[b] = (pb[b, first].astype(F32) + rxo[b].astype(F32)).astype(BF16)
        c_copies[b] = remote(
            cs.at[b], rx2.at[:, cols], rs_sem.at[2, b], rr_sem.at[2, b], (ctx, first * 2 + core)
        )
        c_copies[b].start()
    for b in order:
        d_copies[b].wait_recv()
        c_copies[b].wait_recv()
        cols = pl.ds(b * BLK, BLK)
        total = pb[b, y].astype(F32) + rx1[:, cols].astype(F32) + rx2[:, cols].astype(F32)
        out_ref[:, cols] = total.astype(BF16)

    for row, count in ((0, 2), (2, 5)):
        @pl.when(z == row)
        def _():
            for i in range(RCH):
                for k in range(count):
                    s_copy(i, 1, k).wait_send()

    for row, count in ((1, 1), (3, 2), (4, 3), (5, 1), (6, 1)):
        @pl.when(z == row)
        def _():
            for k in range(count):
                m_copy(rowm, abuf, k, 0, 2).wait_send()

    for copy in e_copies.values():
        copy.wait_send()
    for b in order:
        o_copies[b].wait_send()
        d_copies[b].wait_send()
        c_copies[b].wait_send()


def body(nz, projected, conv_weight, log_decay, write_rate, doc_bounds, out_gate, norm_gain, out_weight):
    v = pltpu.VMEM
    dma = pltpu.SemaphoreType.DMA
    vspec = pl.BlockSpec(memory_space=pltpu.VMEM)
    aspec = pl.BlockSpec(memory_space=pl.ANY)
    scratch = [
        v((3, TAPS, 512), F32), v((HEADS, 256), F32), v((HEADS, 256), F32),
        pltpu.SMEM((2, 8), jnp.int32), v((1, 128), F32),
        v((3, 256, 512), BF16), v((3, 8, 512), BF16), v((3, 136, 512), F32), v((256, 512), BF16),
        v((512, 4096), BF16), v((512, 4096), BF16),
        v((128, 128), F32), v((128, 128), F32), v((6, 128, 128), BF16),
        v((NP, 256, 128), BF16), v((NP, 256, 128), BF16), v((NP, 128, 128), BF16),
        v((NP, 128, 128), BF16), v((NP, 128, 128), BF16), v((NP, 128, 128), BF16), v((NP, 128, 128), BF16),
        v((HEADS, 128, 128), BF16),
        v((NP, 256, 128), BF16), v((NP, 256, 128), BF16),
        v((HEADS, 256, 128), BF16), v((HEADS, 128, 128), BF16), v((HEADS, 128, 128), F32),
        v((HEADS, 256, 128), BF16), v((NX, 256, 128), BF16),
        v((HEADS, 32, 128), F32), v((HEADS, 32, 128), BF16), v((NX, 32, 128), BF16), v((NX, 8, 128), F32), v((NX, 256, 128), BF16),
        v((NX + 1, 128, 128), BF16), v((NX + 1, 128, 128), F32), v((NX + 1, 128, 128), BF16),
        v((NX + 1, 128, 128), F32), v((256, 128), BF16), v((256, 128), BF16), v((256, 128), BF16),
        v((256, 128), BF16), v((256, 128), BF16),
        v((128, 128), BF16), v((128, 128), BF16), v((NX - 1, 128, 128), BF16), v((NX, 128, 128), BF16),
        v((HEADS, 256, 128), BF16), v((HEADS, 256, 128), F32), v((HEADS, 256, 128), F32),
        v((2, 128, 512), BF16), v((128, 512), BF16), v((128, 4096), F32),
        v((NBLK, NY, 32, BLK), BF16), v((NBLK, 32, BLK), BF16), v((32, 4096), BF16), v((32, 4096), BF16),
        v((NBLK, 32, BLK), BF16),
        dma((8,)), dma((4,)), dma((2,)), dma((3,)), dma((3,)), dma((3,)), dma((3,)), dma((RCH, 5)), dma((RCH,)),
        dma((3,)), dma((2,)), pltpu.SemaphoreType.REGULAR,
        dma((3, 1)), dma((3, 1)), dma((4,)), dma((4,)), dma((3, NBLK)), dma((3, NBLK)),
    ]
    return pl.pallas_call(
        functools.partial(kernel, nz),
        out_shape=pltpu.VMEM((32, 4096), BF16),
        in_specs=[aspec] * 8,
        out_specs=vspec,
        scratch_shapes=scratch,
        compiler_params=pltpu.CompilerParams(
            collective_id=0, has_side_effects=True, vmem_limit_bytes=56 * 1024 * 1024
        ),
    )(
        projected, conv_weight, log_decay, write_rate, doc_bounds.T, out_gate,
        norm_gain.reshape(1, -1), out_weight,
    )


def solution(mesh):
    in_specs = (
        P(None, "ctx", "tp"),
        P(None, None, "tp"),
        P("tp", "ctx"),
        P("tp", "ctx"),
        P(),
        P("ctx", "tp"),
        P(),
        P("tp", None),
    )
    out_specs = P(("ctx", "tp"), None)
    nz = mesh.shape["ctx"] // NX
    assert nz == 8
    return jax.shard_map(
        functools.partial(body, nz), mesh=mesh, in_specs=in_specs, out_specs=out_specs, check_vma=False
    )
```

```python
import functools

import jax
import jax.numpy as jnp
from jax import lax
from jax.experimental import pallas as pl
from jax.experimental.pallas import tpu as pltpu
from jax.sharding import PartitionSpec as P

MESH = pl.DeviceIdType.MESH
F32 = jnp.float32
BF16 = jnp.bfloat16
SPAN = 128
TAPS = 4
NX = 4
NY = 4
HEADS = 4
NP = 8
BLK = 1024
NBLK = 4
RCH = 1
HEAD = 4


def mm(a, b):
    return lax.dot_general(a, b, (((1,), (0,)), ((), ())), preferred_element_type=F32)


def mmt(a, b):
    return lax.dot_general(a, b, (((1,), (1,)), ((), ())), preferred_element_type=F32)


def silu(u):
    return u / (1.0 + jnp.exp(-u))


def kernel(
    nz, proj_hbm, cw_hbm, ld_hbm, wr_hbm, db_hbm, gate_hbm, gain_hbm, w_hbm, out_ref,
    cw_ref, ld_ref, wr_ref, db_ref, gain_ref,
    proj, halo, ext, gate, w_own, w_par,
    gbuf, cbuf, masks, kq, rt, vb, lb, pb_s, xb, yb, xc, wub, wts, t1o1, t2, o2, tos, tin, am, amb, ain, ab, mb,
    pt, po, qt, qo, rowm, abuf, bbuf, mid, prx, srx, snd, es, ein, qfin, lfin, sg,
    nb, nrx, acc, pb, rxo, rx1, rx2, cs,
    lsem, hsem, wsem, xs_sem, xr_sem, as_sem, ar_sem, zs_sem, zr_sem, ps_sem, pr_sem, rdy, es_sem, er_sem, ns_sem, nr_sem, rs_sem, rr_sem,
):
    ctx = lax.axis_index("ctx")
    tp = lax.axis_index("tp")
    z, x = lax.div(ctx, NX), lax.rem(ctx, NX)
    y, core = lax.div(tp, 2), lax.rem(tp, 2)
    nctx = nz * NX
    nxt = lax.rem(ctx + 1, nctx)
    prv = lax.rem(ctx + nctx - 1, nctx)
    zup = lax.rem(z + 1, nz)
    zdn = lax.rem(z + nz - 1, nz)
    right = lax.rem(y + 1, NY)
    left = lax.rem(y + NY - 1, NY)
    opp = lax.rem(y + 2, NY)
    other = 1 - core

    def remote(src, dst, ssem, rsem, device):
        return pltpu.make_async_remote_copy(
            src_ref=src, dst_ref=dst, send_sem=ssem, recv_sem=rsem,
            device_id=device, device_id_type=MESH,
        )

    barrier = pltpu.get_barrier_semaphore()
    peers = [(nxt, tp), (prv, tp)]
    peers += [(z * NX + lax.rem(x + r, NX), tp) for r in range(1, NX)]
    peers += [(zup * NX + x, tp), (zdn * NX + x, tp)]
    peers += [(ctx, right * 2 + core), (ctx, left * 2 + core), (ctx, y * 2 + other)]
    for device in peers:
        pl.semaphore_signal(barrier, inc=1, device_id=device, device_id_type=MESH)

    loads = [
        pltpu.make_async_copy(proj_hbm, proj, lsem.at[0]),
        pltpu.make_async_copy(gate_hbm, gate, lsem.at[1]),
        pltpu.make_async_copy(w_hbm, w_own, lsem.at[2]),
    ]
    small = [
        pltpu.make_async_copy(ld_hbm, ld_ref, lsem.at[3]),
        pltpu.make_async_copy(wr_hbm, wr_ref, lsem.at[4]),
        pltpu.make_async_copy(db_hbm, db_ref, lsem.at[5]),
        pltpu.make_async_copy(cw_hbm, cw_ref, lsem.at[6]),
        pltpu.make_async_copy(gain_hbm, gain_ref, lsem.at[7]),
    ]
    for copy in small:
        copy.start()
    loads[0].start()

    row_i = lax.broadcasted_iota(jnp.int32, (128, 128), 0)
    col_i = lax.broadcasted_iota(jnp.int32, (128, 128), 1)
    eye = row_i == col_i
    eye_f = jnp.where(eye, 1.0, 0.0)
    for level in range(1, 7):
        low = lax.shift_right_logical(row_i, level)
        low_j = lax.shift_right_logical(col_i, level)
        same = lax.shift_right_logical(row_i, level + 1) == lax.shift_right_logical(col_i, level + 1)
        masks[level - 1] = jnp.where(same & (low > low_j), 1.0, 0.0).astype(BF16)

    for copy in small:
        copy.wait()

    gbuf[...] = jnp.zeros((128, 128), F32)
    gbuf[0:4, :] = ld_ref[:, 0:128]
    gbuf[4:8, :] = ld_ref[:, 128:256]
    gbuf[8:12, :] = wr_ref[:, 0:128]
    gbuf[12:16, :] = wr_ref[:, 128:256]
    run = gbuf[0:8, :]
    lane = lax.broadcasted_iota(jnp.int32, (8, 128), 1)
    for step in (1, 2, 4, 8, 16, 32, 64):
        run = run + jnp.where(lane >= step, pltpu.roll(run, step, 1), 0.0)
    gbuf[0:8, :] = run
    cbuf[...] = gbuf[...].T

    keeps = []
    for span in range(2):
        hit = jnp.int32(0)
        for d in range(db_ref.shape[1]):
            hit = hit + jnp.where(db_ref[0, d] == ctx * 2 + span, 1, 0)
        keeps.append(1.0 - jnp.minimum(hit, 1).astype(F32))

    ones = jnp.full((128, 128), 1.0, BF16)

    def activate(s, h, first, count):
        cols = pl.ds(h * 128, 128)
        u = cw_ref[s, 0:1, cols] * ext[s, 8 + first : 8 + first + count, cols]
        for j in range(1, TAPS):
            lo = 8 + first - j
            u = u + cw_ref[s, j : j + 1, cols] * ext[s, lo : lo + count, cols]
        return silu(u)

    def unit(a):
        ss = mm((a * a).astype(BF16), ones)
        return (a * lax.rsqrt(ss + 1e-06)).astype(BF16)

    def fill(streams, span, first, count):
        for s in streams:
            for h in range(HEADS):
                p = span * HEADS + h
                a = activate(s, h, first, count)
                if s == 1:
                    kq[p, first : first + count, :] = unit(a)
                elif s == 0:
                    kq[p, 128 + first : 128 + first + count, :] = unit(a)
                else:
                    vb[p, first : first + count, :] = a.astype(BF16)

    def transposed(p, skip=0):
        beta = gbuf[8 + p : 9 + p, :]
        g = gbuf[p : p + 1, :]
        if skip:
            g = g - g[:, skip - 1 : skip]
            beta = jnp.where(col_i[0:1, :] >= skip, beta, 0.0)
        scale = beta * jnp.exp(g)
        rt[p, 0:128, :] = (kq[p, 0:128, :].astype(F32).T * scale).astype(BF16)
        rt[p, 128:256, :] = (vb[p].astype(F32).T * beta).astype(BF16)

    def decays(p):
        gcol = jnp.broadcast_to(cbuf[:, p : p + 1], (128, 128))
        bcol = jnp.broadcast_to(cbuf[:, 8 + p : 9 + p], (128, 128))
        dm = jnp.exp(jnp.minimum(gcol - gbuf[p : p + 1, :], 0.0))
        return dm, bcol * dm

    def scores(p):
        a = mmt(kq[p, 0:128, :], kq[p, 0:128, :])
        return jnp.where(row_i > col_i, decays(p)[1] * a, 0.0)

    def pairs(low):
        pair = lax.shift_right_logical(row_i, 1) == lax.shift_right_logical(col_i, 1)
        return (eye_f - jnp.where(pair, low, 0.0)).astype(BF16)

    def updates(p):
        wu = mmt(rt[p], xb[p])
        wub[p] = wu.astype(BF16)
        g = gbuf[p : p + 1, :]
        wts[p] = (wu * jnp.exp(g[:, 127:128] - g)).astype(BF16)

    def maps(p):
        span, h = p // HEADS, p % HEADS
        to = mm(wts[p], kq[p, 0:128, :])
        last = jnp.exp(gbuf[p : p + 1, 127:128])
        t = keeps[span] * (last * eye_f - to[0:128])
        if span == 0:
            t1o1[h, 0:128, :] = t.astype(BF16)
            t1o1[h, 128:256, :] = to[128:256].astype(BF16)
        else:
            t2[h] = t.astype(BF16)
            o2[h] = to[128:256]

    first_span = range(HEADS)
    second_span = range(HEADS, NP)

    rows = proj_hbm.shape[1]
    last_rows = pl.ds(rows - 8, 8)
    halo_copy = remote(
        proj_hbm.at[pl.ds(1, 2), last_rows, :], halo.at[pl.ds(1, 2)], hsem.at[0], hsem.at[1], (nxt, tp)
    )
    halo_query = remote(
        proj_hbm.at[pl.ds(0, 1), last_rows, :], halo.at[pl.ds(0, 1)], hsem.at[2], hsem.at[3], (nxt, tp)
    )
    w_copy = remote(w_hbm, w_par, wsem.at[0], wsem.at[1], (ctx, y * 2 + other))

    def enter():
        pl.semaphore_wait(barrier, len(peers))
        halo_copy.start()
        halo_query.start()
        loads[1].start()
        loads[2].start()
        w_copy.start()

        @pl.when((z == 1) | (z == 6))
        def _():
            pl.semaphore_signal(rdy, inc=1, device_id=(zdn * NX + x, tp), device_id_type=MESH)

    def word_from_above(row):
        @pl.when(z == row)
        def _():
            pl.semaphore_wait(rdy, 1)
            if row > 2:
                pl.semaphore_signal(rdy, inc=1, device_id=(zdn * NX + x, tp), device_id_type=MESH)

    loads[0].wait()
    for span in (1, 0):
        for s in (1, 2):
            if span == 0:
                ext[s, 0:8, :] = jnp.zeros((8, 512), F32)
            else:
                ext[s, 0:8, :] = proj[s, SPAN - 8 : SPAN, :].astype(F32) * keeps[1]
            ext[s, 8:136, :] = proj[s, span * SPAN : span * SPAN + SPAN, :].astype(F32)
        fill((1, 2), span, 0, SPAN)
        if span == 1:
            enter()
    for p in range(NP):
        low = scores(p)
        if p < HEADS:
            low = jnp.where(col_i >= HEAD, low, 0.0)
        lb[p] = low.astype(BF16)
        xb[p] = pairs(low)
    for p in second_span:
        transposed(p)
    for p in first_span:
        transposed(p, HEAD)
    for level in range(1, 7):
        for p in range(NP):
            yb[p] = mm(xb[p], lb[p] * masks[level - 1]).astype(BF16)
        for p in range(NP):
            xb[p] = xb[p] - mm(yb[p], xb[p]).astype(BF16)
    for p in range(NP):
        updates(p)
    for p in second_span:
        maps(p)
    for p in first_span:
        to = mm(wts[p], kq[p, 0:128, :])
        last = jnp.exp(gbuf[p : p + 1, 127:128] - gbuf[p : p + 1, HEAD - 1 : HEAD])
        t1o1[p, 0:128, :] = (last * eye_f - to[0:128]).astype(BF16)
        t1o1[p, 128:256, :] = to[128:256].astype(BF16)
    for h in range(HEADS):
        d = mm(t1o1[h], t2[h])
        tos[h, 0:128, :] = d[0:128].astype(BF16)
        tos[h, 128:256, :] = (d[128:256] + o2[h]).astype(BF16)

    x_copies = []
    for r in (2, 1, 3):
        to_x = lax.rem(x + r, NX)
        copy = remote(tos.at[to_x], tin.at[x], xs_sem.at[r - 1], xr_sem.at[r - 1], (z * NX + to_x, tp))
        copy.start()
        x_copies.append(copy)
    tin[x] = tos[x]

    word_from_above(5)

    halo_copy.wait()
    for s in (1, 2):
        ext[s, 0:8, :] = halo[s].astype(F32) * keeps[0]
    fill((1, 2), 0, 0, 16)
    for h in range(HEADS):
        keys = kq[h, 0:16, :].astype(F32)
        gcol = jnp.broadcast_to(cbuf[0:16, h : h + 1], (16, 128))
        bcol = jnp.broadcast_to(cbuf[0:16, 8 + h : 9 + h], (16, 128))
        low = bcol * jnp.exp(jnp.minimum(gcol - gbuf[h : h + 1, :], 0.0))
        low = low * mmt(kq[h, 0:16, :], kq[h, 0:128, :])
        rk = keys * bcol * jnp.exp(gcol)
        rv = vb[h, 0:16, :].astype(F32) * bcol
        ws, us = [], []
        for i in range(HEAD):
            w_row, u_row = rk[i : i + 1, :], rv[i : i + 1, :]
            for j in range(i):
                c = jnp.broadcast_to(low[i : i + 1, j : j + 1], (1, 128))
                w_row = w_row - c * ws[j]
                u_row = u_row - c * us[j]
            ws.append(w_row)
            us.append(u_row)
        end = jnp.broadcast_to(cbuf[HEAD - 1 : HEAD, h : h + 1], (8, 128))
        am[h] = jnp.zeros((32, 128), F32)
        for i in range(HEAD):
            am[h, i : i + 1, :] = -keeps[0] * ws[i]
            am[h, 8 + i : 9 + i, :] = us[i]
        tail = jnp.exp(end - gcol[0:8]) * keys[0:8]
        am[h, 16:24, :] = jnp.where(row_i[0:8] < HEAD, tail, 0.0)
        decay = keeps[0] * jnp.exp(end)
        high = decay.astype(BF16).astype(F32)
        am[h, 24:32, :] = jnp.where(row_i[0:8] < 4, high, decay - high)
        amb[h] = am[h].astype(BF16)
    a_copies = []
    for r in (2, 1, 3):
        to_x = lax.rem(x + r, NX)
        copy = remote(amb.at[to_x], ain.at[x], as_sem.at[r - 1], ar_sem.at[r - 1], (z * NX + to_x, tp))
        copy.start()
        a_copies.append(copy)
    ain[x] = amb[x]
    word_from_above(4)

    corner = (row_i < HEAD) & (col_i < HEAD)
    below = (row_i >= HEAD) & (col_i < HEAD)
    for p in first_span:
        low = scores(p)
        lb[p] = jnp.where(below, low, 0.0).astype(BF16)
        low = jnp.where(corner, low, 0.0)
        yb[p] = low.astype(BF16)
        xc[p] = pairs(low)
    for p in first_span:
        transposed(p)
    for p in first_span:
        yb[p] = mm(xc[p], yb[p] * masks[0]).astype(BF16)
    for p in first_span:
        xb[p] = xb[p] + (xc[p] - eye_f.astype(BF16) - mm(yb[p], xc[p]).astype(BF16))
    for p in first_span:
        yb[p] = mm(xb[p], lb[p]).astype(BF16)
    for p in first_span:
        xb[p] = xb[p] - mm(yb[p], xb[p]).astype(BF16)
    for p in first_span:
        updates(p)
    for p in first_span:
        maps(p)

    word_from_above(3)

    halo_query.wait()
    for span in range(2):
        before = halo[0] if span == 0 else proj[0, SPAN - 8 : SPAN, :]
        ext[0, 0:8, :] = before.astype(F32) * keeps[span]
        ext[0, 8:136, :] = proj[0, span * SPAN : span * SPAN + SPAN, :].astype(F32)
        fill((0,), span, 0, SPAN)
    for p in range(NP):
        a = mmt(kq[p, 128:256, :], kq[p, 0:128, :])
        pb_s[p] = jnp.where(row_i >= col_i, decays(p)[0] * a, 0.0).astype(BF16)
    for h in range(HEADS):
        for span in range(2):
            p = span * HEADS + h
            pw = mmt(pb_s[p], wub[p])
            gcol = jnp.broadcast_to(cbuf[:, p : p + 1], (128, 128))
            q = keeps[span] * (jnp.exp(gcol) * kq[p, 128:256, :].astype(F32) - pw[:, 0:128])
            if span == 0:
                qfin[h, 0:128, :] = q.astype(BF16)
                lfin[h, 0:128, :] = pw[:, 128:256]
            else:
                q2 = mmt(q.astype(BF16), t1o1[h])
                qfin[h, 128:256, :] = q2[:, 0:128].astype(BF16)
                lfin[h, 128:256, :] = pw[:, 128:256] + q2[:, 128:256]
    word_from_above(2)
    word_from_above(0)
    loads[1].wait()
    for h in range(HEADS):
        cols = pl.ds(h * 128, 128)
        sg[h] = silu(gate[:, cols].astype(F32)) * gain_ref[0:1, :]

    for copy in x_copies:
        copy.wait()
    for copy in a_copies:
        copy.wait()

    parts = [ain[j].astype(F32) for j in range(NX)]
    for j in range(NX):
        ab[j] = mm(parts[j][16:24].astype(BF16), tin[j, 0:128, :])
    for j in range(NX):
        wu = jnp.concatenate([parts[j][0:8], parts[j][8:16]], axis=1).astype(BF16)
        low = lax.dot_general(wu, ab[j].astype(BF16), (((0,), (0,)), ((), ())), preferred_element_type=F32)
        decay = parts[j][24:25] + parts[j][28:29]
        mb[j, 0:128, :] = (tin[j, 0:128, :].astype(F32) * decay + low[0:128]).astype(BF16)
        mb[j, 128:256, :] = (tin[j, 128:256, :].astype(F32) + low[128:256]).astype(BF16)
    pt[0] = eye_f.astype(BF16)
    po[0] = jnp.zeros((128, 128), F32)
    pt[1] = mb[0, 0:128, :]
    po[1] = mb[0, 128:256, :].astype(F32)
    cur = mb[0]
    for j in range(1, NX):
        step = mm(cur, mb[j, 0:128, :])
        off = step[128:256] + mb[j, 128:256, :].astype(F32)
        pt[j + 1] = step[0:128].astype(BF16)
        po[j + 1] = off
        cur = jnp.concatenate([step[0:128], off], axis=0).astype(BF16)
    rowm[...] = cur

    crows = 128 // RCH

    def s_copy(i, to, k):
        part = pl.ds(i * crows, crows)
        return remote(snd.at[part, :], srx.at[part, :], zs_sem.at[i, k], zr_sem.at[i], (to * NX + x, tp))

    def m_copy(src, dst, k, slot, to):
        return remote(src, dst, ps_sem.at[k], pr_sem.at[slot], (to * NX + x, tp))

    def chain(first, second):
        new = mm(first[...], second[0:128, :])
        return new[0:128], new[128:256] + second[128:256, :].astype(F32)

    @pl.when(z == 0)
    def _():
        snd[...] = po[NX].astype(BF16)
        for i in range(RCH):
            s_copy(i, 2, 1).start()
            s_copy(i, 1, 0).start()
        srx[...] = jnp.zeros((128, 128), BF16)

    @pl.when(z == 1)
    def _():
        m_copy(rowm, abuf, 0, 0, 2).start()

    @pl.when(z == 3)
    def _():
        m_copy(rowm, abuf, 0, 0, 4).start()
        m_copy(rowm, abuf, 1, 0, 5).start()

    @pl.when(z == 4)
    def _():
        m_copy(rowm, bbuf, 0, 1, 5).start()

    @pl.when(z == 5)
    def _():
        m_copy(rowm, bbuf, 0, 1, 6).start()

    @pl.when((z == 0) | (z == 1) | (z == 3))
    def _():
        abuf[0:128, :] = eye_f.astype(BF16)
        abuf[128:256, :] = jnp.zeros((128, 128), BF16)

    @pl.when(z < 5)
    def _():
        bbuf[0:128, :] = eye_f.astype(BF16)
        bbuf[128:256, :] = jnp.zeros((128, 128), BF16)

    @pl.when(z == 4)
    def _():
        m_copy(rowm, abuf, 0, 0, 4).wait_recv()
        t, o = chain(abuf, rowm)
        mid[0:128, :] = t.astype(BF16)
        mid[128:256, :] = o.astype(BF16)
        m_copy(mid, abuf, 1, 0, 7).start()
        m_copy(mid, abuf, 2, 0, 6).start()

    @pl.when(z == 6)
    def _():
        m_copy(rowm, bbuf, 0, 1, 6).wait_recv()
        t, o = chain(bbuf, rowm)
        mid[0:128, :] = t.astype(BF16)
        mid[128:256, :] = o.astype(BF16)
        m_copy(mid, bbuf, 0, 1, 7).start()

    @pl.when((z == 2) | (z > 4))
    def _():
        m_copy(rowm, abuf, 0, 0, 2).wait_recv()

    @pl.when(z == 2)
    def _():
        new = mm(abuf[...], pt[NX])
        end_t, end_o = new[0:128].astype(BF16), new[128:256] + po[NX]
        s_copy(0, 1, 0).wait_recv()
        snd[...] = (mm(srx[...], end_t) + end_o).astype(BF16)
        for far in (6, 7, 5, 4, 3):
            s_copy(0, far, far - 3).start()

    @pl.when((z == 5) | (z == 7))
    def _():
        m_copy(rowm, bbuf, 0, 1, 5).wait_recv()

    t, o = chain(abuf, bbuf)
    prx[0:128, :] = t.astype(BF16)
    prx[128:256, :] = o.astype(BF16)
    for j in range(NX):
        new = mm(prx[...], pt[j])
        qt[j] = new[0:128].astype(BF16)
        qo[j] = new[128:256] + po[j]

    @pl.when((z > 0) & (z != 2))
    def _():
        s_copy(0, 1, 0).wait_recv()

    def e_copy(r, i, to_x):
        return remote(es.at[r - 1], ein.at[x], es_sem.at[r - 1, i], er_sem.at[r - 1, i], (z * NX + to_x, tp))

    e_copies = {}
    for r in (2, 1, 3):
        to_x = lax.rem(x + r, NX)
        es[r - 1] = (mm(srx[...], qt[to_x]) + qo[to_x]).astype(BF16)
        e_copies[r, 0] = e_copy(r, 0, to_x)
        e_copies[r, 0].start()
    ein[x] = (mm(srx[...], qt[x]) + qo[x]).astype(BF16)

    mean_ones = jnp.full((128, 128), 1.0 / 128.0, BF16)
    n_copies = []
    for r in (0, 1, 3, 2):
        head = lax.rem(x + NX - r, NX)
        if r > 0:
            e_copies[r, 0].wait_recv()
        att = mmt(qfin[head], ein[head]) + lfin[head]
        ms = mm((att * att).astype(BF16), mean_ones)
        nrm = (att * lax.rsqrt(ms + 1e-05) * sg[head]).astype(BF16)
        cols = pl.ds(pl.multiple_of(head * 128, 128), 128)
        for c in range(2):
            for b in range(NY):
                lo = b * 64 + c * 32
                nb[c, b * 32 : b * 32 + 32, cols] = nrm[lo : lo + 32, :]
        copy = remote(
            nb.at[other, :, cols], nrx.at[:, cols], ns_sem.at[r], nr_sem.at[r], (ctx, y * 2 + other)
        )
        copy.start()
        n_copies.append(copy)

    loads[2].wait()
    for b in range(NBLK):
        cols = pl.ds(b * BLK, BLK)
        acc[:, cols] = mm(nb[core], w_own[:, cols])
    w_copy.wait()
    for copy in n_copies:
        copy.wait()

    order = (0, 2, 1, 3)
    half = NBLK // 2
    o_copies, d_copies, c_copies = {}, {}, {}
    for b in order:
        cols = pl.ds(b * BLK, BLK)
        res = (acc[:, cols] + mm(nrx[...], w_par[:, cols])).astype(BF16)
        for d in range(NY):
            pb[b, d] = res[d * 32 : d * 32 + 32, :]
        first, second = (right, left) if b < half else (left, right)
        o_copies[b] = remote(
            pb.at[b, opp], rxo.at[b], rs_sem.at[0, b], rr_sem.at[0, b], (ctx, first * 2 + core)
        )
        o_copies[b].start()
        d_copies[b] = remote(
            pb.at[b, second], rx1.at[:, cols], rs_sem.at[1, b], rr_sem.at[1, b], (ctx, second * 2 + core)
        )
        d_copies[b].start()
    for b in order:
        first = right if b < half else left
        cols = pl.ds(b * BLK, BLK)
        o_copies[b].wait_recv()
        cs[b] = (pb[b, first].astype(F32) + rxo[b].astype(F32)).astype(BF16)
        c_copies[b] = remote(
            cs.at[b], rx2.at[:, cols], rs_sem.at[2, b], rr_sem.at[2, b], (ctx, first * 2 + core)
        )
        c_copies[b].start()
    for b in order:
        d_copies[b].wait_recv()
        c_copies[b].wait_recv()
        cols = pl.ds(b * BLK, BLK)
        total = pb[b, y].astype(F32) + rx1[:, cols].astype(F32) + rx2[:, cols].astype(F32)
        out_ref[:, cols] = total.astype(BF16)

    for row, count in ((0, 2), (2, 5)):
        @pl.when(z == row)
        def _():
            for i in range(RCH):
                for k in range(count):
                    s_copy(i, 1, k).wait_send()

    for row, count in ((1, 1), (3, 2), (4, 3), (5, 1), (6, 1)):
        @pl.when(z == row)
        def _():
            for k in range(count):
                m_copy(rowm, abuf, k, 0, 2).wait_send()

    for copy in e_copies.values():
        copy.wait_send()
    for b in order:
        o_copies[b].wait_send()
        d_copies[b].wait_send()
        c_copies[b].wait_send()


def body(nz, projected, conv_weight, log_decay, write_rate, doc_bounds, out_gate, norm_gain, out_weight):
    v = pltpu.VMEM
    dma = pltpu.SemaphoreType.DMA
    vspec = pl.BlockSpec(memory_space=pltpu.VMEM)
    aspec = pl.BlockSpec(memory_space=pl.ANY)
    scratch = [
        v((3, TAPS, 512), F32), v((HEADS, 256), F32), v((HEADS, 256), F32),
        pltpu.SMEM((2, 8), jnp.int32), v((1, 128), F32),
        v((3, 256, 512), BF16), v((3, 8, 512), BF16), v((3, 136, 512), F32), v((256, 512), BF16),
        v((512, 4096), BF16), v((512, 4096), BF16),
        v((128, 128), F32), v((128, 128), F32), v((6, 128, 128), BF16),
        v((NP, 256, 128), BF16), v((NP, 256, 128), BF16), v((NP, 128, 128), BF16),
        v((NP, 128, 128), BF16), v((NP, 128, 128), BF16), v((NP, 128, 128), BF16), v((NP, 128, 128), BF16),
        v((HEADS, 128, 128), BF16),
        v((NP, 256, 128), BF16), v((NP, 256, 128), BF16),
        v((HEADS, 256, 128), BF16), v((HEADS, 128, 128), BF16), v((HEADS, 128, 128), F32),
        v((HEADS, 256, 128), BF16), v((NX, 256, 128), BF16),
        v((HEADS, 32, 128), F32), v((HEADS, 32, 128), BF16), v((NX, 32, 128), BF16), v((NX, 8, 128), F32), v((NX, 256, 128), BF16),
        v((NX + 1, 128, 128), BF16), v((NX + 1, 128, 128), F32), v((NX + 1, 128, 128), BF16),
        v((NX + 1, 128, 128), F32), v((256, 128), BF16), v((256, 128), BF16), v((256, 128), BF16),
        v((256, 128), BF16), v((256, 128), BF16),
        v((128, 128), BF16), v((128, 128), BF16), v((NX - 1, 128, 128), BF16), v((NX, 128, 128), BF16),
        v((HEADS, 256, 128), BF16), v((HEADS, 256, 128), F32), v((HEADS, 256, 128), F32),
        v((2, 128, 512), BF16), v((128, 512), BF16), v((128, 4096), F32),
        v((NBLK, NY, 32, BLK), BF16), v((NBLK, 32, BLK), BF16), v((32, 4096), BF16), v((32, 4096), BF16),
        v((NBLK, 32, BLK), BF16),
        dma((8,)), dma((4,)), dma((2,)), dma((3,)), dma((3,)), dma((3,)), dma((3,)), dma((RCH, 5)), dma((RCH,)),
        dma((3,)), dma((2,)), pltpu.SemaphoreType.REGULAR,
        dma((3, 1)), dma((3, 1)), dma((4,)), dma((4,)), dma((3, NBLK)), dma((3, NBLK)),
    ]
    return pl.pallas_call(
        functools.partial(kernel, nz),
        out_shape=pltpu.VMEM((32, 4096), BF16),
        in_specs=[aspec] * 8,
        out_specs=vspec,
        scratch_shapes=scratch,
        compiler_params=pltpu.CompilerParams(
            collective_id=0, has_side_effects=True, vmem_limit_bytes=56 * 1024 * 1024
        ),
    )(
        projected, conv_weight, log_decay, write_rate, doc_bounds.T, out_gate,
        norm_gain.reshape(1, -1), out_weight,
    )


def solution(mesh):
    in_specs = (
        P(None, "ctx", "tp"),
        P(None, None, "tp"),
        P("tp", "ctx"),
        P("tp", "ctx"),
        P(),
        P("ctx", "tp"),
        P(),
        P("tp", None),
    )
    out_specs = P(("ctx", "tp"), None)
    nz = mesh.shape["ctx"] // NX
    assert nz == 8
    return jax.shard_map(
        functools.partial(body, nz), mesh=mesh, in_specs=in_specs, out_specs=out_specs, check_vma=False
    )
```
